256 devices in a mesh: dp: 8 (over z_lo, core), expert: 32 (over x, z_hi, y).
Axes of the slice: x: 4, y: 4, z: 8 (z_hi: 2, z_lo: 4; z = z_hi * 4 + z_lo), core: 2. Of those that a mesh axis runs over, the one named last changes fastest.
Arguments:
- tokens: bfloat16 [32768, 2048], P(('dp', 'expert')), may hold values from -6 to 6
- out_grad: bfloat16 [32768, 2048], P(('dp', 'expert')), may hold values from -6 to 6
- expert_ids: int32 [32768, 8], P(('dp', 'expert')), may hold values from 0 to 127, as said below
- route_gates: float32 [32768, 8], P(('dp', 'expert')), may hold values from 0.05 to 1
- swap_flags: int32 [32], replicated, may hold values from 0 to 1, as said below
- gate_proj: bfloat16 [32, 2048, 768], P('expert'), may hold values from -0.125 to 0.125
- up_proj: bfloat16 [32, 2048, 768], P('expert'), may hold values from -0.125 to 0.125
- down_proj: bfloat16 [32, 768, 2048], P('expert'), may hold values from -0.21875 to 0.21875
Outputs:
- layer_out: bfloat16 [32768, 2048], P(('dp', 'expert'))
- grad_tokens: bfloat16 [32768, 2048], P(('dp', 'expert'))
- gate_grads: float32 [32768, 8], P(('dp', 'expert'))
- grad_gate_proj: bfloat16 [32, 2048, 768], P('expert', 'dp')
- grad_up_proj: bfloat16 [32, 2048, 768], P('expert', 'dp')
- grad_down_proj: bfloat16 [32, 768, 2048], P('expert', 'dp')
The draws below stay inside these ranges and needn't reach their ends.
Inputs may be any that keep to these rules, and one draw needn't show every extreme that they name: `expert_ids`: each row names 8 different experts. In the rows of one device no expert is named by more than 16 rows, and one expert below 32, the same for all devices, is named by exactly 16 rows of every device. swap_flags[d] = swap_flags[d + 16] for d < 16.
All inputs are finite; a program needn't handle non-finite values.
Results may differ from the reference program's by a relative error of at most 0.013.
Values may be sent and summed in bfloat16 or wider, within the bound.
No kernel may reach another device: no remote copies, remote signals or barrier semaphores. Data moves between devices by JAX's collectives and lax.ppermute only.
A program may use at most 128 MiB of HBM per device.

```python
import math
import jax
import jax.numpy as jnp
from jax import lax

D = 2048
HIDDEN_SIZE = 768
TOP = 8
TOK_DEV = 128
HELD = 32
EXPERTS = 128
PAIR = 16
REPLICAS = 8
MOST = 16
TOKENS = 32768


def draw_expert_ids(key, part):
    key_rank, key_shift, key_token, key_pick = jax.random.split(jax.random.fold_in(key, 11), 4)
    block_count = TOKENS // TOK_DEV
    mean_load = TOK_DEV * TOP // EXPERTS
    half_experts = EXPERTS // 2
    ranking = jax.random.permutation(key_rank, EXPERTS).astype(jnp.int32)
    first_held = jnp.argmax(ranking < HELD)
    lead_value = ranking[0]
    held_value = ranking[first_held]
    ranking = ranking.at[0].set(held_value).at[first_held].set(lead_value)
    shifts = jax.random.randint(key_shift, (block_count, half_experts), 0, mean_load + 1).astype(jnp.int32)
    shifts = shifts.at[:, 0].set(mean_load)
    load_counts = jnp.concatenate([mean_load + shifts, (mean_load - shifts)[:, ::-1]], axis=1)
    load_ends = jnp.cumsum(load_counts, axis=1)
    positions = jnp.arange(TOK_DEV * TOP, dtype=jnp.int32)

    def rank_of(load_edge):
        return jnp.searchsorted(load_edge, positions, side='right').astype(jnp.int32)
    rank_table = jax.vmap(rank_of)(load_ends)
    labels = ranking[rank_table]
    picks_grid = labels.reshape(block_count, TOP, TOK_DEV).transpose(0, 2, 1)
    token_keys = jax.random.randint(key_token, (block_count, TOK_DEV), 0, 1 << 20) * TOK_DEV + jnp.arange(TOK_DEV, dtype=jnp.int32)
    token_order = jnp.argsort(token_keys, axis=1, stable=True)
    picks_grid = jnp.take_along_axis(picks_grid, token_order[:, :, None], axis=1)
    pick_keys = jax.random.randint(key_pick, (block_count, TOK_DEV, TOP), 0, 1 << 20) * TOP + jnp.arange(TOP, dtype=jnp.int32)
    pick_order = jnp.argsort(pick_keys, axis=2, stable=True)
    picks_grid = jnp.take_along_axis(picks_grid, pick_order, axis=2)
    return picks_grid.reshape(TOKENS, TOP).astype(jnp.int32)


def draw_swap_flags(key, part):
    pair_flags = jax.random.randint(jax.random.fold_in(key, 23), (PAIR,), 0, 2).astype(jnp.int32)
    return jnp.concatenate([pair_flags, pair_flags])


def steps_of(stream_key, dims, cuts, low, high):
    def one(dim, blocks):
        draws = jax.random.uniform(jax.random.fold_in(jax.random.fold_in(stream_key, 6), dim), (blocks,), jnp.float32, low / len(cuts), high / len(cuts))
        return jnp.repeat(jnp.exp(draws), dims[dim] // blocks).reshape((-1,) + (1,) * (len(dims) - dim - 1))

    factor_of = one(*cuts[0])
    for cut in cuts[1:]:
        factor_of = factor_of * one(*cut)
    return factor_of


def noise(own_key, extent, scale, bound, shards=(), held_as=jnp.bfloat16):
    result = scale * jax.random.normal(own_key, extent, jnp.float32)
    if shards:
        result = result * steps_of(own_key, extent, shards, -0.22, 0.18)
    return jnp.clip(result, -bound, bound).astype(held_as)


def setup_inputs(seed: int = 0) -> dict:
    splits = jax.random.split(jax.random.key(seed), 9)
    return {
        "tokens": noise(splits[0], (TOKENS, D), 1.0, 6.0, ((0, 256),)),
        "out_grad": noise(splits[1], (TOKENS, D), 1.0, 6.0, ((0, 256),)),
        "expert_ids": draw_expert_ids(jax.random.fold_in(splits[8], 71), 0),
        "route_gates": jnp.clip(jnp.exp(math.log(1.0) - 2.9957323 * jax.random.uniform(splits[3], (TOKENS, TOP), jnp.float32) ** steps_of(splits[3], (TOKENS, TOP), ((0, 256),), -0.2, 0.2)), 0.05, 1.0),
        "swap_flags": draw_swap_flags(jax.random.fold_in(splits[8], 71), 0),
        "gate_proj": noise(splits[5], (HELD, D, HIDDEN_SIZE), D ** -0.5, 0.125, ((0, 32),)),
        "up_proj": noise(splits[6], (HELD, D, HIDDEN_SIZE), D ** -0.5, 0.125, ((0, 32),)),
        "down_proj": noise(splits[7], (HELD, HIDDEN_SIZE, D), HIDDEN_SIZE ** -0.5, 0.21875, ((0, 32),)),
    }


def slot_table(target):
    tok_rows, pick_count = target.shape
    flat_total = tok_rows * pick_count
    matches = (target[:, :, None] == jnp.arange(HELD, dtype=jnp.int32)[None, None, :]).astype(jnp.int32)
    per_token = jnp.sum(matches, axis=1)
    earlier = jnp.cumsum(per_token, axis=0) - per_token
    position = jnp.take_along_axis(earlier, jnp.minimum(target, HELD - 1), axis=1)
    flat_index = jnp.arange(flat_total, dtype=jnp.int32).reshape(tok_rows, pick_count)
    empty_slots = jnp.full((HELD, MOST), flat_total, jnp.int32)
    return empty_slots.at[target, position].set(flat_index, mode="drop")


def expert_forward(row_block, gate_w, up_w, down_w):
    gate_pre = jnp.dot(row_block, gate_w, preferred_element_type=jnp.float32)
    up_pre = jnp.dot(row_block, up_w, preferred_element_type=jnp.float32)
    gate_sigmoid = jax.nn.sigmoid(gate_pre)
    hidden = (gate_pre * gate_sigmoid * up_pre).astype(jnp.bfloat16)
    expert_out = jnp.dot(hidden, down_w, preferred_element_type=jnp.float32).astype(jnp.bfloat16)
    return gate_pre, up_pre, gate_sigmoid, hidden, expert_out


def expert_backward(gate_pre, up_pre, gate_sigmoid, out_grads, gate_w, up_w, down_w):
    contract_last = (((1,), (1,)), ((), ()))
    hidden_grad = lax.dot_general(out_grads, down_w, contract_last, preferred_element_type=jnp.float32)
    gate_grad = (hidden_grad * up_pre * gate_sigmoid * (1.0 + gate_pre * (1.0 - gate_sigmoid))).astype(jnp.bfloat16)
    up_grad = (hidden_grad * gate_pre * gate_sigmoid).astype(jnp.bfloat16)
    row_grads = lax.dot_general(gate_grad, gate_w, contract_last, preferred_element_type=jnp.float32)
    row_grads = row_grads + lax.dot_general(up_grad, up_w, contract_last, preferred_element_type=jnp.float32)
    return jnp.concatenate([gate_grad, up_grad], axis=1), row_grads.astype(jnp.bfloat16)


def reference(tokens, out_grad, expert_ids, route_gates, swap_flags, gate_proj, up_proj, down_proj):
    block_count = TOKENS // TOK_DEV
    blocks = expert_ids.reshape(block_count, TOK_DEV, TOP)
    target = jnp.where(blocks < HELD, blocks, HELD).astype(jnp.int32)
    slots = lax.map(slot_table, target)
    offsets = (jnp.arange(block_count, dtype=jnp.int32) * (TOK_DEV * TOP))[:, None, None]
    pick_index = jnp.where(slots < TOK_DEV * TOP, slots + offsets, TOKENS * TOP).astype(jnp.int32)
    pick_index = pick_index.reshape(REPLICAS, HELD, HELD, MOST).transpose(2, 0, 1, 3).reshape(HELD, REPLICAS, HELD * MOST)
    zero_row = jnp.zeros((1, D), jnp.bfloat16)
    token_pad = jnp.concatenate([tokens, zero_row], axis=0)
    grad_pad = jnp.concatenate([out_grad, zero_row], axis=0)
    gate_pad = jnp.concatenate([route_gates.reshape(-1), jnp.zeros((1,), jnp.float32)])
    contract_first = (((0,), (0,)), ((), ()))

    def per_expert(running, expert_inputs):
        expert_picks, gate_w, up_w, down_w = expert_inputs

        def per_group(inner_state, group_picks):
            mixed_sum, token_sum, gate_sum, gate_up_sum, down_sum = inner_state
            row_index = group_picks // TOP
            row_block = token_pad[row_index]
            grad_rows = grad_pad[row_index]
            slot_gate = gate_pad[group_picks]
            gate_pre, up_pre, gate_sigmoid, hidden, expert_out = expert_forward(row_block, gate_w, up_w, down_w)
            out_grads = (slot_gate[:, None] * grad_rows.astype(jnp.float32)).astype(jnp.bfloat16)
            both_grads, row_grads = expert_backward(gate_pre, up_pre, gate_sigmoid, out_grads, gate_w, up_w, down_w)
            gate_up_part = lax.dot_general(row_block, both_grads, contract_first, preferred_element_type=jnp.float32)
            down_part = lax.dot_general(hidden, out_grads, contract_first, preferred_element_type=jnp.float32)
            gate_up_sum = gate_up_sum + lax.optimization_barrier(gate_up_part.astype(jnp.bfloat16)).astype(jnp.float32)
            down_sum = down_sum + lax.optimization_barrier(down_part.astype(jnp.bfloat16)).astype(jnp.float32)
            out_values = expert_out.astype(jnp.float32)
            mixed_sum = mixed_sum.at[row_index].add(slot_gate[:, None] * out_values)
            token_sum = token_sum.at[row_index].add(row_grads.astype(jnp.float32))
            gate_sum = gate_sum.at[group_picks].add(jnp.sum(grad_rows.astype(jnp.float32) * out_values, axis=1))
            return (mixed_sum, token_sum, gate_sum, gate_up_sum, down_sum), None

        start_state = (running[0], running[1], running[2], jnp.zeros((D, 2 * HIDDEN_SIZE), jnp.float32), jnp.zeros((HIDDEN_SIZE, D), jnp.float32))
        final_state, unused = lax.scan(per_group, start_state, expert_picks)
        return (final_state[0], final_state[1], final_state[2]), (final_state[3].astype(jnp.bfloat16), final_state[4].astype(jnp.bfloat16))

    start_running = (jnp.zeros((TOKENS + 1, D), jnp.float32), jnp.zeros((TOKENS + 1, D), jnp.float32), jnp.zeros((TOKENS * TOP + 1,), jnp.float32))
    final_running, weight_grads = lax.scan(per_expert, start_running, (pick_index, gate_proj, up_proj, down_proj))
    gate_up_all, down_all = weight_grads
    device_ids = jnp.arange(HELD, dtype=jnp.int32)
    held_by = jnp.where(swap_flags == 1, (device_ids + PAIR) % HELD, device_ids).astype(jnp.int32)
    layer_out = final_running[0][:TOKENS].astype(jnp.bfloat16)
    grad_tokens = final_running[1][:TOKENS].astype(jnp.bfloat16)
    gate_grads = final_running[2][:TOKENS * TOP].reshape(TOKENS, TOP)
    moved_gate_up = gate_up_all[held_by]
    grad_gate_proj = moved_gate_up[:, :, :HIDDEN_SIZE]
    grad_up_proj = moved_gate_up[:, :, HIDDEN_SIZE:]
    grad_down_proj = down_all[held_by]
    return (layer_out, grad_tokens, gate_grads, grad_gate_proj, grad_up_proj, grad_down_proj)
```

```python
import jax
import jax.numpy as jnp
from jax import lax
from jax.sharding import PartitionSpec as P

SLOTS = 4


def partner(x, axis, bit):
    return lax.ppermute(x, axis, [(i, i ^ 1 << bit) for i in range(lax.axis_size(axis))])


def slot_table(target, devices, slot_most):
    tok_rows, pick_count = target.shape
    flat_total = tok_rows * pick_count
    matches = (target[:, :, None] == jnp.arange(devices, dtype=jnp.int32)[None, None, :]).astype(
        jnp.int32
    )
    per_token = jnp.sum(matches, axis=1)
    earlier = jnp.cumsum(per_token, axis=0) - per_token
    position = jnp.take_along_axis(earlier, jnp.minimum(target, devices - 1), axis=1)
    flat_index = jnp.arange(flat_total, dtype=jnp.int32).reshape(tok_rows, pick_count)
    empty_slots = jnp.full((devices, slot_most), flat_total, jnp.int32)
    return empty_slots.at[target, position].set(flat_index, mode="drop")


def expert_forward(row_block, gate_w, up_w, down_w):
    gate_pre = jnp.dot(row_block, gate_w, preferred_element_type=jnp.float32)
    up_pre = jnp.dot(row_block, up_w, preferred_element_type=jnp.float32)
    gate_sigmoid = jax.nn.sigmoid(gate_pre)
    hidden = (gate_pre * gate_sigmoid * up_pre).astype(jnp.bfloat16)
    expert_out = jnp.dot(hidden, down_w, preferred_element_type=jnp.float32).astype(jnp.bfloat16)
    return (gate_pre, up_pre, gate_sigmoid, hidden, expert_out)


def expert_backward(gate_pre, up_pre, gate_sigmoid, out_grads, gate_w, up_w, down_w):
    contract_last = (((1,), (1,)), ((), ()))
    hidden_grad = lax.dot_general(
        out_grads, down_w, contract_last, preferred_element_type=jnp.float32
    )
    gate_grad = (
        hidden_grad * up_pre * gate_sigmoid * (1.0 + gate_pre * (1.0 - gate_sigmoid))
    ).astype(jnp.bfloat16)
    up_grad = (hidden_grad * gate_pre * gate_sigmoid).astype(jnp.bfloat16)
    row_grads = lax.dot_general(
        gate_grad, gate_w, contract_last, preferred_element_type=jnp.float32
    )
    row_grads = row_grads + lax.dot_general(
        up_grad, up_w, contract_last, preferred_element_type=jnp.float32
    )
    return (jnp.concatenate([gate_grad, up_grad], axis=1), row_grads.astype(jnp.bfloat16))


def on_device(tokens, out_grad, expert_ids, route_gates, swap_flags, gate_proj, up_proj, down_proj):
    devices = lax.axis_size("expert")
    swap_bit = devices.bit_length() - 2
    my_index = lax.axis_index("expert")
    tok_rows, model_width = tokens.shape
    pick_count = expert_ids.shape[1]
    hidden_width = gate_proj.shape[2]
    slot_most = 2 * tok_rows * pick_count // (SLOTS * devices)
    flat_total = tok_rows * pick_count
    in_layer = expert_ids < devices
    is_moved = swap_flags[my_index] == 1
    own_weights = (gate_proj[0], up_proj[0], down_proj[0])
    target = jnp.where(in_layer, expert_ids, devices)
    gate_w, up_w, down_w = own_weights
    slot_index = slot_table(target, devices, slot_most)
    row_index = slot_index // pick_count
    zero_row = jnp.zeros((1, model_width), jnp.bfloat16)
    token_pad = jnp.concatenate([tokens, zero_row], axis=0)
    grad_pad = jnp.concatenate([out_grad, zero_row], axis=0)
    gate_pad = jnp.concatenate([route_gates.reshape(-1), jnp.zeros((1,), jnp.float32)])
    slot_gate = gate_pad[slot_index]
    send_rows = token_pad[row_index]
    grad_rows = grad_pad[row_index]
    send_grads = (slot_gate[:, :, None] * grad_rows.astype(jnp.float32)).astype(jnp.bfloat16)
    block_shape = (devices, slot_most, model_width)
    arrived_rows = lax.all_to_all(send_rows, "expert", split_axis=0, concat_axis=0, tiled=True)
    row_block = arrived_rows.reshape(-1, model_width)
    gate_pre, up_pre, gate_sigmoid, hidden, expert_out = expert_forward(
        row_block, gate_w, up_w, down_w
    )
    returned_out = lax.all_to_all(
        expert_out.reshape(block_shape), "expert", split_axis=0, concat_axis=0, tiled=True
    )
    arrived_grads = lax.all_to_all(send_grads, "expert", split_axis=0, concat_axis=0, tiled=True)
    out_grads = arrived_grads.reshape(-1, model_width)
    both_grads, row_grads = expert_backward(
        gate_pre, up_pre, gate_sigmoid, out_grads, gate_w, up_w, down_w
    )
    returned_grads = lax.all_to_all(
        row_grads.reshape(block_shape), "expert", split_axis=0, concat_axis=0, tiled=True
    )
    flat_rows = row_index.reshape(-1)
    out_values = returned_out.reshape(-1, model_width).astype(jnp.float32)
    mixed_sum = (
        jnp.zeros((tok_rows + 1, model_width), jnp.float32)
        .at[flat_rows]
        .add(slot_gate.reshape(-1)[:, None] * out_values)
    )
    layer_out = mixed_sum[:tok_rows].astype(jnp.bfloat16)
    token_sum = (
        jnp.zeros((tok_rows + 1, model_width), jnp.float32)
        .at[flat_rows]
        .add(returned_grads.reshape(-1, model_width).astype(jnp.float32))
    )
    grad_tokens = token_sum[:tok_rows].astype(jnp.bfloat16)
    gate_dots = jnp.sum(grad_rows.reshape(-1, model_width).astype(jnp.float32) * out_values, axis=1)
    gate_grads = (
        jnp.zeros((flat_total + 1,), jnp.float32)
        .at[slot_index.reshape(-1)]
        .add(gate_dots)[:flat_total]
        .reshape(tok_rows, pick_count)
    )
    contract_first = (((0,), (0,)), ((), ()))
    columns = row_block
    gate_up_sum = lax.psum_scatter(
        lax.dot_general(
            columns, both_grads, contract_first, preferred_element_type=jnp.float32
        ).astype(jnp.bfloat16),
        "dp",
        scatter_dimension=0,
        tiled=True,
    )
    columns = hidden
    down_sum = lax.psum_scatter(
        lax.dot_general(
            columns, out_grads, contract_first, preferred_element_type=jnp.float32
        ).astype(jnp.bfloat16),
        "dp",
        scatter_dimension=0,
        tiled=True,
    )
    other_gate_up = partner(gate_up_sum, "expert", swap_bit)
    other_down = partner(down_sum, "expert", swap_bit)
    gate_up_sum = jnp.where(is_moved, other_gate_up, gate_up_sum)
    down_sum = jnp.where(is_moved, other_down, down_sum)
    grad_gate = gate_up_sum[:, :hidden_width]
    grad_up = gate_up_sum[:, hidden_width:]
    return (layer_out, grad_tokens, gate_grads, grad_gate[None], grad_up[None], down_sum[None])


def solution(mesh):
    return jax.shard_map(
        on_device,
        mesh=mesh,
        in_specs=(
            P(("dp", "expert"), None),
            P(("dp", "expert"), None),
            P(("dp", "expert"), None),
            P(("dp", "expert"), None),
            P(),
            P("expert", None, None),
            P("expert", None, None),
            P("expert", None, None),
        ),
        out_specs=(
            P(("dp", "expert"), None),
            P(("dp", "expert"), None),
            P(("dp", "expert"), None),
            P("expert", "dp", None),
            P("expert", "dp", None),
            P("expert", "dp", None),
        ),
        check_vma=False,
    )
```

```python
import jax
import jax.numpy as jnp
from jax import lax
from jax.sharding import PartitionSpec as P

MOST = 16
X_SIZE, HI_SIZE, Y_SIZE = 4, 2, 4
LO_SIZE, CORES = 4, 2
PLANE = X_SIZE * Y_SIZE
SIDE = 128

BOTH = ("dp", "expert")
PLANE_GROUPS = [
    [x * HI_SIZE * Y_SIZE + hi * Y_SIZE + y for x in range(X_SIZE) for y in range(Y_SIZE)]
    for hi in range(HI_SIZE)
]
LINE_GROUPS = [[lo * CORES + core for lo in range(LO_SIZE)] for core in range(CORES)]


def across(value):
    experts = lax.axis_size("expert")
    pairs = []
    for dp in range(lax.axis_size("dp")):
        lo, core = divmod(dp, CORES)
        other_dp = (LO_SIZE - 1 - lo) * CORES + core
        for expert in range(experts):
            pairs.append((dp * experts + expert, other_dp * experts + (expert ^ Y_SIZE)))
    return lax.ppermute(value, BOTH, pairs)


def to_plane(blocks):
    return lax.all_to_all(
        blocks, "expert", split_axis=0, concat_axis=0, axis_index_groups=PLANE_GROUPS, tiled=True
    )


def half_experts(half):
    place = lax.broadcasted_iota(jnp.int32, (1, 1, PLANE), 2)
    return (place // Y_SIZE) * (HI_SIZE * Y_SIZE) + half * Y_SIZE + place % Y_SIZE


def split_columns(values):
    high = lax.reduce_precision(values, 8, 7)
    middle = lax.reduce_precision(values - high, 8, 7)
    low = lax.reduce_precision(values - high - middle, 8, 7)
    rest = jnp.zeros((values.shape[0], SIDE - 3 * PLANE), jnp.float32)
    return jnp.concatenate([high, middle, low, rest], axis=1).astype(jnp.bfloat16)


def join_columns(columns):
    parts = columns[:, : 3 * PLANE].astype(jnp.float32)
    return parts[:, :PLANE] + parts[:, PLANE : 2 * PLANE] + parts[:, 2 * PLANE :]


def selection(gate_table):
    rows = gate_table.shape[0]
    chosen = jnp.transpose(gate_table) > 0
    before = (
        lax.broadcasted_iota(jnp.int32, (rows, rows), 0)
        < lax.broadcasted_iota(jnp.int32, (rows, rows), 1)
    ).astype(jnp.bfloat16)
    rank = jnp.dot(chosen.astype(jnp.bfloat16), before, preferred_element_type=jnp.float32)
    slot = lax.broadcasted_iota(jnp.int32, (1, MOST, 1), 1).astype(jnp.float32)
    hit = jnp.logical_and(rank[:, None, :] == slot, chosen[:, None, :])
    return hit.astype(jnp.bfloat16).reshape(PLANE * MOST, rows)


def fill(picked, values):
    return jnp.dot(picked, values, preferred_element_type=jnp.float32).astype(jnp.bfloat16)


def collect(picked, values):
    return lax.dot_general(
        picked, values, (((0,), (0,)), ((), ())), preferred_element_type=jnp.float32
    )


def line_sum(partial, core):
    rows = partial.shape[0] // (LO_SIZE * CORES)
    parts = partial.reshape(LO_SIZE, CORES, rows, partial.shape[1])
    give = lax.dynamic_index_in_dim(parts, 1 - core, axis=1, keepdims=False)
    keep = lax.dynamic_index_in_dim(parts, core, axis=1, keepdims=False)
    taken = lax.ppermute(give, "dp", [(i, i ^ 1) for i in range(LO_SIZE * CORES)])
    both = (keep.astype(jnp.float32) + taken.astype(jnp.float32)).astype(jnp.bfloat16)
    arrived = lax.all_to_all(
        both, "dp", split_axis=0, concat_axis=0, axis_index_groups=LINE_GROUPS, tiled=True
    )
    return jnp.sum(arrived.astype(jnp.float32), axis=0).astype(jnp.bfloat16)


def on_device(tokens, out_grad, expert_ids, route_gates, swap_flags, gate_proj, up_proj, down_proj):
    devices = lax.axis_size("expert")
    my_expert = lax.axis_index("expert")
    core = lax.axis_index("dp") % CORES
    half = (my_expert // Y_SIZE) % HI_SIZE
    place = (my_expert // (HI_SIZE * Y_SIZE)) * Y_SIZE + my_expert % Y_SIZE
    width = tokens.shape[1]
    hidden_width = gate_proj.shape[2]
    gate_w, up_w, down_w = gate_proj[0], up_proj[0], down_proj[0]

    own_names = half_experts(half)
    far_names = half_experts(1 - half)
    own_hits = expert_ids[:, :, None] == own_names
    far_hits = expert_ids[:, :, None] == far_names
    own_gates = jnp.sum(jnp.where(own_hits, route_gates[:, :, None], 0.0), axis=1)
    far_gates = jnp.sum(jnp.where(far_hits, route_gates[:, :, None], 0.0), axis=1)

    far_tokens = across(jnp.concatenate([tokens, split_columns(far_gates)], axis=1))
    far_cotangents = across(out_grad)

    own_picked = selection(own_gates)
    near_source = jnp.concatenate([tokens, split_columns(own_gates), out_grad], axis=1)
    near_rows = to_plane(fill(own_picked, near_source).reshape(PLANE, MOST, -1))
    near_rows = near_rows.reshape(PLANE * MOST, -1)

    far_picked = selection(join_columns(far_tokens[:, width:]))
    far_rows = to_plane(fill(far_picked, far_tokens).reshape(PLANE, MOST, -1))
    far_rows = far_rows.reshape(PLANE * MOST, -1)
    far_grads = to_plane(fill(far_picked, far_cotangents).reshape(PLANE, MOST, -1))
    far_grads = far_grads.reshape(PLANE * MOST, -1)

    row_block = jnp.concatenate([near_rows[:, :width], far_rows[:, :width]], axis=0)
    side_block = jnp.concatenate(
        [near_rows[:, width : width + SIDE], far_rows[:, width:]], axis=0
    ).astype(jnp.float32)
    grad_block = jnp.concatenate([near_rows[:, width + SIDE :], far_grads], axis=0)
    lane = lax.broadcasted_iota(jnp.int32, (1, SIDE), 1)
    mine = jnp.logical_and(lane % PLANE == place, lane < 3 * PLANE)
    slot_gate = jnp.sum(jnp.where(mine, side_block, 0.0), axis=1, keepdims=True)

    gate_pre = jnp.dot(row_block, gate_w, preferred_element_type=jnp.float32)
    up_pre = jnp.dot(row_block, up_w, preferred_element_type=jnp.float32)
    sigmoid = jax.nn.sigmoid(gate_pre)
    hidden = (gate_pre * sigmoid * up_pre).astype(jnp.bfloat16)
    expert_out = jnp.dot(hidden, down_w, preferred_element_type=jnp.float32)
    grad_rows = grad_block.astype(jnp.float32)
    gate_dots = jnp.sum(grad_rows * expert_out, axis=1, keepdims=True)
    weighted_out = (slot_gate * expert_out).astype(jnp.bfloat16)
    pick_grad = (slot_gate * grad_rows).astype(jnp.bfloat16)

    contract_last = (((1,), (1,)), ((), ()))
    contract_first = (((0,), (0,)), ((), ()))
    down_part = lax.dot_general(
        hidden, pick_grad, contract_first, preferred_element_type=jnp.float32
    ).astype(jnp.bfloat16)
    down_sum = line_sum(down_part, core)
    hidden_grad = lax.dot_general(
        pick_grad, down_w, contract_last, preferred_element_type=jnp.float32
    )
    gate_grad = (hidden_grad * up_pre * sigmoid * (1.0 + gate_pre * (1.0 - sigmoid))).astype(
        jnp.bfloat16
    )
    up_grad = (hidden_grad * gate_pre * sigmoid).astype(jnp.bfloat16)
    both_grads = jnp.concatenate([gate_grad, up_grad], axis=1)
    gate_up_part = lax.dot_general(
        row_block, both_grads, contract_first, preferred_element_type=jnp.float32
    ).astype(jnp.bfloat16)
    gate_up_sum = line_sum(gate_up_part, core)
    row_grads = lax.dot_general(gate_grad, gate_w, contract_last, preferred_element_type=jnp.float32)
    row_grads = row_grads + lax.dot_general(
        up_grad, up_w, contract_last, preferred_element_type=jnp.float32
    )
    row_grads = row_grads.astype(jnp.bfloat16)

    dot_table = jnp.where(lane[:, :PLANE] == place, gate_dots, 0.0)
    out_rows = jnp.concatenate([weighted_out, split_columns(dot_table)], axis=1)

    def give_back(rows):
        halves = rows.reshape(2, PLANE, MOST, -1)
        sent = jnp.concatenate([halves[0], halves[1]], axis=1)
        returned = to_plane(sent)
        near = collect(own_picked, returned[:, :MOST].reshape(PLANE * MOST, -1))
        far = collect(far_picked, returned[:, MOST:].reshape(PLANE * MOST, -1))
        return near, across(far.astype(jnp.bfloat16)).astype(jnp.float32)

    near_out, far_out = give_back(out_rows)
    layer_out = (near_out[:, :width] + far_out[:, :width]).astype(jnp.bfloat16)
    near_dots = join_columns(near_out[:, width:])
    far_dots = join_columns(far_out[:, width:])
    gate_grads = jnp.sum(
        jnp.where(own_hits, near_dots[:, None, :], 0.0)
        + jnp.where(far_hits, far_dots[:, None, :], 0.0),
        axis=2,
    )
    near_token, far_token = give_back(row_grads)
    grad_tokens = (near_token + far_token).astype(jnp.bfloat16)

    is_moved = swap_flags[my_expert] == 1
    swap = [(i, i ^ (devices // 2)) for i in range(devices)]
    other_down = lax.ppermute(down_sum, "expert", swap)
    other_gate_up = lax.ppermute(gate_up_sum, "expert", swap)
    down_sum = jnp.where(is_moved, other_down, down_sum)
    gate_up_sum = jnp.where(is_moved, other_gate_up, gate_up_sum)
    grad_gate = gate_up_sum[:, :hidden_width]
    grad_up = gate_up_sum[:, hidden_width:]
    return (layer_out, grad_tokens, gate_grads, grad_gate[None], grad_up[None], down_sum[None])


def solution(mesh):
    return jax.shard_map(
        on_device,
        mesh=mesh,
        in_specs=(
            P(("dp", "expert"), None),
            P(("dp", "expert"), None),
            P(("dp", "expert"), None),
            P(("dp", "expert"), None),
            P(),
            P("expert", None, None),
            P("expert", None, None),
            P("expert", None, None),
        ),
        out_specs=(
            P(("dp", "expert"), None),
            P(("dp", "expert"), None),
            P(("dp", "expert"), None),
            P("expert", "dp", None),
            P("expert", "dp", None),
            P("expert", "dp", None),
        ),
        check_vma=False,
    )
```

```python
import jax
import jax.numpy as jnp
from jax import lax
from jax.sharding import PartitionSpec as P

MOST = 16
X_SIZE, HI_SIZE, Y_SIZE = 4, 2, 4
LO_SIZE, CORES = 4, 2
PLANE = X_SIZE * Y_SIZE
SIDE = 128

BOTH = ("dp", "expert")
PLANE_GROUPS = [
    [x * HI_SIZE * Y_SIZE + hi * Y_SIZE + y for x in range(X_SIZE) for y in range(Y_SIZE)]
    for hi in range(HI_SIZE)
]


def across(value):
    experts = lax.axis_size("expert")
    pairs = []
    for dp in range(lax.axis_size("dp")):
        lo, core = divmod(dp, CORES)
        other_dp = (LO_SIZE - 1 - lo) * CORES + core
        for expert in range(experts):
            pairs.append((dp * experts + expert, other_dp * experts + (expert ^ Y_SIZE)))
    return lax.ppermute(value, BOTH, pairs)


def to_plane(blocks):
    return lax.all_to_all(
        blocks, "expert", split_axis=0, concat_axis=0, axis_index_groups=PLANE_GROUPS, tiled=True
    )


def half_experts(half):
    place = lax.broadcasted_iota(jnp.int32, (1, 1, PLANE), 2)
    return (place // Y_SIZE) * (HI_SIZE * Y_SIZE) + half * Y_SIZE + place % Y_SIZE


def split_columns(values):
    high = lax.reduce_precision(values, 8, 7)
    middle = lax.reduce_precision(values - high, 8, 7)
    low = lax.reduce_precision(values - high - middle, 8, 7)
    rest = jnp.zeros((values.shape[0], SIDE - 3 * PLANE), jnp.float32)
    return jnp.concatenate([high, middle, low, rest], axis=1).astype(jnp.bfloat16)


def join_columns(columns):
    parts = columns[:, : 3 * PLANE].astype(jnp.float32)
    return parts[:, :PLANE] + parts[:, PLANE : 2 * PLANE] + parts[:, 2 * PLANE :]


def selection(gate_table):
    rows = gate_table.shape[0]
    chosen = jnp.transpose(gate_table) > 0
    before = (
        lax.broadcasted_iota(jnp.int32, (rows, rows), 0)
        < lax.broadcasted_iota(jnp.int32, (rows, rows), 1)
    ).astype(jnp.bfloat16)
    rank = jnp.dot(chosen.astype(jnp.bfloat16), before, preferred_element_type=jnp.float32)
    slot = lax.broadcasted_iota(jnp.int32, (1, MOST, 1), 1).astype(jnp.float32)
    hit = jnp.logical_and(rank[:, None, :] == slot, chosen[:, None, :])
    return hit.astype(jnp.bfloat16).reshape(PLANE * MOST, rows)


def fill(picked, values):
    return jnp.dot(picked, values, preferred_element_type=jnp.float32).astype(jnp.bfloat16)


def collect(picked, values):
    return lax.dot_general(
        picked, values, (((0,), (0,)), ((), ())), preferred_element_type=jnp.float32
    )


def neighbours(steps):
    return [(a * CORES + core, b * CORES + core) for a, b in steps for core in range(CORES)]


def shard_of(parts, index):
    index = jnp.clip(index, 0, LO_SIZE - 1)
    return lax.dynamic_index_in_dim(parts, index, axis=0, keepdims=False).astype(jnp.float32)


def core_swap(partial, core):
    rows = partial.shape[0] // (LO_SIZE * CORES)
    parts = partial.reshape(LO_SIZE, CORES, rows, partial.shape[1])
    give = lax.dynamic_index_in_dim(parts, 1 - core, axis=1, keepdims=False)
    keep = lax.dynamic_index_in_dim(parts, core, axis=1, keepdims=False)
    taken = lax.ppermute(give, "dp", [(i, i ^ 1) for i in range(LO_SIZE * CORES)])
    return (keep.astype(jnp.float32) + taken.astype(jnp.float32)).astype(jnp.bfloat16)


def line_sum(parts, lo):
    first = jnp.where(lo == 0, parts[LO_SIZE - 1], parts[0])
    arrived = lax.ppermute(first, "dp", neighbours([(0, 1), (3, 2)])).astype(jnp.float32)
    up = (shard_of(parts, lo + 2) + arrived).astype(jnp.bfloat16)
    down = (shard_of(parts, lo - 2) + arrived).astype(jnp.bfloat16)
    up = lax.ppermute(up, "dp", neighbours([(0, 1), (1, 2)])).astype(jnp.float32)
    down = lax.ppermute(down, "dp", neighbours([(3, 2), (2, 1)])).astype(jnp.float32)
    up = (shard_of(parts, lo + 1) + up).astype(jnp.bfloat16)
    down = (shard_of(parts, lo - 1) + down).astype(jnp.bfloat16)
    up = lax.ppermute(up, "dp", neighbours([(0, 1), (1, 2), (2, 3)])).astype(jnp.float32)
    down = lax.ppermute(down, "dp", neighbours([(3, 2), (2, 1), (1, 0)])).astype(jnp.float32)
    return (shard_of(parts, lo) + up + down).astype(jnp.bfloat16)


CONTRACT_LAST = (((1,), (1,)), ((), ()))
CONTRACT_FIRST = (((0,), (0,)), ((), ()))


def expert(rows, place, gate_w, up_w, down_w):
    width = gate_w.shape[0]
    row_block = rows[:, :width]
    grad_rows = rows[:, width + SIDE :].astype(jnp.float32)
    lane = lax.broadcasted_iota(jnp.int32, (1, SIDE), 1)
    mine = jnp.logical_and(lane % PLANE == place, lane < 3 * PLANE)
    side_block = rows[:, width : width + SIDE].astype(jnp.float32)
    slot_gate = jnp.sum(jnp.where(mine, side_block, 0.0), axis=1, keepdims=True)
    gate_pre = jnp.dot(row_block, gate_w, preferred_element_type=jnp.float32)
    up_pre = jnp.dot(row_block, up_w, preferred_element_type=jnp.float32)
    sigmoid = jax.nn.sigmoid(gate_pre)
    hidden = (gate_pre * sigmoid * up_pre).astype(jnp.bfloat16)
    pick_grad = (slot_gate * grad_rows).astype(jnp.bfloat16)
    hidden_grad = lax.dot_general(
        pick_grad, down_w, CONTRACT_LAST, preferred_element_type=jnp.float32
    )
    gate_grad = (hidden_grad * up_pre * sigmoid * (1.0 + gate_pre * (1.0 - sigmoid))).astype(
        jnp.bfloat16
    )
    up_grad = (hidden_grad * gate_pre * sigmoid).astype(jnp.bfloat16)
    expert_out = jnp.dot(hidden, down_w, preferred_element_type=jnp.float32)
    gate_dots = jnp.sum(grad_rows * expert_out, axis=1, keepdims=True)
    weighted_out = (slot_gate * expert_out).astype(jnp.bfloat16)
    row_grads = lax.dot_general(gate_grad, gate_w, CONTRACT_LAST, preferred_element_type=jnp.float32)
    row_grads = row_grads + lax.dot_general(
        up_grad, up_w, CONTRACT_LAST, preferred_element_type=jnp.float32
    )
    dot_table = jnp.where(lane[:, :PLANE] == place, gate_dots, 0.0)
    back = jnp.concatenate(
        [weighted_out, split_columns(dot_table), row_grads.astype(jnp.bfloat16)], axis=1
    )
    both_grads = jnp.concatenate([gate_grad, up_grad], axis=1)
    return back, row_block, hidden, pick_grad, both_grads


def on_device(tokens, out_grad, expert_ids, route_gates, swap_flags, gate_proj, up_proj, down_proj):
    devices = lax.axis_size("expert")
    my_expert = lax.axis_index("expert")
    lo = lax.axis_index("dp") // CORES
    core = lax.axis_index("dp") % CORES
    half = (my_expert // Y_SIZE) % HI_SIZE
    place = (my_expert // (HI_SIZE * Y_SIZE)) * Y_SIZE + my_expert % Y_SIZE
    width = tokens.shape[1]
    hidden_width = gate_proj.shape[2]
    weights = (gate_proj[0], up_proj[0], down_proj[0])

    own_names = half_experts(half)
    far_names = half_experts(1 - half)
    own_hits = expert_ids[:, :, None] == own_names
    far_hits = expert_ids[:, :, None] == far_names
    own_gates = jnp.sum(jnp.where(own_hits, route_gates[:, :, None], 0.0), axis=1)
    far_gates = jnp.sum(jnp.where(far_hits, route_gates[:, :, None], 0.0), axis=1)

    far_source = across(jnp.concatenate([tokens, split_columns(far_gates), out_grad], axis=1))
    near_picked = selection(own_gates)
    near_source = jnp.concatenate([tokens, split_columns(own_gates), out_grad], axis=1)
    near_blocks = fill(near_picked, near_source).reshape(PLANE, MOST, -1)
    near_rows = to_plane(near_blocks).reshape(PLANE * MOST, -1)

    far_source, near_blocks = lax.optimization_barrier((far_source, near_blocks))
    far_picked = selection(join_columns(far_source[:, width : width + SIDE]))
    far_rows = to_plane(fill(far_picked, far_source).reshape(PLANE, MOST, -1))
    far_rows = far_rows.reshape(PLANE * MOST, -1)

    near_back, near_x, near_hidden, near_pick, near_grads = expert(near_rows, place, *weights)
    far_rows, near_back = lax.optimization_barrier((far_rows, near_back))
    near_returned = to_plane(near_back.reshape(PLANE, MOST, -1)).reshape(PLANE * MOST, -1)
    far_back, far_x, far_hidden, far_pick, far_grads = expert(far_rows, place, *weights)

    down_part = lax.dot_general(
        jnp.concatenate([near_hidden, far_hidden], axis=0),
        jnp.concatenate([near_pick, far_pick], axis=0),
        CONTRACT_FIRST,
        preferred_element_type=jnp.float32,
    ).astype(jnp.bfloat16)
    gate_up_part = lax.dot_general(
        jnp.concatenate([near_x, far_x], axis=0),
        jnp.concatenate([near_grads, far_grads], axis=0),
        CONTRACT_FIRST,
        preferred_element_type=jnp.float32,
    ).astype(jnp.bfloat16)
    down_parts = core_swap(down_part, core)
    gate_up_parts = core_swap(gate_up_part, core)
    down_sum = line_sum(down_parts, lo)
    gate_up_sum = line_sum(gate_up_parts, lo)

    far_returned = to_plane(far_back.reshape(PLANE, MOST, -1)).reshape(PLANE * MOST, -1)
    near_total = collect(near_picked, near_returned)
    far_total = across(collect(far_picked, far_returned).astype(jnp.bfloat16)).astype(jnp.float32)
    layer_out = (near_total[:, :width] + far_total[:, :width]).astype(jnp.bfloat16)
    grad_tokens = (near_total[:, width + SIDE :] + far_total[:, width + SIDE :]).astype(jnp.bfloat16)
    near_dots = join_columns(near_total[:, width : width + SIDE])
    far_dots = join_columns(far_total[:, width : width + SIDE])
    gate_grads = jnp.sum(
        jnp.where(own_hits, near_dots[:, None, :], 0.0)
        + jnp.where(far_hits, far_dots[:, None, :], 0.0),
        axis=2,
    )

    is_moved = swap_flags[my_expert] == 1
    swap = [(i, i ^ (devices // 2)) for i in range(devices)]
    other_down = lax.ppermute(down_sum, "expert", swap)
    other_gate_up = lax.ppermute(gate_up_sum, "expert", swap)
    down_sum = jnp.where(is_moved, other_down, down_sum)
    gate_up_sum = jnp.where(is_moved, other_gate_up, gate_up_sum)
    grad_gate = gate_up_sum[:, :hidden_width]
    grad_up = gate_up_sum[:, hidden_width:]
    return (layer_out, grad_tokens, gate_grads, grad_gate[None], grad_up[None], down_sum[None])


def solution(mesh):
    return jax.shard_map(
        on_device,
        mesh=mesh,
        in_specs=(
            P(("dp", "expert"), None),
            P(("dp", "expert"), None),
            P(("dp", "expert"), None),
            P(("dp", "expert"), None),
            P(),
            P("expert", None, None),
            P("expert", None, None),
            P("expert", None, None),
        ),
        out_specs=(
            P(("dp", "expert"), None),
            P(("dp", "expert"), None),
            P(("dp", "expert"), None),
            P("expert", "dp", None),
            P("expert", "dp", None),
            P("expert", "dp", None),
        ),
        check_vma=False,
    )
```

```python
import functools

import jax
import jax.numpy as jnp
from jax import lax
from jax.experimental import pallas as pl
from jax.experimental.pallas import tpu as pltpu
from jax.sharding import PartitionSpec as P

MOST = 16
HI_SIZE, Y_SIZE = 2, 4
LO_SIZE, CORES = 4, 2
PLANE = 16
SIDE = 128
PARTS = 3

BOTH = ("dp", "expert")
PLANE_GROUPS = [
    [x * HI_SIZE * Y_SIZE + hi * Y_SIZE + y for x in range(PLANE // Y_SIZE) for y in range(Y_SIZE)]
    for hi in range(HI_SIZE)
]
CONTRACT_LAST = (((1,), (1,)), ((), ()))
CONTRACT_FIRST = (((0,), (0,)), ((), ()))
BF16, F32 = jnp.bfloat16, jnp.float32
WHOLE = pl.BlockSpec(memory_space=pltpu.VMEM)
SCALAR = pl.BlockSpec(memory_space=pltpu.SMEM)
ANYWHERE = pl.BlockSpec(memory_space=pl.ANY)


def limits():
    return pltpu.CompilerParams(vmem_limit_bytes=48 << 20)


def cost(flops, moved):
    return pl.CostEstimate(flops=flops, bytes_accessed=moved, transcendentals=0)


def across(value):
    experts = lax.axis_size("expert")
    pairs = []
    for dp in range(lax.axis_size("dp")):
        lo, core = divmod(dp, CORES)
        other_dp = (LO_SIZE - 1 - lo) * CORES + core
        for expert in range(experts):
            pairs.append((dp * experts + expert, other_dp * experts + (expert ^ Y_SIZE)))
    return lax.ppermute(value, BOTH, pairs)


def to_plane(blocks):
    return lax.all_to_all(
        blocks, "expert", split_axis=0, concat_axis=0, axis_index_groups=PLANE_GROUPS, tiled=True
    )


def lane_names(shape, half):
    place = lax.broadcasted_iota(jnp.int32, shape, 1) & (PLANE - 1)
    return (place >> 2) * (HI_SIZE * Y_SIZE) + half * Y_SIZE + (place & (Y_SIZE - 1))


def split_parts(values, shape):
    part = lax.broadcasted_iota(jnp.int32, shape, 1) >> 4
    high = values.astype(BF16).astype(F32)
    middle = (values - high).astype(BF16).astype(F32)
    low = values - high - middle
    chosen = jnp.where(part == 0, high, jnp.where(part == 1, middle, low))
    return jnp.where(part < PARTS, chosen, 0.0).astype(BF16)


def route_kernel(half_ref, ids_ref, gates_ref, own_ref, far_ref):
    half = half_ref[0]
    shape = own_ref.shape
    for which, ref in ((half, own_ref), (1 - half, far_ref)):
        names = lane_names(shape, which)
        total = jnp.zeros(shape, F32)
        for k in range(ids_ref.shape[1]):
            total += jnp.where(ids_ref[:, k : k + 1] == names, gates_ref[:, k : k + 1], 0.0)
        ref[...] = split_parts(total, shape)


def route(half, ids, gates):
    table = jax.ShapeDtypeStruct((ids.shape[0], SIDE), BF16)
    return pl.pallas_call(
        route_kernel,
        out_shape=(table, table),
        in_specs=[SCALAR, WHOLE, WHOLE],
        out_specs=(WHOLE, WHOLE),
        cost_estimate=cost(1000000, 200000),
        name="route",
    )(half, ids, gates)


def fill_kernel(sides_ref, tokens_ref, grads_ref, blocks_ref, picked_ref):
    rows = sides_ref.shape[0]
    width = tokens_ref.shape[1]
    turned = jnp.transpose(sides_ref[...].astype(F32))
    chosen = jnp.where(turned[:PLANE] > 0, 1.0, 0.0)
    before = jnp.where(
        lax.broadcasted_iota(jnp.int32, (rows, rows), 0)
        < lax.broadcasted_iota(jnp.int32, (rows, rows), 1),
        1.0,
        0.0,
    ).astype(BF16)
    rank = jnp.dot(chosen.astype(BF16), before, preferred_element_type=F32)
    rank = jnp.where(chosen > 0, rank, -1.0)
    slot = lax.broadcasted_iota(jnp.int32, (MOST, rows), 0).astype(F32)
    for j in range(PLANE):
        hit = jnp.where(rank[j : j + 1] == slot, 1.0, 0.0)
        picked_ref[j * MOST : (j + 1) * MOST, :] = hit.astype(BF16)
    picked = picked_ref[...]
    blocks_ref[:, width : width + SIDE] = jnp.dot(
        picked, sides_ref[...], preferred_element_type=F32
    ).astype(BF16)
    step = min(512, width)
    for n in range(0, width, step):
        blocks_ref[:, n : n + step] = jnp.dot(
            picked, tokens_ref[:, n : n + step], preferred_element_type=F32
        ).astype(BF16)
        blocks_ref[:, width + SIDE + n : width + SIDE + n + step] = jnp.dot(
            picked, grads_ref[:, n : n + step], preferred_element_type=F32
        ).astype(BF16)


def fill(sides, tokens, grads):
    rows, width = tokens.shape
    slots = PLANE * MOST
    return pl.pallas_call(
        fill_kernel,
        out_shape=(
            jax.ShapeDtypeStruct((slots, 2 * width + SIDE), BF16),
            jax.ShapeDtypeStruct((slots, rows), BF16),
        ),
        in_specs=[WHOLE] * 3,
        out_specs=(WHOLE, WHOLE),
        compiler_params=limits(),
        cost_estimate=cost(4 * slots * rows * width, 8 * slots * width),
        name="fill",
    )(sides, tokens, grads)


def expert_kernel(
    which, place_ref, rows_ref, gate_hbm, up_hbm, down_hbm, *refs
):
    if which:
        refs = refs[1:]
    back_ref, hidden_ref, pick_ref, grads_ref, gate_w, up_w, down_w, sems = refs
    copies = [
        pltpu.make_async_copy(source, target, sems.at[i])
        for i, (source, target) in enumerate(
            ((gate_hbm, gate_w), (up_hbm, up_w), (down_hbm, down_w))
        )
    ]
    for copy in copies:
        copy.start()
    place = place_ref[0]
    slots = rows_ref.shape[0]
    width, hidden_width = gate_w.shape
    lane = lax.broadcasted_iota(jnp.int32, (slots, SIDE), 1)
    mine = jnp.where((lane & (PLANE - 1)) == place, 1.0, 0.0)
    side = rows_ref[:, width : width + SIDE].astype(F32)
    slot_gate = jnp.sum(side * mine, axis=1, keepdims=True)
    pick_ref[...] = (slot_gate * rows_ref[:, width + SIDE :].astype(F32)).astype(BF16)
    for copy in copies:
        copy.wait()

    step = min(256, hidden_width)

    def forward(j, carry):
        span = pl.ds(pl.multiple_of(j * step, step), step)
        gate_pre = jnp.dot(rows_ref[:, :width], gate_w[:, span], preferred_element_type=F32)
        up_pre = jnp.dot(rows_ref[:, :width], up_w[:, span], preferred_element_type=F32)
        hidden_grad = lax.dot_general(
            pick_ref[...], down_w[span, :], CONTRACT_LAST, preferred_element_type=F32
        )
        sigmoid = jax.nn.sigmoid(gate_pre)
        silu = gate_pre * sigmoid
        hidden_ref[:, span] = (silu * up_pre).astype(BF16)
        gate_grad = hidden_grad * up_pre * sigmoid * (1.0 + gate_pre * (1.0 - sigmoid))
        grads_ref[:, span] = gate_grad.astype(BF16)
        second = pl.ds(pl.multiple_of(hidden_width + j * step, step), step)
        grads_ref[:, second] = (hidden_grad * silu).astype(BF16)
        return carry

    lax.fori_loop(0, hidden_width // step, forward, 0)

    wide = min(256, width)
    lead = back_ref.shape[:2]

    def outward(n, dots):
        start = pl.multiple_of(n * wide, wide)
        out = jnp.dot(hidden_ref[...], down_w[:, pl.ds(start, wide)], preferred_element_type=F32)
        ahead = pl.ds(pl.multiple_of(width + SIDE + n * wide, SIDE), wide)
        dots += jnp.sum(rows_ref[:, ahead].astype(F32) * out, axis=1, keepdims=True)
        back_ref[:, :, pl.ds(start, wide)] = (slot_gate * out).astype(BF16).reshape(*lead, wide)
        row_grad = lax.dot_general(
            grads_ref[:, :hidden_width],
            gate_w[pl.ds(start, wide), :],
            CONTRACT_LAST,
            preferred_element_type=F32,
        )
        row_grad += lax.dot_general(
            grads_ref[:, hidden_width:],
            up_w[pl.ds(start, wide), :],
            CONTRACT_LAST,
            preferred_element_type=F32,
        )
        back_ref[:, :, ahead] = row_grad.astype(BF16).reshape(*lead, wide)
        return dots

    dots = lax.fori_loop(0, width // wide, outward, jnp.zeros((slots, 1), F32))
    table = split_parts(dots * mine, (slots, SIDE))
    back_ref[:, :, width : width + SIDE] = table.reshape(*lead, SIDE)


def run_expert(which, place, rows, weights, back):
    slots = rows.shape[0]
    width, hidden_width = weights[0].shape
    full = 2 * width + SIDE
    out_shape = (
        jax.ShapeDtypeStruct((PLANE, 2 * MOST, full), BF16),
        jax.ShapeDtypeStruct((slots, hidden_width), BF16),
        jax.ShapeDtypeStruct((slots, width), BF16),
        jax.ShapeDtypeStruct((slots, 2 * hidden_width), BF16),
    )
    operands = [place, rows, *weights] + ([back] if which else [])
    return pl.pallas_call(
        functools.partial(expert_kernel, which),
        grid=(1,),
        out_shape=out_shape,
        in_specs=[SCALAR, pl.BlockSpec((slots, full), lambda i: (0, 0))]
        + [ANYWHERE] * (len(operands) - 2),
        out_specs=(
            pl.BlockSpec((PLANE, MOST, full), lambda i: (0, which, 0)),
            pl.BlockSpec((slots, hidden_width), lambda i: (0, 0)),
            pl.BlockSpec((slots, width), lambda i: (0, 0)),
            pl.BlockSpec((slots, 2 * hidden_width), lambda i: (0, 0)),
        ),
        scratch_shapes=[
            pltpu.VMEM((width, hidden_width), BF16),
            pltpu.VMEM((width, hidden_width), BF16),
            pltpu.VMEM((hidden_width, width), BF16),
            pltpu.SemaphoreType.DMA((3,)),
        ],
        input_output_aliases={5: 0} if which else {},
        compiler_params=limits(),
        cost_estimate=cost(12 * slots * width * hidden_width, 6 * width * hidden_width),
        name="expert",
    )(*operands)


def wide_kernel(has_sum, select_ref, near_x, far_x, near_grads, far_grads, *refs):
    out_ref = refs[-1]
    columns = out_ref.shape[2]
    step = min(512, columns)
    for n in range(0, columns, step):
        total = lax.dot_general(
            near_x[...], near_grads[:, n : n + step], CONTRACT_FIRST, preferred_element_type=F32
        )
        total += lax.dot_general(
            far_x[...], far_grads[:, n : n + step], CONTRACT_FIRST, preferred_element_type=F32
        )
        if has_sum:
            total += refs[0][0, :, n : n + step].astype(F32)
        out_ref[0, :, n : n + step] = total.astype(BF16)


def wide_grads(select, rows, grads, width, taken=None):
    shard = width // (LO_SIZE * CORES)
    slots, columns = grads[0].shape
    block = pl.BlockSpec((1, shard, columns), lambda z, s: (z, 0, 0))
    pick = pl.BlockSpec((slots, shard), lambda z, s: (0, z * CORES + s[0]))
    same = pl.BlockSpec((slots, columns), lambda z, s: (0, 0))
    extra = [] if taken is None else [taken]
    return pl.pallas_call(
        functools.partial(wide_kernel, taken is not None),
        grid_spec=pltpu.PrefetchScalarGridSpec(
            num_scalar_prefetch=1,
            grid=(LO_SIZE,),
            in_specs=[pick, pick, same, same] + [block] * len(extra),
            out_specs=block,
        ),
        out_shape=jax.ShapeDtypeStruct((LO_SIZE, shard, columns), BF16),
        compiler_params=limits(),
        cost_estimate=cost(2 * slots * width * columns, 2 * width * columns),
        name="wide",
    )(select, *rows, *grads, *extra)


def down_kernel(core_ref, near_hidden, far_hidden, near_pick, far_pick, give_ref, keep_ref, acc):
    core = core_ref[0]
    shard = give_ref.shape[1]
    acc[...] = lax.dot_general(
        near_hidden[...], near_pick[...], CONTRACT_FIRST, preferred_element_type=F32
    )
    acc[...] += lax.dot_general(
        far_hidden[...], far_pick[...], CONTRACT_FIRST, preferred_element_type=F32
    )
    for z in range(LO_SIZE):
        for which, ref in ((1 - core, give_ref), (core, keep_ref)):
            start = pl.multiple_of((z * CORES + which) * shard, shard)
            ref[z] = acc[pl.ds(start, shard), :].astype(BF16)


def down_grads(core, hidden, pick):
    slots, hidden_width = hidden[0].shape
    width = pick[0].shape[1]
    shard = hidden_width // (LO_SIZE * CORES)
    step = min(512, width)
    same = pl.BlockSpec((slots, hidden_width), lambda n, s: (0, 0))
    part = pl.BlockSpec((slots, step), lambda n, s: (0, n))
    block = pl.BlockSpec((LO_SIZE, shard, step), lambda n, s: (0, 0, n))
    shape = jax.ShapeDtypeStruct((LO_SIZE, shard, width), BF16)
    return pl.pallas_call(
        down_kernel,
        grid_spec=pltpu.PrefetchScalarGridSpec(
            num_scalar_prefetch=1,
            grid=(width // step,),
            in_specs=[same, same, part, part],
            out_specs=(block, block),
            scratch_shapes=[pltpu.VMEM((hidden_width, step), F32)],
        ),
        out_shape=(shape, shape),
        compiler_params=limits(),
        cost_estimate=cost(4 * slots * width * hidden_width, 4 * width * hidden_width),
        name="down",
    )(core, *hidden, *pick)


def turned_picks(picked_ref):
    return jnp.transpose(picked_ref[...].astype(F32)).astype(BF16)


def gather_rows(turned, returned_ref, start, size):
    block = returned_ref[:, :, start : start + size].reshape(PLANE * MOST, size)
    return jnp.dot(turned, block, preferred_element_type=F32)


def spans(width):
    step = min(512, width)
    return [(n, step) for n in range(0, width, step)]


def collect_kernel(picked_ref, returned_ref, out_ref):
    turned = turned_picks(picked_ref)
    full = out_ref.shape[1]
    width = (full - SIDE) // 2
    for start, size in spans(width) + [(width, SIDE)] + [
        (width + SIDE + n, step) for n, step in spans(width)
    ]:
        out_ref[:, start : start + size] = gather_rows(turned, returned_ref, start, size).astype(
            BF16
        )


def collect(picked, returned, which):
    slots, rows = picked.shape
    full = returned.shape[2]
    return pl.pallas_call(
        collect_kernel,
        grid=(1,),
        in_specs=[
            pl.BlockSpec((slots, rows), lambda i: (0, 0)),
            pl.BlockSpec((PLANE, MOST, full), lambda i: (0, which, 0)),
        ],
        out_specs=pl.BlockSpec((rows, full), lambda i: (0, 0)),
        out_shape=jax.ShapeDtypeStruct((rows, full), BF16),
        compiler_params=limits(),
        cost_estimate=cost(2 * slots * rows * full, 2 * slots * full),
        name="collect",
    )(picked, returned)


def finish_kernel(half_ref, ids_ref, picked_ref, returned_ref, far_ref, out_ref, token_ref, gate_ref):
    turned = turned_picks(picked_ref)
    rows, width = out_ref.shape
    for n, step in spans(width):
        near = gather_rows(turned, returned_ref, n, step)
        out_ref[:, n : n + step] = (near + far_ref[:, n : n + step].astype(F32)).astype(BF16)
        start = width + SIDE + n
        near = gather_rows(turned, returned_ref, start, step)
        far = far_ref[:, start : start + step].astype(F32)
        token_ref[:, n : n + step] = (near + far).astype(BF16)
    near_dots = gather_rows(turned, returned_ref, width, SIDE)
    far_dots = far_ref[:, width : width + SIDE].astype(F32)
    half = half_ref[0]
    near_names = lane_names((rows, SIDE), half)
    far_names = lane_names((rows, SIDE), 1 - half)
    for k in range(ids_ref.shape[1]):
        ids = ids_ref[:, k : k + 1]
        found = jnp.where(ids == near_names, near_dots, 0.0)
        found += jnp.where(ids == far_names, far_dots, 0.0)
        gate_ref[:, k : k + 1] = jnp.sum(found, axis=1, keepdims=True)


def finish(half, ids, picked, returned, far_total):
    slots, rows = picked.shape
    full = returned.shape[2]
    width = (full - SIDE) // 2
    whole = lambda shape: pl.BlockSpec(shape, lambda i: (0,) * len(shape))
    wide = jax.ShapeDtypeStruct((rows, width), BF16)
    return pl.pallas_call(
        finish_kernel,
        grid=(1,),
        in_specs=[
            SCALAR,
            whole(ids.shape),
            whole(picked.shape),
            pl.BlockSpec((PLANE, MOST, full), lambda i: (0, 0, 0)),
            whole(far_total.shape),
        ],
        out_specs=(whole((rows, width)), whole((rows, width)), whole(ids.shape)),
        out_shape=(wide, wide, jax.ShapeDtypeStruct(ids.shape, F32)),
        compiler_params=limits(),
        cost_estimate=cost(2 * slots * rows * full, 2 * slots * full),
        name="finish",
    )(half, ids, picked, returned, far_total)


def neighbours(steps):
    return [(a * CORES + core, b * CORES + core) for a, b in steps for core in range(CORES)]


def core_swap(give):
    return lax.ppermute(give, "dp", [(i, i ^ 1) for i in range(LO_SIZE * CORES)])


def shard_of(parts, index):
    index = jnp.clip(index, 0, LO_SIZE - 1)
    return lax.dynamic_index_in_dim(parts, index, axis=0, keepdims=False).astype(F32)


def line_sum(parts, lo):
    first = jnp.where(lo == 0, parts[LO_SIZE - 1], parts[0])
    arrived = lax.ppermute(first, "dp", neighbours([(0, 1), (3, 2)])).astype(F32)
    up = (shard_of(parts, lo + 2) + arrived).astype(BF16)
    down = (shard_of(parts, lo - 2) + arrived).astype(BF16)
    up = lax.ppermute(up, "dp", neighbours([(0, 1), (1, 2)]))
    down = lax.ppermute(down, "dp", neighbours([(3, 2), (2, 1)]))
    middle = up
    up = (shard_of(parts, lo + 1) + up.astype(F32)).astype(BF16)
    down = (shard_of(parts, lo - 1) + down.astype(F32)).astype(BF16)
    up = lax.ppermute(up, "dp", neighbours([(0, 1), (1, 2), (2, 3)])).astype(F32)
    down = lax.ppermute(down, "dp", neighbours([(3, 2), (2, 1), (1, 0)])).astype(F32)
    return (shard_of(parts, lo) + up + down).astype(BF16), middle


def on_device(tokens, out_grad, expert_ids, route_gates, swap_flags, gate_proj, up_proj, down_proj):
    devices = lax.axis_size("expert")
    my_expert = lax.axis_index("expert")
    lo = lax.axis_index("dp") // CORES
    core = lax.axis_index("dp") % CORES
    half = ((my_expert // Y_SIZE) % HI_SIZE).astype(jnp.int32)[None]
    place = (my_expert // (HI_SIZE * Y_SIZE)) * Y_SIZE + my_expert % Y_SIZE
    place = place.astype(jnp.int32)[None]
    here = core.astype(jnp.int32)[None]
    width = tokens.shape[1]
    hidden_width = gate_proj.shape[2]
    weights = (gate_proj[0], up_proj[0], down_proj[0])

    far_tokens = across(tokens)
    far_out_grad = across(out_grad)
    own_sides, far_sides = route(half, expert_ids, route_gates)
    far_sides = across(far_sides)
    near_blocks, near_picked = fill(own_sides, tokens, out_grad)
    near_rows = to_plane(near_blocks.reshape(PLANE, MOST, -1)).reshape(PLANE * MOST, -1)

    far_tokens, near_blocks = lax.optimization_barrier((far_tokens, near_blocks))
    far_blocks, far_picked = fill(far_sides, far_tokens, far_out_grad)
    far_rows = to_plane(far_blocks.reshape(PLANE, MOST, -1)).reshape(PLANE * MOST, -1)

    back, near_hidden, near_pick, near_grads = run_expert(0, place, near_rows, weights, None)
    back, far_hidden, far_pick, far_grads = run_expert(1, place, far_rows, weights, back)

    rows, grads = (near_rows, far_rows), (near_grads, far_grads)
    taken = core_swap(wide_grads(1 - here, rows, grads, width))
    give_down, keep_down = down_grads(here, (near_hidden, far_hidden), (near_pick, far_pick))
    taken_down = core_swap(give_down)
    gate_up_parts = wide_grads(here, rows, grads, width, taken)
    down_parts = (keep_down.astype(F32) + taken_down.astype(F32)).astype(BF16)
    gate_up_sum, middle = line_sum(gate_up_parts, lo)
    down_sum, unused = line_sum(down_parts, lo)

    returned = to_plane(back)
    returned, middle = lax.optimization_barrier((returned, middle))
    far_total = across(collect(far_picked, returned, 1))
    layer_out, grad_tokens, gate_grads = finish(half, expert_ids, near_picked, returned, far_total)

    is_moved = swap_flags[my_expert] == 1
    swap = [(i, i ^ (devices // 2)) for i in range(devices)]
    other_gate_up = lax.ppermute(gate_up_sum, "expert", swap)
    other_down = lax.ppermute(down_sum, "expert", swap)
    gate_up_sum = jnp.where(is_moved, other_gate_up, gate_up_sum)
    down_sum = jnp.where(is_moved, other_down, down_sum)
    grad_gate = gate_up_sum[:, :hidden_width]
    grad_up = gate_up_sum[:, hidden_width:]
    return (layer_out, grad_tokens, gate_grads, grad_gate[None], grad_up[None], down_sum[None])


def solution(mesh):
    return jax.shard_map(
        on_device,
        mesh=mesh,
        in_specs=(
            P(("dp", "expert"), None),
            P(("dp", "expert"), None),
            P(("dp", "expert"), None),
            P(("dp", "expert"), None),
            P(),
            P("expert", None, None),
            P("expert", None, None),
            P("expert", None, None),
        ),
        out_specs=(
            P(("dp", "expert"), None),
            P(("dp", "expert"), None),
            P(("dp", "expert"), None),
            P("expert", "dp", None),
            P("expert", "dp", None),
            P("expert", "dp", None),
        ),
        check_vma=False,
    )
```

```python
import functools

import jax
import jax.numpy as jnp
from jax import lax
from jax.experimental import pallas as pl
from jax.experimental.pallas import tpu as pltpu
from jax.sharding import PartitionSpec as P

MOST = 16
X_SIZE, HI_SIZE, Y_SIZE = 4, 2, 4
LO_SIZE, CORES = 4, 2
PLANE = 16
SIDE = 128
PARTS = 3

BOTH = ("dp", "expert")
PLANE_GROUPS = [
    [x * HI_SIZE * Y_SIZE + hi * Y_SIZE + y for y in range(Y_SIZE) for x in range(X_SIZE)]
    for hi in range(HI_SIZE)
]
CONTRACT_LAST = (((1,), (1,)), ((), ()))
CONTRACT_FIRST = (((0,), (0,)), ((), ()))
BF16, F32 = jnp.bfloat16, jnp.float32
WHOLE = pl.BlockSpec(memory_space=pltpu.VMEM)
SCALAR = pl.BlockSpec(memory_space=pltpu.SMEM)
ANYWHERE = pl.BlockSpec(memory_space=pl.ANY)


def limits():
    return pltpu.CompilerParams(vmem_limit_bytes=48 << 20)


def cost(flops, moved):
    return pl.CostEstimate(flops=flops, bytes_accessed=moved, transcendentals=0)


def across(value):
    experts = lax.axis_size("expert")
    pairs = []
    for dp in range(lax.axis_size("dp")):
        lo, core = divmod(dp, CORES)
        other_dp = (LO_SIZE - 1 - lo) * CORES + core
        for expert in range(experts):
            pairs.append((dp * experts + expert, other_dp * experts + (expert ^ Y_SIZE)))
    return lax.ppermute(value, BOTH, pairs)


def to_plane(blocks):
    return lax.all_to_all(
        blocks, "expert", split_axis=0, concat_axis=0, axis_index_groups=PLANE_GROUPS, tiled=True
    )


def lane_names(shape, half):
    place = lax.broadcasted_iota(jnp.int32, shape, 1) & (PLANE - 1)
    return (place & (X_SIZE - 1)) * (HI_SIZE * Y_SIZE) + half * Y_SIZE + (place >> 2)


def split_parts(values, shape):
    part = lax.broadcasted_iota(jnp.int32, shape, 1) >> 4
    high = values.astype(BF16).astype(F32)
    middle = (values - high).astype(BF16).astype(F32)
    low = values - high - middle
    chosen = jnp.where(part == 0, high, jnp.where(part == 1, middle, low))
    return jnp.where(part < PARTS, chosen, 0.0).astype(BF16)


def route_kernel(half_ref, ids_ref, gates_ref, own_ref, far_ref):
    half = half_ref[0]
    shape = own_ref.shape
    for which, ref in ((half, own_ref), (1 - half, far_ref)):
        names = lane_names(shape, which)
        total = jnp.zeros(shape, F32)
        for k in range(ids_ref.shape[1]):
            total += jnp.where(ids_ref[:, k : k + 1] == names, gates_ref[:, k : k + 1], 0.0)
        ref[...] = split_parts(total, shape)


def route(half, ids, gates):
    table = jax.ShapeDtypeStruct((ids.shape[0], SIDE), BF16)
    return pl.pallas_call(
        route_kernel,
        out_shape=(table, table),
        in_specs=[SCALAR, WHOLE, WHOLE],
        out_specs=(WHOLE, WHOLE),
        cost_estimate=cost(1000000, 200000),
        name="route",
    )(half, ids, gates)


def fill_kernel(sides_ref, tokens_ref, grads_ref, blocks_ref, picked_ref):
    rows = sides_ref.shape[0]
    width = tokens_ref.shape[1]
    turned = jnp.transpose(sides_ref[...].astype(F32))
    chosen = jnp.where(turned[:PLANE] > 0, 1.0, 0.0)
    before = jnp.where(
        lax.broadcasted_iota(jnp.int32, (rows, rows), 0)
        < lax.broadcasted_iota(jnp.int32, (rows, rows), 1),
        1.0,
        0.0,
    ).astype(BF16)
    rank = jnp.dot(chosen.astype(BF16), before, preferred_element_type=F32)
    rank = jnp.where(chosen > 0, rank, -1.0)
    slot = lax.broadcasted_iota(jnp.int32, (MOST, rows), 0).astype(F32)
    for j in range(PLANE):
        hit = jnp.where(rank[j : j + 1] == slot, 1.0, 0.0)
        picked_ref[j * MOST : (j + 1) * MOST, :] = hit.astype(BF16)
    picked = picked_ref[...]
    blocks_ref[:, width : width + SIDE] = jnp.dot(
        picked, sides_ref[...], preferred_element_type=F32
    ).astype(BF16)
    step = min(512, width)
    for n in range(0, width, step):
        blocks_ref[:, n : n + step] = jnp.dot(
            picked, tokens_ref[:, n : n + step], preferred_element_type=F32
        ).astype(BF16)
        blocks_ref[:, width + SIDE + n : width + SIDE + n + step] = jnp.dot(
            picked, grads_ref[:, n : n + step], preferred_element_type=F32
        ).astype(BF16)


def fill(sides, tokens, grads):
    rows, width = tokens.shape
    slots = PLANE * MOST
    return pl.pallas_call(
        fill_kernel,
        out_shape=(
            jax.ShapeDtypeStruct((slots, 2 * width + SIDE), BF16),
            jax.ShapeDtypeStruct((slots, rows), BF16),
        ),
        in_specs=[WHOLE] * 3,
        out_specs=(WHOLE, WHOLE),
        compiler_params=limits(),
        cost_estimate=cost(4 * slots * rows * width, 8 * slots * width),
        name="fill",
    )(sides, tokens, grads)


def expert_kernel(
    place_ref,
    rows_ref,
    gate_hbm,
    up_hbm,
    down_hbm,
    back_ref,
    hidden_ref,
    pick_ref,
    grads_ref,
    gate_w,
    up_w,
    down_w,
    sems,
):
    width, hidden_width = gate_w.shape
    step = min(256, hidden_width)
    chunks = []
    for j in range(hidden_width // step):
        span = pl.ds(j * step, step)
        pairs = (
            (gate_hbm.at[:, span], gate_w.at[:, span]),
            (up_hbm.at[:, span], up_w.at[:, span]),
            (down_hbm.at[span, :], down_w.at[span, :]),
        )
        chunks.append(
            [pltpu.make_async_copy(*pair, sems.at[j, i]) for i, pair in enumerate(pairs)]
        )
    for chunk in chunks:
        for copy in chunk:
            copy.start()
    place = place_ref[0]
    slots = rows_ref.shape[0]
    lane = lax.broadcasted_iota(jnp.int32, (slots, SIDE), 1)
    mine = jnp.where((lane & (PLANE - 1)) == place, 1.0, 0.0)
    side = rows_ref[:, width : width + SIDE].astype(F32)
    slot_gate = jnp.sum(side * mine, axis=1, keepdims=True)
    pick_ref[...] = (slot_gate * rows_ref[:, width + SIDE :].astype(F32)).astype(BF16)

    for j, chunk in enumerate(chunks):
        for copy in chunk:
            copy.wait()
        span = slice(j * step, (j + 1) * step)
        gate_pre = jnp.dot(rows_ref[:, :width], gate_w[:, span], preferred_element_type=F32)
        up_pre = jnp.dot(rows_ref[:, :width], up_w[:, span], preferred_element_type=F32)
        hidden_grad = lax.dot_general(
            pick_ref[...], down_w[span, :], CONTRACT_LAST, preferred_element_type=F32
        )
        sigmoid = jax.nn.sigmoid(gate_pre)
        silu = gate_pre * sigmoid
        hidden_ref[:, span] = (silu * up_pre).astype(BF16)
        gate_grad = hidden_grad * up_pre * sigmoid * (1.0 + gate_pre * (1.0 - sigmoid))
        grads_ref[:, span] = gate_grad.astype(BF16)
        second = slice(hidden_width + j * step, hidden_width + (j + 1) * step)
        grads_ref[:, second] = (hidden_grad * silu).astype(BF16)

    wide = min(256, width)
    lead = back_ref.shape[:2]

    def outward(n, dots):
        start = pl.multiple_of(n * wide, wide)
        out = jnp.dot(hidden_ref[...], down_w[:, pl.ds(start, wide)], preferred_element_type=F32)
        ahead = pl.ds(pl.multiple_of(width + SIDE + n * wide, SIDE), wide)
        dots += jnp.sum(rows_ref[:, ahead].astype(F32) * out, axis=1, keepdims=True)
        back_ref[:, :, pl.ds(start, wide)] = (slot_gate * out).astype(BF16).reshape(*lead, wide)
        row_grad = lax.dot_general(
            grads_ref[:, :hidden_width],
            gate_w[pl.ds(start, wide), :],
            CONTRACT_LAST,
            preferred_element_type=F32,
        )
        row_grad += lax.dot_general(
            grads_ref[:, hidden_width:],
            up_w[pl.ds(start, wide), :],
            CONTRACT_LAST,
            preferred_element_type=F32,
        )
        back_ref[:, :, ahead] = row_grad.astype(BF16).reshape(*lead, wide)
        return dots

    dots = lax.fori_loop(0, width // wide, outward, jnp.zeros((slots, 1), F32))
    table = split_parts(dots * mine, (slots, SIDE))
    back_ref[:, :, width : width + SIDE] = table.reshape(*lead, SIDE)


def run_expert(place, rows, weights):
    slots = rows.shape[0]
    width, hidden_width = weights[0].shape
    full = 2 * width + SIDE
    pieces = hidden_width // min(256, hidden_width)
    return pl.pallas_call(
        expert_kernel,
        out_shape=(
            jax.ShapeDtypeStruct((PLANE, MOST, full), BF16),
            jax.ShapeDtypeStruct((slots, hidden_width), BF16),
            jax.ShapeDtypeStruct((slots, width), BF16),
            jax.ShapeDtypeStruct((slots, 2 * hidden_width), BF16),
        ),
        in_specs=[SCALAR, WHOLE] + [ANYWHERE] * 3,
        out_specs=(WHOLE,) * 4,
        scratch_shapes=[
            pltpu.VMEM((width, hidden_width), BF16),
            pltpu.VMEM((width, hidden_width), BF16),
            pltpu.VMEM((hidden_width, width), BF16),
            pltpu.SemaphoreType.DMA((pieces, 3)),
        ],
        compiler_params=limits(),
        cost_estimate=cost(12 * slots * width * hidden_width, 6 * width * hidden_width),
        name="expert",
    )(place, rows, *weights)


def wide_kernel(keep, shard, where_ref, near_x, far_x, near_grads, far_grads, *refs):
    turned, columns = refs[-2:]
    slots = near_x.shape[0]

    @pl.when(pl.program_id(0) == 0)
    def _():
        for z in range(LO_SIZE):
            span = pl.ds(pl.multiple_of((z * CORES + where_ref[0]) * shard, shard), shard)
            here = slice(z * shard, (z + 1) * shard)
            turned[here, :slots] = jnp.transpose(near_x[:, span])
            turned[here, slots:] = jnp.transpose(far_x[:, span])

    columns[:slots] = near_grads[...]
    columns[slots:] = far_grads[...]
    total = jnp.dot(turned[...], columns[...], preferred_element_type=F32)
    if keep:
        taken_ref, out_ref, first_ref = refs[:3]
        for z in range(LO_SIZE):
            part = total[z * shard : (z + 1) * shard] + taken_ref[z].astype(F32)
            part = part.astype(BF16)
            out_ref[z] = part
            if z in (0, LO_SIZE - 1):

                @pl.when((where_ref[1] == 0) == (z != 0))
                def _():
                    first_ref[...] = part
    else:
        for z in range(LO_SIZE):
            refs[0][z] = total[z * shard : (z + 1) * shard].astype(BF16)


def wide_grads(where, rows, grads, width, taken=None):
    shard = width // (LO_SIZE * CORES)
    slots, columns = grads[0].shape
    step = min(512, columns)
    block = pl.BlockSpec((LO_SIZE, shard, step), lambda n, s: (0, 0, n))
    tokens = pl.BlockSpec((slots, width), lambda n, s: (0, 0))
    part = pl.BlockSpec((slots, step), lambda n, s: (0, n))
    shape = jax.ShapeDtypeStruct((LO_SIZE, shard, columns), BF16)
    extra = [] if taken is None else [taken]
    first = jax.ShapeDtypeStruct((shard, columns), BF16)
    first_block = pl.BlockSpec((shard, step), lambda n, s: (0, n))
    return pl.pallas_call(
        functools.partial(wide_kernel, taken is not None, shard),
        grid_spec=pltpu.PrefetchScalarGridSpec(
            num_scalar_prefetch=1,
            grid=(columns // step,),
            in_specs=[tokens, tokens, part, part] + [block] * len(extra),
            out_specs=(block, first_block) if extra else block,
            scratch_shapes=[
                pltpu.VMEM((LO_SIZE * shard, 2 * slots), BF16),
                pltpu.VMEM((2 * slots, step), BF16),
            ],
        ),
        out_shape=(shape, first) if extra else shape,
        compiler_params=limits(),
        cost_estimate=cost(2 * slots * width * columns, 2 * width * columns),
        name="wide",
    )(where, *rows, *grads, *extra)


def down_kernel(
    core_ref, near_hidden, far_hidden, near_pick, far_pick, give_ref, keep_ref, turned, columns, acc
):
    core = core_ref[0]
    shard = give_ref.shape[1]
    slots = near_hidden.shape[0]

    @pl.when(pl.program_id(0) == 0)
    def _():
        turned[:, :slots] = jnp.transpose(near_hidden[...])
        turned[:, slots:] = jnp.transpose(far_hidden[...])

    columns[:slots] = near_pick[...]
    columns[slots:] = far_pick[...]
    acc[...] = jnp.dot(turned[...], columns[...], preferred_element_type=F32)
    for z in range(LO_SIZE):
        for which, ref in ((1 - core, give_ref), (core, keep_ref)):
            start = pl.multiple_of((z * CORES + which) * shard, shard)
            ref[z] = acc[pl.ds(start, shard), :].astype(BF16)


def down_grads(core, hidden, pick):
    slots, hidden_width = hidden[0].shape
    width = pick[0].shape[1]
    shard = hidden_width // (LO_SIZE * CORES)
    step = min(512, width)
    same = pl.BlockSpec((slots, hidden_width), lambda n, s: (0, 0))
    part = pl.BlockSpec((slots, step), lambda n, s: (0, n))
    block = pl.BlockSpec((LO_SIZE, shard, step), lambda n, s: (0, 0, n))
    shape = jax.ShapeDtypeStruct((LO_SIZE, shard, width), BF16)
    return pl.pallas_call(
        down_kernel,
        grid_spec=pltpu.PrefetchScalarGridSpec(
            num_scalar_prefetch=1,
            grid=(width // step,),
            in_specs=[same, same, part, part],
            out_specs=(block, block),
            scratch_shapes=[
                pltpu.VMEM((hidden_width, 2 * slots), BF16),
                pltpu.VMEM((2 * slots, step), BF16),
                pltpu.VMEM((hidden_width, step), F32),
            ],
        ),
        out_shape=(shape, shape),
        compiler_params=limits(),
        cost_estimate=cost(4 * slots * width * hidden_width, 4 * width * hidden_width),
        name="down",
    )(core, *hidden, *pick)


def turned_picks(picked_ref):
    return jnp.transpose(picked_ref[...].astype(F32)).astype(BF16)


def gather_rows(turned, returned_ref, start, size):
    block = returned_ref[:, :, start : start + size].reshape(PLANE * MOST, size)
    return jnp.dot(turned, block, preferred_element_type=F32)


def spans(width):
    step = min(512, width)
    return [(n, step) for n in range(0, width, step)]


def collect_kernel(picked_ref, returned_ref, out_ref):
    turned = turned_picks(picked_ref)
    full = out_ref.shape[1]
    width = (full - SIDE) // 2
    for start, size in spans(width) + [(width, SIDE)] + [
        (width + SIDE + n, step) for n, step in spans(width)
    ]:
        out_ref[:, start : start + size] = gather_rows(turned, returned_ref, start, size).astype(
            BF16
        )


def collect(picked, returned):
    slots, rows = picked.shape
    full = returned.shape[2]
    return pl.pallas_call(
        collect_kernel,
        in_specs=[WHOLE, WHOLE],
        out_specs=WHOLE,
        out_shape=jax.ShapeDtypeStruct((rows, full), BF16),
        compiler_params=limits(),
        cost_estimate=cost(2 * slots * rows * full, 2 * slots * full),
        name="collect",
    )(picked, returned)


def finish_kernel(half_ref, ids_ref, picked_ref, returned_ref, far_ref, out_ref, token_ref, gate_ref):
    turned = turned_picks(picked_ref)
    rows, width = out_ref.shape
    for n, step in spans(width):
        near = gather_rows(turned, returned_ref, n, step)
        out_ref[:, n : n + step] = (near + far_ref[:, n : n + step].astype(F32)).astype(BF16)
        start = width + SIDE + n
        near = gather_rows(turned, returned_ref, start, step)
        far = far_ref[:, start : start + step].astype(F32)
        token_ref[:, n : n + step] = (near + far).astype(BF16)
    near_dots = gather_rows(turned, returned_ref, width, SIDE)
    far_dots = far_ref[:, width : width + SIDE].astype(F32)
    half = half_ref[0]
    near_names = lane_names((rows, SIDE), half)
    far_names = lane_names((rows, SIDE), 1 - half)
    for k in range(ids_ref.shape[1]):
        ids = ids_ref[:, k : k + 1]
        found = jnp.where(ids == near_names, near_dots, 0.0)
        found += jnp.where(ids == far_names, far_dots, 0.0)
        gate_ref[:, k : k + 1] = jnp.sum(found, axis=1, keepdims=True)


def finish(half, ids, picked, returned, far_total):
    slots, rows = picked.shape
    full = returned.shape[2]
    width = (full - SIDE) // 2
    wide = jax.ShapeDtypeStruct((rows, width), BF16)
    return pl.pallas_call(
        finish_kernel,
        in_specs=[SCALAR] + [WHOLE] * 4,
        out_specs=(WHOLE,) * 3,
        out_shape=(wide, wide, jax.ShapeDtypeStruct(ids.shape, F32)),
        compiler_params=limits(),
        cost_estimate=cost(2 * slots * rows * full, 2 * slots * full),
        name="finish",
    )(half, ids, picked, returned, far_total)


def neighbours(steps):
    return [(a * CORES + core, b * CORES + core) for a, b in steps for core in range(CORES)]


def core_swap(give):
    return lax.ppermute(give, "dp", [(i, i ^ 1) for i in range(LO_SIZE * CORES)])


def shard_of(parts, index):
    index = jnp.clip(index, 0, LO_SIZE - 1)
    return lax.dynamic_index_in_dim(parts, index, axis=0, keepdims=False).astype(F32)


def line_sum(parts, first, lo):
    arrived = lax.ppermute(first, "dp", neighbours([(0, 1), (3, 2)])).astype(F32)
    up = (shard_of(parts, lo + 2) + arrived).astype(BF16)
    down = (shard_of(parts, lo - 2) + arrived).astype(BF16)
    middle = up
    up = lax.ppermute(up, "dp", neighbours([(0, 1), (1, 2)]))
    down = lax.ppermute(down, "dp", neighbours([(3, 2), (2, 1)]))
    up = (shard_of(parts, lo + 1) + up.astype(F32)).astype(BF16)
    down = (shard_of(parts, lo - 1) + down.astype(F32)).astype(BF16)
    up = lax.ppermute(up, "dp", neighbours([(0, 1), (1, 2), (2, 3)])).astype(F32)
    down = lax.ppermute(down, "dp", neighbours([(3, 2), (2, 1), (1, 0)])).astype(F32)
    return (shard_of(parts, lo) + up + down).astype(BF16), middle


def on_device(tokens, out_grad, expert_ids, route_gates, swap_flags, gate_proj, up_proj, down_proj):
    devices = lax.axis_size("expert")
    my_expert = lax.axis_index("expert")
    lo = lax.axis_index("dp") // CORES
    core = lax.axis_index("dp") % CORES
    half = ((my_expert // Y_SIZE) % HI_SIZE).astype(jnp.int32)[None]
    place = (my_expert % Y_SIZE) * X_SIZE + my_expert // (HI_SIZE * Y_SIZE)
    place = place.astype(jnp.int32)[None]
    here = core.astype(jnp.int32)[None]
    line = lo.astype(jnp.int32)[None]
    width = tokens.shape[1]
    hidden_width = gate_proj.shape[2]
    weights = (gate_proj[0], up_proj[0], down_proj[0])

    far_tokens = across(tokens)
    far_out_grad = across(out_grad)
    own_sides, far_sides = route(half, expert_ids, route_gates)
    far_sides = across(far_sides)
    far_tokens, far_sides, own_sides = lax.optimization_barrier((far_tokens, far_sides, own_sides))
    near_blocks, near_picked = fill(own_sides, tokens, out_grad)
    near_rows = to_plane(near_blocks.reshape(PLANE, MOST, -1)).reshape(PLANE * MOST, -1)
    far_blocks, far_picked = fill(far_sides, far_tokens, far_out_grad)
    far_blocks, near_blocks = lax.optimization_barrier((far_blocks, near_blocks))
    far_rows = to_plane(far_blocks.reshape(PLANE, MOST, -1)).reshape(PLANE * MOST, -1)

    near_back, near_hidden, near_pick, near_grads = run_expert(place, near_rows, weights)
    far_back, far_hidden, far_pick, far_grads = run_expert(place, far_rows, weights)

    rows, grads = (near_rows, far_rows), (near_grads, far_grads)
    give = wide_grads(jnp.concatenate([1 - here, line]), rows, grads, width)
    taken = core_swap(give)
    far_back, give = lax.optimization_barrier((far_back, give))
    far_returned = to_plane(far_back)
    give_down, keep_down = down_grads(here, (near_hidden, far_hidden), (near_pick, far_pick))
    taken, keep_down = lax.optimization_barrier((taken, keep_down))
    gate_up_parts, first = wide_grads(jnp.concatenate([here, line]), rows, grads, width, taken)
    give_down, first = lax.optimization_barrier((give_down, first))
    taken_down = core_swap(give_down)
    gate_up_sum, middle = line_sum(gate_up_parts, first, lo)
    down_parts = (keep_down.astype(F32) + taken_down.astype(F32)).astype(BF16)
    first_down = jnp.where(lo == 0, down_parts[LO_SIZE - 1], down_parts[0])
    down_sum, unused = line_sum(down_parts, first_down, lo)

    near_back, far_returned = lax.optimization_barrier((near_back, far_returned))
    near_returned = to_plane(near_back)
    far_returned, middle = lax.optimization_barrier((far_returned, middle))
    far_total = across(collect(far_picked, far_returned))
    layer_out, grad_tokens, gate_grads = finish(
        half, expert_ids, near_picked, near_returned, far_total
    )

    is_moved = swap_flags[my_expert] == 1
    swap = [(i, i ^ (devices // 2)) for i in range(devices)]
    other_gate_up = lax.ppermute(gate_up_sum, "expert", swap)
    other_down = lax.ppermute(down_sum, "expert", swap)
    gate_up_sum = jnp.where(is_moved, other_gate_up, gate_up_sum)
    down_sum = jnp.where(is_moved, other_down, down_sum)
    grad_gate = gate_up_sum[:, :hidden_width]
    grad_up = gate_up_sum[:, hidden_width:]
    return (layer_out, grad_tokens, gate_grads, grad_gate[None], grad_up[None], down_sum[None])


def solution(mesh):
    return jax.shard_map(
        on_device,
        mesh=mesh,
        in_specs=(
            P(("dp", "expert"), None),
            P(("dp", "expert"), None),
            P(("dp", "expert"), None),
            P(("dp", "expert"), None),
            P(),
            P("expert", None, None),
            P("expert", None, None),
            P("expert", None, None),
        ),
        out_specs=(
            P(("dp", "expert"), None),
            P(("dp", "expert"), None),
            P(("dp", "expert"), None),
            P("expert", "dp", None),
            P("expert", "dp", None),
            P("expert", "dp", None),
        ),
        check_vma=False,
    )
```

```python
import functools

import jax
import jax.numpy as jnp
from jax import lax
from jax.experimental import pallas as pl
from jax.experimental.pallas import tpu as pltpu
from jax.sharding import PartitionSpec as P

MOST = 16
X_SIZE, HI_SIZE, Y_SIZE = 4, 2, 4
LO_SIZE, CORES = 4, 2
PLANE = 16
SIDE = 128
PARTS = 3

BOTH = ("dp", "expert")
PLANE_GROUPS = [
    [x * HI_SIZE * Y_SIZE + hi * Y_SIZE + y for y in range(Y_SIZE) for x in range(X_SIZE)]
    for hi in range(HI_SIZE)
]
CONTRACT_LAST = (((1,), (1,)), ((), ()))
CONTRACT_FIRST = (((0,), (0,)), ((), ()))
BF16, F32 = jnp.bfloat16, jnp.float32
WHOLE = pl.BlockSpec(memory_space=pltpu.VMEM)
SCALAR = pl.BlockSpec(memory_space=pltpu.SMEM)
ANYWHERE = pl.BlockSpec(memory_space=pl.ANY)


def limits():
    return pltpu.CompilerParams(vmem_limit_bytes=48 << 20)


def cost(flops, moved):
    return pl.CostEstimate(flops=flops, bytes_accessed=moved, transcendentals=0)


def across(value):
    experts = lax.axis_size("expert")
    pairs = []
    for dp in range(lax.axis_size("dp")):
        lo, core = divmod(dp, CORES)
        other_dp = (LO_SIZE - 1 - lo) * CORES + core
        for expert in range(experts):
            pairs.append((dp * experts + expert, other_dp * experts + (expert ^ Y_SIZE)))
    return lax.ppermute(value, BOTH, pairs)


def to_plane(blocks):
    return lax.all_to_all(
        blocks, "expert", split_axis=0, concat_axis=0, axis_index_groups=PLANE_GROUPS, tiled=True
    )


def lane_names(shape, half):
    place = lax.broadcasted_iota(jnp.int32, shape, 1) & (PLANE - 1)
    return (place & (X_SIZE - 1)) * (HI_SIZE * Y_SIZE) + half * Y_SIZE + (place >> 2)


def split_parts(values, shape):
    part = lax.broadcasted_iota(jnp.int32, shape, 1) >> 4
    high = values.astype(BF16).astype(F32)
    middle = (values - high).astype(BF16).astype(F32)
    low = values - high - middle
    chosen = jnp.where(part == 0, high, jnp.where(part == 1, middle, low))
    return jnp.where(part < PARTS, chosen, 0.0).astype(BF16)


def route_kernel(half_ref, ids_ref, gates_ref, own_ref, far_ref):
    half = half_ref[0]
    shape = own_ref.shape
    for which, ref in ((half, own_ref), (1 - half, far_ref)):
        names = lane_names(shape, which)
        total = jnp.zeros(shape, F32)
        for k in range(ids_ref.shape[1]):
            total += jnp.where(ids_ref[:, k : k + 1] == names, gates_ref[:, k : k + 1], 0.0)
        ref[...] = split_parts(total, shape)


def route(half, ids, gates):
    table = jax.ShapeDtypeStruct((ids.shape[0], SIDE), BF16)
    return pl.pallas_call(
        route_kernel,
        out_shape=(table, table),
        in_specs=[SCALAR, WHOLE, WHOLE],
        out_specs=(WHOLE, WHOLE),
        cost_estimate=cost(1000000, 200000),
        name="route",
    )(half, ids, gates)


def fill_kernel(sides_ref, tokens_ref, grads_ref, blocks_ref, picked_ref):
    rows = sides_ref.shape[0]
    width = tokens_ref.shape[1]
    turned = jnp.transpose(sides_ref[...].astype(F32))
    chosen = jnp.where(turned[:PLANE] > 0, 1.0, 0.0)
    before = jnp.where(
        lax.broadcasted_iota(jnp.int32, (rows, rows), 0)
        < lax.broadcasted_iota(jnp.int32, (rows, rows), 1),
        1.0,
        0.0,
    ).astype(BF16)
    rank = jnp.dot(chosen.astype(BF16), before, preferred_element_type=F32)
    rank = jnp.where(chosen > 0, rank, -1.0)
    slot = lax.broadcasted_iota(jnp.int32, (MOST, rows), 0).astype(F32)
    for j in range(PLANE):
        hit = jnp.where(rank[j : j + 1] == slot, 1.0, 0.0)
        picked_ref[j * MOST : (j + 1) * MOST, :] = hit.astype(BF16)
    picked = picked_ref[...]
    blocks_ref[:, width : width + SIDE] = jnp.dot(
        picked, sides_ref[...], preferred_element_type=F32
    ).astype(BF16)
    step = min(512, width)
    for n in range(0, width, step):
        blocks_ref[:, n : n + step] = jnp.dot(
            picked, tokens_ref[:, n : n + step], preferred_element_type=F32
        ).astype(BF16)
        blocks_ref[:, width + SIDE + n : width + SIDE + n + step] = jnp.dot(
            picked, grads_ref[:, n : n + step], preferred_element_type=F32
        ).astype(BF16)


def fill(sides, tokens, grads, weight):
    rows, width = tokens.shape
    slots = PLANE * MOST
    return pl.pallas_call(
        fill_kernel,
        out_shape=(
            jax.ShapeDtypeStruct((slots, 2 * width + SIDE), BF16),
            jax.ShapeDtypeStruct((slots, rows), BF16),
        ),
        in_specs=[WHOLE] * 3,
        out_specs=(WHOLE, WHOLE),
        compiler_params=limits(),
        cost_estimate=cost(weight, 8 * slots * width),
        name="fill",
    )(sides, tokens, grads)


def expert_kernel(
    place_ref,
    rows_ref,
    gate_hbm,
    up_hbm,
    down_hbm,
    back_ref,
    hidden_ref,
    pick_ref,
    grads_ref,
    gate_w,
    up_w,
    down_w,
    sems,
):
    width, hidden_width = gate_w.shape
    step = min(256, hidden_width)
    chunks = []
    for j in range(hidden_width // step):
        span = pl.ds(j * step, step)
        pairs = (
            (gate_hbm.at[:, span], gate_w.at[:, span]),
            (up_hbm.at[:, span], up_w.at[:, span]),
            (down_hbm.at[span, :], down_w.at[span, :]),
        )
        chunks.append(
            [pltpu.make_async_copy(*pair, sems.at[j, i]) for i, pair in enumerate(pairs)]
        )
    for chunk in chunks:
        for copy in chunk:
            copy.start()
    place = place_ref[0]
    slots = rows_ref.shape[0]
    lane = lax.broadcasted_iota(jnp.int32, (slots, SIDE), 1)
    mine = jnp.where((lane & (PLANE - 1)) == place, 1.0, 0.0)
    side = rows_ref[:, width : width + SIDE].astype(F32)
    slot_gate = jnp.sum(side * mine, axis=1, keepdims=True)
    pick_ref[...] = (slot_gate * rows_ref[:, width + SIDE :].astype(F32)).astype(BF16)

    for j, chunk in enumerate(chunks):
        for copy in chunk:
            copy.wait()
        span = slice(j * step, (j + 1) * step)
        gate_pre = jnp.dot(rows_ref[:, :width], gate_w[:, span], preferred_element_type=F32)
        up_pre = jnp.dot(rows_ref[:, :width], up_w[:, span], preferred_element_type=F32)
        hidden_grad = lax.dot_general(
            pick_ref[...], down_w[span, :], CONTRACT_LAST, preferred_element_type=F32
        )
        sigmoid = jax.nn.sigmoid(gate_pre)
        silu = gate_pre * sigmoid
        hidden_ref[:, span] = (silu * up_pre).astype(BF16)
        gate_grad = hidden_grad * up_pre * sigmoid * (1.0 + gate_pre * (1.0 - sigmoid))
        grads_ref[:, span] = gate_grad.astype(BF16)
        second = slice(hidden_width + j * step, hidden_width + (j + 1) * step)
        grads_ref[:, second] = (hidden_grad * silu).astype(BF16)

    wide = min(256, width)
    lead = back_ref.shape[:2]

    def outward(n, dots):
        start = pl.multiple_of(n * wide, wide)
        out = jnp.dot(hidden_ref[...], down_w[:, pl.ds(start, wide)], preferred_element_type=F32)
        ahead = pl.ds(pl.multiple_of(width + SIDE + n * wide, SIDE), wide)
        dots += jnp.sum(rows_ref[:, ahead].astype(F32) * out, axis=1, keepdims=True)
        back_ref[:, :, pl.ds(start, wide)] = (slot_gate * out).astype(BF16).reshape(*lead, wide)
        row_grad = lax.dot_general(
            grads_ref[:, :hidden_width],
            gate_w[pl.ds(start, wide), :],
            CONTRACT_LAST,
            preferred_element_type=F32,
        )
        row_grad += lax.dot_general(
            grads_ref[:, hidden_width:],
            up_w[pl.ds(start, wide), :],
            CONTRACT_LAST,
            preferred_element_type=F32,
        )
        back_ref[:, :, ahead] = row_grad.astype(BF16).reshape(*lead, wide)
        return dots

    dots = lax.fori_loop(0, width // wide, outward, jnp.zeros((slots, 1), F32))
    table = split_parts(dots * mine, (slots, SIDE))
    back_ref[:, :, width : width + SIDE] = table.reshape(*lead, SIDE)


def run_expert(place, rows, weights):
    slots = rows.shape[0]
    width, hidden_width = weights[0].shape
    full = 2 * width + SIDE
    pieces = hidden_width // min(256, hidden_width)
    return pl.pallas_call(
        expert_kernel,
        out_shape=(
            jax.ShapeDtypeStruct((PLANE, MOST, full), BF16),
            jax.ShapeDtypeStruct((slots, hidden_width), BF16),
            jax.ShapeDtypeStruct((slots, width), BF16),
            jax.ShapeDtypeStruct((slots, 2 * hidden_width), BF16),
        ),
        in_specs=[SCALAR, WHOLE] + [ANYWHERE] * 3,
        out_specs=(WHOLE,) * 4,
        scratch_shapes=[
            pltpu.VMEM((width, hidden_width), BF16),
            pltpu.VMEM((width, hidden_width), BF16),
            pltpu.VMEM((hidden_width, width), BF16),
            pltpu.SemaphoreType.DMA((pieces, 3)),
        ],
        compiler_params=limits(),
        cost_estimate=cost(12 * slots * width * hidden_width, 6 * width * hidden_width),
        name="expert",
    )(place, rows, *weights)


def shard_start(where_ref, core, r, shard):
    lo = (where_ref[1] + r) & (LO_SIZE - 1)
    return pl.multiple_of((lo * CORES + core) * shard, shard)


def wide_kernel(keep, shard, where_ref, near_x, far_x, near_grads, far_grads, *refs):
    turned, columns = refs[-2:]
    slots = near_x.shape[0]
    core = where_ref[0] if keep else 1 - where_ref[0]

    @pl.when(pl.program_id(0) == 0)
    def _():
        for r in range(LO_SIZE):
            span = pl.ds(shard_start(where_ref, core, r, shard), shard)
            here = slice(r * shard, (r + 1) * shard)
            turned[here, :slots] = jnp.transpose(near_x[:, span])
            turned[here, slots:] = jnp.transpose(far_x[:, span])

    columns[:slots] = near_grads[...]
    columns[slots:] = far_grads[...]
    total = jnp.dot(turned[...], columns[...], preferred_element_type=F32)
    for r in range(LO_SIZE):
        part = total[r * shard : (r + 1) * shard]
        if keep:
            refs[1 + r][...] = (part + refs[0][r].astype(F32)).astype(BF16)
        else:
            refs[0][r] = part.astype(BF16)


def wide_grads(where, rows, grads, width, taken=None):
    shard = width // (LO_SIZE * CORES)
    slots, columns = grads[0].shape
    step = min(512, columns)
    block = pl.BlockSpec((LO_SIZE, shard, step), lambda n, s: (0, 0, n))
    tokens = pl.BlockSpec((slots, width), lambda n, s: (0, 0))
    part = pl.BlockSpec((slots, step), lambda n, s: (0, n))
    one = pl.BlockSpec((shard, step), lambda n, s: (0, n))
    keep = taken is not None
    if keep:
        out_shape = (jax.ShapeDtypeStruct((shard, columns), BF16),) * LO_SIZE
    else:
        out_shape = jax.ShapeDtypeStruct((LO_SIZE, shard, columns), BF16)
    return pl.pallas_call(
        functools.partial(wide_kernel, keep, shard),
        grid_spec=pltpu.PrefetchScalarGridSpec(
            num_scalar_prefetch=1,
            grid=(columns // step,),
            in_specs=[tokens, tokens, part, part] + ([block] if keep else []),
            out_specs=(one,) * LO_SIZE if keep else block,
            scratch_shapes=[
                pltpu.VMEM((LO_SIZE * shard, 2 * slots), BF16),
                pltpu.VMEM((2 * slots, step), BF16),
            ],
        ),
        out_shape=out_shape,
        compiler_params=limits(),
        cost_estimate=cost(2 * slots * width * columns, 2 * width * columns),
        name="wide",
    )(where, *rows, *grads, *([taken] if keep else []))


def down_kernel(
    where_ref, near_hidden, far_hidden, near_pick, far_pick, give_ref, keep_ref, turned, columns, acc
):
    core = where_ref[0]
    shard = give_ref.shape[1]
    slots = near_hidden.shape[0]

    @pl.when(pl.program_id(0) == 0)
    def _():
        turned[:, :slots] = jnp.transpose(near_hidden[...])
        turned[:, slots:] = jnp.transpose(far_hidden[...])

    columns[:slots] = near_pick[...]
    columns[slots:] = far_pick[...]
    acc[...] = jnp.dot(turned[...], columns[...], preferred_element_type=F32)
    for r in range(LO_SIZE):
        for which, ref in ((1 - core, give_ref), (core, keep_ref)):
            start = shard_start(where_ref, which, r, shard)
            ref[r] = acc[pl.ds(start, shard), :].astype(BF16)


def down_grads(where, hidden, pick):
    slots, hidden_width = hidden[0].shape
    width = pick[0].shape[1]
    shard = hidden_width // (LO_SIZE * CORES)
    step = min(512, width)
    same = pl.BlockSpec((slots, hidden_width), lambda n, s: (0, 0))
    part = pl.BlockSpec((slots, step), lambda n, s: (0, n))
    block = pl.BlockSpec((LO_SIZE, shard, step), lambda n, s: (0, 0, n))
    shape = jax.ShapeDtypeStruct((LO_SIZE, shard, width), BF16)
    return pl.pallas_call(
        down_kernel,
        grid_spec=pltpu.PrefetchScalarGridSpec(
            num_scalar_prefetch=1,
            grid=(width // step,),
            in_specs=[same, same, part, part],
            out_specs=(block, block),
            scratch_shapes=[
                pltpu.VMEM((hidden_width, 2 * slots), BF16),
                pltpu.VMEM((2 * slots, step), BF16),
                pltpu.VMEM((hidden_width, step), F32),
            ],
        ),
        out_shape=(shape, shape),
        compiler_params=limits(),
        cost_estimate=cost(4 * slots * width * hidden_width, 4 * width * hidden_width),
        name="down",
    )(where, *hidden, *pick)


def turned_picks(picked_ref):
    return jnp.transpose(picked_ref[...].astype(F32)).astype(BF16)


def gather_rows(turned, returned_ref, start, size):
    block = returned_ref[:, :, start : start + size].reshape(PLANE * MOST, size)
    return jnp.dot(turned, block, preferred_element_type=F32)


def spans(width):
    step = min(512, width)
    return [(n, step) for n in range(0, width, step)]


def collect_kernel(picked_ref, returned_ref, out_ref):
    turned = turned_picks(picked_ref)
    full = out_ref.shape[1]
    width = (full - SIDE) // 2
    for start, size in spans(width) + [(width, SIDE)] + [
        (width + SIDE + n, step) for n, step in spans(width)
    ]:
        out_ref[:, start : start + size] = gather_rows(turned, returned_ref, start, size).astype(
            BF16
        )


def collect(picked, returned):
    slots, rows = picked.shape
    full = returned.shape[2]
    return pl.pallas_call(
        collect_kernel,
        in_specs=[WHOLE, WHOLE],
        out_specs=WHOLE,
        out_shape=jax.ShapeDtypeStruct((rows, full), BF16),
        compiler_params=limits(),
        cost_estimate=cost(2 * slots * rows * full, 2 * slots * full),
        name="collect",
    )(picked, returned)


def finish_kernel(half_ref, ids_ref, picked_ref, returned_ref, far_ref, out_ref, token_ref, gate_ref):
    turned = turned_picks(picked_ref)
    rows, width = out_ref.shape
    for n, step in spans(width):
        near = gather_rows(turned, returned_ref, n, step)
        out_ref[:, n : n + step] = (near + far_ref[:, n : n + step].astype(F32)).astype(BF16)
        start = width + SIDE + n
        near = gather_rows(turned, returned_ref, start, step)
        far = far_ref[:, start : start + step].astype(F32)
        token_ref[:, n : n + step] = (near + far).astype(BF16)
    near_dots = gather_rows(turned, returned_ref, width, SIDE)
    far_dots = far_ref[:, width : width + SIDE].astype(F32)
    half = half_ref[0]
    near_names = lane_names((rows, SIDE), half)
    far_names = lane_names((rows, SIDE), 1 - half)
    for k in range(ids_ref.shape[1]):
        ids = ids_ref[:, k : k + 1]
        found = jnp.where(ids == near_names, near_dots, 0.0)
        found += jnp.where(ids == far_names, far_dots, 0.0)
        gate_ref[:, k : k + 1] = jnp.sum(found, axis=1, keepdims=True)


def finish(half, ids, picked, returned, far_total):
    slots, rows = picked.shape
    full = returned.shape[2]
    width = (full - SIDE) // 2
    wide = jax.ShapeDtypeStruct((rows, width), BF16)
    return pl.pallas_call(
        finish_kernel,
        in_specs=[SCALAR] + [WHOLE] * 4,
        out_specs=(WHOLE,) * 3,
        out_shape=(wide, wide, jax.ShapeDtypeStruct(ids.shape, F32)),
        compiler_params=limits(),
        cost_estimate=cost(2 * slots * rows * full, 2 * slots * full),
        name="finish",
    )(half, ids, picked, returned, far_total)


def core_swap(give):
    return lax.ppermute(give, "dp", [(i, i ^ 1) for i in range(LO_SIZE * CORES)])


def shift(value, distance, leave=()):
    pairs = [(lo, (lo + distance) % LO_SIZE) for lo in range(LO_SIZE) if lo not in leave]
    pairs = [(a * CORES + c, b * CORES + c) for a, b in pairs for c in range(CORES)]
    return lax.ppermute(value, "dp", pairs)


def between_halves(value, steps):
    experts = lax.axis_size("expert")
    pairs = [
        ((a * CORES + c) * experts + e, (b * CORES + c) * experts + (e ^ Y_SIZE))
        for a, b in steps
        for c in range(CORES)
        for e in range(experts)
    ]
    return lax.ppermute(value, BOTH, pairs)


def total(terms):
    result = terms[0].astype(F32)
    for term in terms[1:]:
        result = result + term.astype(F32)
    return result.astype(BF16)


def line_sums(wide, down):
    last = LO_SIZE - 1
    half_way = between_halves(wide[2], [(0, last), (last, 0)])
    wide_one = shift(wide[1], 1)
    half_way, wide_one, down_send = lax.optimization_barrier((half_way, wide_one, down[1]))
    down_one = shift(down_send, 1)
    relayed = between_halves(half_way, [(last, 2), (0, 1)])
    direct = shift(wide[2], 2, leave=(0, last))
    wide_three = shift(wide[3], 3)
    wide_three, down_one = lax.optimization_barrier((wide_three, down_one))
    wide_sum = total([wide[0], wide_one, direct, wide_three, relayed])
    down_sum = total([down[0], down_one, shift(down[2], 2), shift(down[3], 3)])
    return wide_sum, down_sum


def on_device(tokens, out_grad, expert_ids, route_gates, swap_flags, gate_proj, up_proj, down_proj):
    devices = lax.axis_size("expert")
    my_expert = lax.axis_index("expert")
    lo = lax.axis_index("dp") // CORES
    core = lax.axis_index("dp") % CORES
    half = ((my_expert // Y_SIZE) % HI_SIZE).astype(jnp.int32)[None]
    place = (my_expert % Y_SIZE) * X_SIZE + my_expert // (HI_SIZE * Y_SIZE)
    place = place.astype(jnp.int32)[None]
    where = jnp.stack([core, lo]).astype(jnp.int32)
    width = tokens.shape[1]
    hidden_width = gate_proj.shape[2]
    weights = (gate_proj[0], up_proj[0], down_proj[0])

    far_tokens = across(tokens)
    far_out_grad = across(out_grad)
    own_sides, far_sides = route(half, expert_ids, route_gates)
    far_sides = across(far_sides)
    near_blocks, near_picked = fill(own_sides, tokens, out_grad, 10**9)
    near_rows = to_plane(near_blocks.reshape(PLANE, MOST, -1)).reshape(PLANE * MOST, -1)
    far_blocks, far_picked = fill(far_sides, far_tokens, far_out_grad, 10**12)
    far_blocks, near_blocks = lax.optimization_barrier((far_blocks, near_blocks))
    far_rows = to_plane(far_blocks.reshape(PLANE, MOST, -1)).reshape(PLANE * MOST, -1)

    near_back, near_hidden, near_pick, near_grads = run_expert(place, near_rows, weights)
    far_back, far_hidden, far_pick, far_grads = run_expert(place, far_rows, weights)

    rows, grads = (near_rows, far_rows), (near_grads, far_grads)
    give = wide_grads(where, rows, grads, width)
    taken = core_swap(give)
    far_back, give = lax.optimization_barrier((far_back, give))
    far_returned = to_plane(far_back)
    give_down, keep_down = down_grads(where, (near_hidden, far_hidden), (near_pick, far_pick))
    taken, keep_down = lax.optimization_barrier((taken, keep_down))
    gate_up_parts = wide_grads(where, rows, grads, width, taken)
    give_down, unused = lax.optimization_barrier((give_down, gate_up_parts[0]))
    taken_down = core_swap(give_down)
    down_parts = [total([keep_down[r], taken_down[r]]) for r in range(LO_SIZE)]
    gate_up_sum, down_sum = line_sums(gate_up_parts, down_parts)

    near_back, far_returned = lax.optimization_barrier((near_back, far_returned))
    near_returned = to_plane(near_back)
    far_total = across(collect(far_picked, far_returned))
    layer_out, grad_tokens, gate_grads = finish(
        half, expert_ids, near_picked, near_returned, far_total
    )

    is_moved = swap_flags[my_expert] == 1
    swap = [(i, i ^ (devices // 2)) for i in range(devices)]
    other_gate_up = lax.ppermute(gate_up_sum, "expert", swap)
    other_down = lax.ppermute(down_sum, "expert", swap)
    gate_up_sum = jnp.where(is_moved, other_gate_up, gate_up_sum)
    down_sum = jnp.where(is_moved, other_down, down_sum)
    grad_gate = gate_up_sum[:, :hidden_width]
    grad_up = gate_up_sum[:, hidden_width:]
    return (layer_out, grad_tokens, gate_grads, grad_gate[None], grad_up[None], down_sum[None])


def solution(mesh):
    return jax.shard_map(
        on_device,
        mesh=mesh,
        in_specs=(
            P(("dp", "expert"), None),
            P(("dp", "expert"), None),
            P(("dp", "expert"), None),
            P(("dp", "expert"), None),
            P(),
            P("expert", None, None),
            P("expert", None, None),
            P("expert", None, None),
        ),
        out_specs=(
            P(("dp", "expert"), None),
            P(("dp", "expert"), None),
            P(("dp", "expert"), None),
            P("expert", "dp", None),
            P("expert", "dp", None),
            P("expert", "dp", None),
        ),
        check_vma=False,
    )
```

```python
import functools

import jax
import jax.numpy as jnp
from jax import lax
from jax.experimental import pallas as pl
from jax.experimental.pallas import tpu as pltpu
from jax.sharding import PartitionSpec as P

MOST = 16
X_SIZE, HI_SIZE, Y_SIZE = 4, 2, 4
LO_SIZE, CORES = 4, 2
PLANE = 16
SIDE = 128
PARTS = 3

BOTH = ("dp", "expert")
PLANE_GROUPS = [
    [x * HI_SIZE * Y_SIZE + hi * Y_SIZE + y for y in range(Y_SIZE) for x in range(X_SIZE)]
    for hi in range(HI_SIZE)
]
CONTRACT_LAST = (((1,), (1,)), ((), ()))
CONTRACT_FIRST = (((0,), (0,)), ((), ()))
BF16, F32 = jnp.bfloat16, jnp.float32
WHOLE = pl.BlockSpec(memory_space=pltpu.VMEM)
SCALAR = pl.BlockSpec(memory_space=pltpu.SMEM)
ANYWHERE = pl.BlockSpec(memory_space=pl.ANY)


def block_of(shape):
    return pl.BlockSpec(shape, lambda i: (0,) * len(shape))


def limits():
    return pltpu.CompilerParams(vmem_limit_bytes=60 << 20)


def cost(flops, moved):
    return pl.CostEstimate(flops=flops, bytes_accessed=moved, transcendentals=0)


def across(value):
    experts = lax.axis_size("expert")
    pairs = []
    for dp in range(lax.axis_size("dp")):
        lo, core = divmod(dp, CORES)
        other_dp = (LO_SIZE - 1 - lo) * CORES + core
        for expert in range(experts):
            pairs.append((dp * experts + expert, other_dp * experts + (expert ^ Y_SIZE)))
    return lax.ppermute(value, BOTH, pairs)


def to_plane(blocks):
    return lax.all_to_all(
        blocks, "expert", split_axis=0, concat_axis=0, axis_index_groups=PLANE_GROUPS, tiled=True
    )


def lane_names(shape, half):
    place = lax.broadcasted_iota(jnp.int32, shape, 1) & (PLANE - 1)
    return (place & (X_SIZE - 1)) * (HI_SIZE * Y_SIZE) + half * Y_SIZE + (place >> 2)


def split_parts(values, shape):
    part = lax.broadcasted_iota(jnp.int32, shape, 1) >> 4
    high = values.astype(BF16).astype(F32)
    middle = (values - high).astype(BF16).astype(F32)
    low = values - high - middle
    chosen = jnp.where(part == 0, high, jnp.where(part == 1, middle, low))
    return jnp.where(part < PARTS, chosen, 0.0).astype(BF16)


def route_kernel(half_ref, ids_ref, gates_ref, own_ref, far_ref):
    half = half_ref[0]
    shape = own_ref.shape
    for which, ref in ((half, own_ref), (1 - half, far_ref)):
        names = lane_names(shape, which)
        total = jnp.zeros(shape, F32)
        for k in range(ids_ref.shape[1]):
            total += jnp.where(ids_ref[:, k : k + 1] == names, gates_ref[:, k : k + 1], 0.0)
        ref[...] = split_parts(total, shape)


def route(half, ids, gates):
    table = jax.ShapeDtypeStruct((ids.shape[0], SIDE), BF16)
    return pl.pallas_call(
        route_kernel,
        out_shape=(table, table),
        in_specs=[SCALAR, WHOLE, WHOLE],
        out_specs=(WHOLE, WHOLE),
        cost_estimate=cost(1000000, 200000),
        name="route",
    )(half, ids, gates)


def fill_kernel(sides_ref, tokens_ref, grads_ref, blocks_ref, picked_ref):
    rows = sides_ref.shape[0]
    width = tokens_ref.shape[1]
    turned = jnp.transpose(sides_ref[...].astype(F32))
    chosen = jnp.where(turned[:PLANE] > 0, 1.0, 0.0)
    before = jnp.where(
        lax.broadcasted_iota(jnp.int32, (rows, rows), 0)
        < lax.broadcasted_iota(jnp.int32, (rows, rows), 1),
        1.0,
        0.0,
    ).astype(BF16)
    rank = jnp.dot(chosen.astype(BF16), before, preferred_element_type=F32)
    rank = jnp.where(chosen > 0, rank, -1.0)
    slot = lax.broadcasted_iota(jnp.int32, (MOST, rows), 0).astype(F32)
    for j in range(PLANE):
        hit = jnp.where(rank[j : j + 1] == slot, 1.0, 0.0)
        picked_ref[j * MOST : (j + 1) * MOST, :] = hit.astype(BF16)
    picked = picked_ref[...]
    blocks_ref[:, width : width + SIDE] = jnp.dot(
        picked, sides_ref[...], preferred_element_type=F32
    ).astype(BF16)
    step = min(512, width)
    for n in range(0, width, step):
        blocks_ref[:, n : n + step] = jnp.dot(
            picked, tokens_ref[:, n : n + step], preferred_element_type=F32
        ).astype(BF16)
        blocks_ref[:, width + SIDE + n : width + SIDE + n + step] = jnp.dot(
            picked, grads_ref[:, n : n + step], preferred_element_type=F32
        ).astype(BF16)


def fill(sides, tokens, grads, weight):
    rows, width = tokens.shape
    slots = PLANE * MOST
    return pl.pallas_call(
        fill_kernel,
        out_shape=(
            jax.ShapeDtypeStruct((slots, 2 * width + SIDE), BF16),
            jax.ShapeDtypeStruct((slots, rows), BF16),
        ),
        grid=(1,),
        in_specs=[block_of(sides.shape), block_of(tokens.shape), block_of(grads.shape)],
        out_specs=(block_of((slots, 2 * width + SIDE)), block_of((slots, rows))),
        compiler_params=limits(),
        cost_estimate=cost(weight, 8 * slots * width),
        name="fill",
    )(sides, tokens, grads)


def expert_kernel(
    place_ref,
    rows_ref,
    gate_hbm,
    up_hbm,
    down_hbm,
    back_ref,
    hidden_ref,
    pick_ref,
    grads_ref,
    gate_w,
    up_w,
    down_w,
    sems,
):
    width, hidden_width = gate_w.shape
    step = min(256, hidden_width)
    chunks = []
    for j in range(hidden_width // step):
        span = pl.ds(j * step, step)
        pairs = (
            (gate_hbm.at[:, span], gate_w.at[:, span]),
            (up_hbm.at[:, span], up_w.at[:, span]),
            (down_hbm.at[span, :], down_w.at[span, :]),
        )
        chunks.append(
            [pltpu.make_async_copy(*pair, sems.at[j, i]) for i, pair in enumerate(pairs)]
        )
    for chunk in chunks:
        for copy in chunk:
            copy.start()
    place = place_ref[0]
    slots = rows_ref.shape[0]
    lane = lax.broadcasted_iota(jnp.int32, (slots, SIDE), 1)
    mine = jnp.where((lane & (PLANE - 1)) == place, 1.0, 0.0)
    side = rows_ref[:, width : width + SIDE].astype(F32)
    slot_gate = jnp.sum(side * mine, axis=1, keepdims=True)
    pick_ref[...] = (slot_gate * rows_ref[:, width + SIDE :].astype(F32)).astype(BF16)

    for j, chunk in enumerate(chunks):
        for copy in chunk:
            copy.wait()
        span = slice(j * step, (j + 1) * step)
        gate_pre = jnp.dot(rows_ref[:, :width], gate_w[:, span], preferred_element_type=F32)
        up_pre = jnp.dot(rows_ref[:, :width], up_w[:, span], preferred_element_type=F32)
        hidden_grad = lax.dot_general(
            pick_ref[...], down_w[span, :], CONTRACT_LAST, preferred_element_type=F32
        )
        sigmoid = jax.nn.sigmoid(gate_pre)
        silu = gate_pre * sigmoid
        hidden_ref[:, span] = (silu * up_pre).astype(BF16)
        gate_grad = hidden_grad * up_pre * sigmoid * (1.0 + gate_pre * (1.0 - sigmoid))
        grads_ref[:, span] = gate_grad.astype(BF16)
        second = slice(hidden_width + j * step, hidden_width + (j + 1) * step)
        grads_ref[:, second] = (hidden_grad * silu).astype(BF16)

    wide = min(256, width)
    lead = back_ref.shape[:2]

    def outward(n, dots):
        start = pl.multiple_of(n * wide, wide)
        out = jnp.dot(hidden_ref[...], down_w[:, pl.ds(start, wide)], preferred_element_type=F32)
        ahead = pl.ds(pl.multiple_of(width + SIDE + n * wide, SIDE), wide)
        dots += jnp.sum(rows_ref[:, ahead].astype(F32) * out, axis=1, keepdims=True)
        back_ref[:, :, pl.ds(start, wide)] = (slot_gate * out).astype(BF16).reshape(*lead, wide)
        row_grad = lax.dot_general(
            grads_ref[:, :hidden_width],
            gate_w[pl.ds(start, wide), :],
            CONTRACT_LAST,
            preferred_element_type=F32,
        )
        row_grad += lax.dot_general(
            grads_ref[:, hidden_width:],
            up_w[pl.ds(start, wide), :],
            CONTRACT_LAST,
            preferred_element_type=F32,
        )
        back_ref[:, :, ahead] = row_grad.astype(BF16).reshape(*lead, wide)
        return dots

    dots = lax.fori_loop(0, width // wide, outward, jnp.zeros((slots, 1), F32))
    table = split_parts(dots * mine, (slots, SIDE))
    back_ref[:, :, width : width + SIDE] = table.reshape(*lead, SIDE)


def run_expert(place, rows, weights):
    slots = rows.shape[0]
    width, hidden_width = weights[0].shape
    full = 2 * width + SIDE
    pieces = hidden_width // min(256, hidden_width)
    return pl.pallas_call(
        expert_kernel,
        out_shape=(
            jax.ShapeDtypeStruct((PLANE, MOST, full), BF16),
            jax.ShapeDtypeStruct((slots, hidden_width), BF16),
            jax.ShapeDtypeStruct((slots, width), BF16),
            jax.ShapeDtypeStruct((slots, 2 * hidden_width), BF16),
        ),
        grid=(1,),
        in_specs=[SCALAR, block_of(rows.shape)] + [ANYWHERE] * 3,
        out_specs=(
            block_of((PLANE, MOST, full)),
            block_of((slots, hidden_width)),
            block_of((slots, width)),
            block_of((slots, 2 * hidden_width)),
        ),
        scratch_shapes=[
            pltpu.VMEM((width, hidden_width), BF16),
            pltpu.VMEM((width, hidden_width), BF16),
            pltpu.VMEM((hidden_width, width), BF16),
            pltpu.SemaphoreType.DMA((pieces, 3)),
        ],
        compiler_params=limits(),
        cost_estimate=cost(12 * slots * width * hidden_width, 6 * width * hidden_width),
        name="expert",
    )(place, rows, *weights)


def shard_start(where_ref, core, r, shard):
    lo = (where_ref[1] + r) & (LO_SIZE - 1)
    return pl.multiple_of((lo * CORES + core) * shard, shard)


def wide_kernel(keep, shard, where_ref, near_x, far_x, near_grads, far_grads, *refs):
    turned, columns = refs[-2:]
    slots = near_x.shape[0]
    core = where_ref[0] if keep else 1 - where_ref[0]

    @pl.when(pl.program_id(0) == 0)
    def _():
        for r in range(LO_SIZE):
            span = pl.ds(shard_start(where_ref, core, r, shard), shard)
            here = slice(r * shard, (r + 1) * shard)
            turned[here, :slots] = jnp.transpose(near_x[:, span])
            turned[here, slots:] = jnp.transpose(far_x[:, span])

    columns[:slots] = near_grads[...]
    columns[slots:] = far_grads[...]
    total = jnp.dot(turned[...], columns[...], preferred_element_type=F32)
    for r in range(LO_SIZE):
        part = total[r * shard : (r + 1) * shard]
        if keep:
            part = (part + refs[0][r].astype(F32)).astype(BF16)
            refs[1 + r][...] = part
            if r & 1:
                @pl.when((where_ref[1] == 0) == (r != 1))
                def _():
                    refs[1 + LO_SIZE][...] = part
        else:
            refs[0][r] = part.astype(BF16)


def wide_grads(where, rows, grads, width, taken=None):
    shard = width // (LO_SIZE * CORES)
    slots, columns = grads[0].shape
    step = min(512, columns)
    block = pl.BlockSpec((LO_SIZE, shard, step), lambda n, s: (0, 0, n))
    tokens = pl.BlockSpec((slots, width), lambda n, s: (0, 0))
    part = pl.BlockSpec((slots, step), lambda n, s: (0, n))
    one = pl.BlockSpec((shard, step), lambda n, s: (0, n))
    keep = taken is not None
    if keep:
        out_shape = (jax.ShapeDtypeStruct((shard, columns), BF16),) * (LO_SIZE + 1)
    else:
        out_shape = jax.ShapeDtypeStruct((LO_SIZE, shard, columns), BF16)
    return pl.pallas_call(
        functools.partial(wide_kernel, keep, shard),
        grid_spec=pltpu.PrefetchScalarGridSpec(
            num_scalar_prefetch=1,
            grid=(columns // step,),
            in_specs=[tokens, tokens, part, part] + ([block] if keep else []),
            out_specs=(one,) * (LO_SIZE + 1) if keep else block,
            scratch_shapes=[
                pltpu.VMEM((LO_SIZE * shard, 2 * slots), BF16),
                pltpu.VMEM((2 * slots, step), BF16),
            ],
        ),
        out_shape=out_shape,
        compiler_params=limits(),
        cost_estimate=cost(2 * slots * width * columns, 2 * width * columns),
        name="wide",
    )(where, *rows, *grads, *([taken] if keep else []))


def down_kernel(
    where_ref, near_hidden, far_hidden, near_pick, far_pick, give_ref, keep_ref, turned, columns, acc
):
    core = where_ref[0]
    shard = give_ref.shape[1]
    slots = near_hidden.shape[0]

    @pl.when(pl.program_id(0) == 0)
    def _():
        turned[:, :slots] = jnp.transpose(near_hidden[...])
        turned[:, slots:] = jnp.transpose(far_hidden[...])

    columns[:slots] = near_pick[...]
    columns[slots:] = far_pick[...]
    acc[...] = jnp.dot(turned[...], columns[...], preferred_element_type=F32)
    for r in range(LO_SIZE):
        for which, ref in ((1 - core, give_ref), (core, keep_ref)):
            start = shard_start(where_ref, which, r, shard)
            ref[r] = acc[pl.ds(start, shard), :].astype(BF16)


def down_grads(where, hidden, pick):
    slots, hidden_width = hidden[0].shape
    width = pick[0].shape[1]
    shard = hidden_width // (LO_SIZE * CORES)
    step = min(512, width)
    same = pl.BlockSpec((slots, hidden_width), lambda n, s: (0, 0))
    part = pl.BlockSpec((slots, step), lambda n, s: (0, n))
    block = pl.BlockSpec((LO_SIZE, shard, step), lambda n, s: (0, 0, n))
    shape = jax.ShapeDtypeStruct((LO_SIZE, shard, width), BF16)
    return pl.pallas_call(
        down_kernel,
        grid_spec=pltpu.PrefetchScalarGridSpec(
            num_scalar_prefetch=1,
            grid=(width // step,),
            in_specs=[same, same, part, part],
            out_specs=(block, block),
            scratch_shapes=[
                pltpu.VMEM((hidden_width, 2 * slots), BF16),
                pltpu.VMEM((2 * slots, step), BF16),
                pltpu.VMEM((hidden_width, step), F32),
            ],
        ),
        out_shape=(shape, shape),
        compiler_params=limits(),
        cost_estimate=cost(4 * slots * width * hidden_width, 4 * width * hidden_width),
        name="down",
    )(where, *hidden, *pick)


def turned_picks(picked_ref):
    return jnp.transpose(picked_ref[...].astype(F32)).astype(BF16)


def gather_rows(turned, returned_ref, start, size):
    block = returned_ref[:, :, start : start + size].reshape(PLANE * MOST, size)
    return jnp.dot(turned, block, preferred_element_type=F32)


def spans(width):
    step = min(512, width)
    return [(n, step) for n in range(0, width, step)]


def collect_kernel(picked_ref, returned_ref, out_ref):
    turned = turned_picks(picked_ref)
    full = out_ref.shape[1]
    width = (full - SIDE) // 2
    for start, size in spans(width) + [(width, SIDE)] + [
        (width + SIDE + n, step) for n, step in spans(width)
    ]:
        out_ref[:, start : start + size] = gather_rows(turned, returned_ref, start, size).astype(
            BF16
        )


def collect(picked, returned):
    slots, rows = picked.shape
    full = returned.shape[2]
    return pl.pallas_call(
        collect_kernel,
        grid=(1,),
        in_specs=[block_of(picked.shape), block_of(returned.shape)],
        out_specs=block_of((rows, full)),
        out_shape=jax.ShapeDtypeStruct((rows, full), BF16),
        compiler_params=limits(),
        cost_estimate=cost(2 * slots * rows * full, 2 * slots * full),
        name="collect",
    )(picked, returned)


def finish_kernel(half_ref, ids_ref, picked_ref, returned_ref, far_ref, out_ref, token_ref, gate_ref):
    turned = turned_picks(picked_ref)
    rows, width = out_ref.shape
    for n, step in spans(width):
        near = gather_rows(turned, returned_ref, n, step)
        out_ref[:, n : n + step] = (near + far_ref[:, n : n + step].astype(F32)).astype(BF16)
        start = width + SIDE + n
        near = gather_rows(turned, returned_ref, start, step)
        far = far_ref[:, start : start + step].astype(F32)
        token_ref[:, n : n + step] = (near + far).astype(BF16)
    near_dots = gather_rows(turned, returned_ref, width, SIDE)
    far_dots = far_ref[:, width : width + SIDE].astype(F32)
    half = half_ref[0]
    near_names = lane_names((rows, SIDE), half)
    far_names = lane_names((rows, SIDE), 1 - half)
    for k in range(ids_ref.shape[1]):
        ids = ids_ref[:, k : k + 1]
        found = jnp.where(ids == near_names, near_dots, 0.0)
        found += jnp.where(ids == far_names, far_dots, 0.0)
        gate_ref[:, k : k + 1] = jnp.sum(found, axis=1, keepdims=True)


def finish(half, ids, picked, returned, far_total):
    slots, rows = picked.shape
    full = returned.shape[2]
    width = (full - SIDE) // 2
    wide = jax.ShapeDtypeStruct((rows, width), BF16)
    return pl.pallas_call(
        finish_kernel,
        grid=(1,),
        in_specs=[SCALAR]
        + [block_of(value.shape) for value in (ids, picked, returned, far_total)],
        out_specs=(block_of((rows, width)), block_of((rows, width)), block_of(ids.shape)),
        out_shape=(wide, wide, jax.ShapeDtypeStruct(ids.shape, F32)),
        compiler_params=limits(),
        cost_estimate=cost(2 * slots * rows * full, 2 * slots * full),
        name="finish",
    )(half, ids, picked, returned, far_total)


def core_swap(give):
    return lax.ppermute(give, "dp", [(i, i ^ 1) for i in range(LO_SIZE * CORES)])


def move(value, steps):
    pairs = [(a * CORES + c, b * CORES + c) for a, b in steps for c in range(CORES)]
    return lax.ppermute(value, "dp", pairs)


def to_next(value):
    return move(value, [(0, 1), (1, 2)]), move(value, [(3, 2), (2, 1)])


def to_owner(up, down):
    return move(up, [(0, 1), (1, 2), (2, 3)]), move(down, [(3, 2), (2, 1), (1, 0)])


def total(terms):
    result = terms[0].astype(F32)
    for term in terms[1:]:
        result = result + term.astype(F32)
    return result.astype(BF16)


def on_device(tokens, out_grad, expert_ids, route_gates, swap_flags, gate_proj, up_proj, down_proj):
    devices = lax.axis_size("expert")
    my_expert = lax.axis_index("expert")
    lo = lax.axis_index("dp") // CORES
    core = lax.axis_index("dp") % CORES
    half = ((my_expert // Y_SIZE) % HI_SIZE).astype(jnp.int32)[None]
    place = (my_expert % Y_SIZE) * X_SIZE + my_expert // (HI_SIZE * Y_SIZE)
    place = place.astype(jnp.int32)[None]
    where = jnp.stack([core, lo]).astype(jnp.int32)
    width = tokens.shape[1]
    hidden_width = gate_proj.shape[2]
    weights = (gate_proj[0], up_proj[0], down_proj[0])

    far_tokens = across(tokens)
    far_out_grad = across(out_grad)
    own_sides, far_sides = route(half, expert_ids, route_gates)
    far_sides = across(far_sides)
    near_blocks, near_picked = fill(own_sides, tokens, out_grad, 10**9)
    near_rows = to_plane(near_blocks.reshape(PLANE, MOST, -1)).reshape(PLANE * MOST, -1)
    far_blocks, far_picked = fill(far_sides, far_tokens, far_out_grad, 10**12)
    far_blocks, near_blocks = lax.optimization_barrier((far_blocks, near_blocks))
    far_rows = to_plane(far_blocks.reshape(PLANE, MOST, -1)).reshape(PLANE * MOST, -1)

    near_back, near_hidden, near_pick, near_grads = run_expert(place, near_rows, weights)
    far_back, far_hidden, far_pick, far_grads = run_expert(place, far_rows, weights)

    rows, grads = (near_rows, far_rows), (near_grads, far_grads)
    give = wide_grads(where, rows, grads, width)
    taken = core_swap(give)
    far_back, give = lax.optimization_barrier((far_back, give))
    far_returned = to_plane(far_back)
    give_down, keep_down = down_grads(where, (near_hidden, far_hidden), (near_pick, far_pick))
    taken, keep_down = lax.optimization_barrier((taken, keep_down))
    *wide, wide_first = wide_grads(where, rows, grads, width, taken)
    give_down, unused = lax.optimization_barrier((give_down, wide_first))

    arrived = move(wide_first, [(0, 1), (3, 2)])
    taken_down = core_swap(give_down)
    narrow = [total([keep_down[r], taken_down[r]]) for r in range(LO_SIZE)]
    narrow_arrived = move(jnp.where(lo == 0, narrow[3], narrow[1]), [(0, 1), (3, 2)])

    near_back, far_returned = lax.optimization_barrier((near_back, far_returned))
    near_returned = to_plane(near_back)
    collected = collect(far_picked, far_returned)
    far_total = across(collected)
    arrived, unused = lax.optimization_barrier((arrived, collected))

    up, down = to_next(total([wide[2], arrived]))
    narrow_up, narrow_down = to_next(total([narrow[2], narrow_arrived]))
    up, down, far_total = lax.optimization_barrier((up, down, far_total))
    up, down = total([wide[1], up]), total([wide[3], down])
    sent = lax.optimization_barrier((up, down))
    narrow_up, narrow_down, unused = lax.optimization_barrier((narrow_up, narrow_down, sent))
    narrow_up, narrow_down = total([narrow[1], narrow_up]), total([narrow[3], narrow_down])
    up, down = to_owner(*sent)
    narrow_up, narrow_down = to_owner(narrow_up, narrow_down)
    gate_up_sum = total([wide[0], up, down])
    down_sum = total([narrow[0], narrow_up, narrow_down])

    layer_out, grad_tokens, gate_grads = finish(
        half, expert_ids, near_picked, near_returned, far_total
    )

    is_moved = swap_flags[my_expert] == 1
    swap = [(i, i ^ (devices // 2)) for i in range(devices)]
    other_gate_up = lax.ppermute(gate_up_sum, "expert", swap)
    other_down = lax.ppermute(down_sum, "expert", swap)
    gate_up_sum = jnp.where(is_moved, other_gate_up, gate_up_sum)
    down_sum = jnp.where(is_moved, other_down, down_sum)
    grad_gate = gate_up_sum[:, :hidden_width]
    grad_up = gate_up_sum[:, hidden_width:]
    return (layer_out, grad_tokens, gate_grads, grad_gate[None], grad_up[None], down_sum[None])


def solution(mesh):
    return jax.shard_map(
        on_device,
        mesh=mesh,
        in_specs=(
            P(("dp", "expert"), None),
            P(("dp", "expert"), None),
            P(("dp", "expert"), None),
            P(("dp", "expert"), None),
            P(),
            P("expert", None, None),
            P("expert", None, None),
            P("expert", None, None),
        ),
        out_specs=(
            P(("dp", "expert"), None),
            P(("dp", "expert"), None),
            P(("dp", "expert"), None),
            P("expert", "dp", None),
            P("expert", "dp", None),
            P("expert", "dp", None),
        ),
        check_vma=False,
    )
```

```python
import functools

import jax
import jax.numpy as jnp
from jax import lax
from jax.experimental import pallas as pl
from jax.experimental.pallas import tpu as pltpu
from jax.sharding import PartitionSpec as P

MOST = 16
X_SIZE, HI_SIZE, Y_SIZE = 4, 2, 4
LO_SIZE, CORES = 4, 2
PLANE = 16
SIDE = 128
PARTS = 3

BOTH = ("dp", "expert")
PLANE_GROUPS = [
    [x * HI_SIZE * Y_SIZE + hi * Y_SIZE + y for y in range(Y_SIZE) for x in range(X_SIZE)]
    for hi in range(HI_SIZE)
]
CONTRACT_LAST = (((1,), (1,)), ((), ()))
CONTRACT_FIRST = (((0,), (0,)), ((), ()))
BF16, F32 = jnp.bfloat16, jnp.float32
WHOLE = pl.BlockSpec(memory_space=pltpu.VMEM)
SCALAR = pl.BlockSpec(memory_space=pltpu.SMEM)
ANYWHERE = pl.BlockSpec(memory_space=pl.ANY)


def block_of(shape):
    return pl.BlockSpec(shape, lambda i: (0,) * len(shape))


def limits():
    return pltpu.CompilerParams(vmem_limit_bytes=62 << 20)


def cost(flops, moved):
    return pl.CostEstimate(flops=flops, bytes_accessed=moved, transcendentals=0)


def across(value):
    experts = lax.axis_size("expert")
    pairs = []
    for dp in range(lax.axis_size("dp")):
        lo, core = divmod(dp, CORES)
        other_dp = (lo ^ 1) * CORES + core
        for expert in range(experts):
            pairs.append((dp * experts + expert, other_dp * experts + (expert ^ Y_SIZE)))
    return lax.ppermute(value, BOTH, pairs)


def to_plane(blocks):
    return lax.all_to_all(
        blocks, "expert", split_axis=0, concat_axis=0, axis_index_groups=PLANE_GROUPS, tiled=True
    )


def lane_names(shape, half):
    place = lax.broadcasted_iota(jnp.int32, shape, 1) & (PLANE - 1)
    return (place & (X_SIZE - 1)) * (HI_SIZE * Y_SIZE) + half * Y_SIZE + (place >> 2)


def split_parts(values, shape):
    part = lax.broadcasted_iota(jnp.int32, shape, 1) >> 4
    high = values.astype(BF16).astype(F32)
    middle = (values - high).astype(BF16).astype(F32)
    low = values - high - middle
    chosen = jnp.where(part == 0, high, jnp.where(part == 1, middle, low))
    return jnp.where(part < PARTS, chosen, 0.0).astype(BF16)


def route_kernel(half_ref, ids_ref, gates_ref, own_ref, far_ref):
    half = half_ref[0]
    shape = own_ref.shape
    for which, ref in ((half, own_ref), (1 - half, far_ref)):
        names = lane_names(shape, which)
        total = jnp.zeros(shape, F32)
        for k in range(ids_ref.shape[1]):
            total += jnp.where(ids_ref[:, k : k + 1] == names, gates_ref[:, k : k + 1], 0.0)
        ref[...] = split_parts(total, shape)


def route(half, ids, gates):
    table = jax.ShapeDtypeStruct((ids.shape[0], SIDE), BF16)
    return pl.pallas_call(
        route_kernel,
        out_shape=(table, table),
        in_specs=[SCALAR, WHOLE, WHOLE],
        out_specs=(WHOLE, WHOLE),
        cost_estimate=cost(1000000, 200000),
        name="route",
    )(half, ids, gates)


def fill_kernel(sides_ref, tokens_ref, grads_ref, blocks_ref, picked_ref):
    rows = sides_ref.shape[0]
    width = tokens_ref.shape[1]
    turned = jnp.transpose(sides_ref[...].astype(F32))
    chosen = jnp.where(turned[:PLANE] > 0, 1.0, 0.0)
    before = jnp.where(
        lax.broadcasted_iota(jnp.int32, (rows, rows), 0)
        < lax.broadcasted_iota(jnp.int32, (rows, rows), 1),
        1.0,
        0.0,
    ).astype(BF16)
    rank = jnp.dot(chosen.astype(BF16), before, preferred_element_type=F32)
    rank = jnp.where(chosen > 0, rank, -1.0)
    slot = lax.broadcasted_iota(jnp.int32, (MOST, rows), 0).astype(F32)
    for j in range(PLANE):
        hit = jnp.where(rank[j : j + 1] == slot, 1.0, 0.0)
        picked_ref[j * MOST : (j + 1) * MOST, :] = hit.astype(BF16)
    picked = picked_ref[...]
    blocks_ref[:, width : width + SIDE] = jnp.dot(
        picked, sides_ref[...], preferred_element_type=F32
    ).astype(BF16)
    step = min(512, width)
    for n in range(0, width, step):
        blocks_ref[:, n : n + step] = jnp.dot(
            picked, tokens_ref[:, n : n + step], preferred_element_type=F32
        ).astype(BF16)
        blocks_ref[:, width + SIDE + n : width + SIDE + n + step] = jnp.dot(
            picked, grads_ref[:, n : n + step], preferred_element_type=F32
        ).astype(BF16)


def fill(sides, tokens, grads, weight):
    rows, width = tokens.shape
    slots = PLANE * MOST
    return pl.pallas_call(
        fill_kernel,
        out_shape=(
            jax.ShapeDtypeStruct((slots, 2 * width + SIDE), BF16),
            jax.ShapeDtypeStruct((slots, rows), BF16),
        ),
        grid=(1,),
        in_specs=[block_of(sides.shape), block_of(tokens.shape), block_of(grads.shape)],
        out_specs=(block_of((slots, 2 * width + SIDE)), block_of((slots, rows))),
        compiler_params=limits(),
        cost_estimate=cost(weight, 8 * slots * width),
        name="fill",
    )(sides, tokens, grads)


def expert_kernel(
    place_ref,
    rows_ref,
    gate_hbm,
    up_hbm,
    down_hbm,
    back_ref,
    hidden_ref,
    pick_ref,
    grads_ref,
    gate_w,
    up_w,
    down_w,
    sems,
):
    width, hidden_width = gate_w.shape
    step = min(256, hidden_width)
    chunks = []
    for j in range(hidden_width // step):
        span = pl.ds(j * step, step)
        pairs = (
            (gate_hbm.at[:, span], gate_w.at[:, span]),
            (up_hbm.at[:, span], up_w.at[:, span]),
            (down_hbm.at[span, :], down_w.at[span, :]),
        )
        chunks.append(
            [pltpu.make_async_copy(*pair, sems.at[j, i]) for i, pair in enumerate(pairs)]
        )
    for chunk in chunks:
        for copy in chunk:
            copy.start()
    place = place_ref[0]
    slots = rows_ref.shape[0]
    lane = lax.broadcasted_iota(jnp.int32, (slots, SIDE), 1)
    mine = jnp.where((lane & (PLANE - 1)) == place, 1.0, 0.0)
    side = rows_ref[:, width : width + SIDE].astype(F32)
    slot_gate = jnp.sum(side * mine, axis=1, keepdims=True)
    pick_ref[...] = (slot_gate * rows_ref[:, width + SIDE :].astype(F32)).astype(BF16)

    for j, chunk in enumerate(chunks):
        for copy in chunk:
            copy.wait()
        span = slice(j * step, (j + 1) * step)
        gate_pre = jnp.dot(rows_ref[:, :width], gate_w[:, span], preferred_element_type=F32)
        up_pre = jnp.dot(rows_ref[:, :width], up_w[:, span], preferred_element_type=F32)
        hidden_grad = lax.dot_general(
            pick_ref[...], down_w[span, :], CONTRACT_LAST, preferred_element_type=F32
        )
        sigmoid = jax.nn.sigmoid(gate_pre)
        silu = gate_pre * sigmoid
        hidden_ref[:, span] = (silu * up_pre).astype(BF16)
        gate_grad = hidden_grad * up_pre * sigmoid * (1.0 + gate_pre * (1.0 - sigmoid))
        grads_ref[:, span] = gate_grad.astype(BF16)
        second = slice(hidden_width + j * step, hidden_width + (j + 1) * step)
        grads_ref[:, second] = (hidden_grad * silu).astype(BF16)

    wide = min(256, width)
    lead = back_ref.shape[:2]

    def outward(n, dots):
        start = pl.multiple_of(n * wide, wide)
        out = jnp.dot(hidden_ref[...], down_w[:, pl.ds(start, wide)], preferred_element_type=F32)
        ahead = pl.ds(pl.multiple_of(width + SIDE + n * wide, SIDE), wide)
        dots += jnp.sum(rows_ref[:, ahead].astype(F32) * out, axis=1, keepdims=True)
        back_ref[:, :, pl.ds(start, wide)] = (slot_gate * out).astype(BF16).reshape(*lead, wide)
        row_grad = lax.dot_general(
            grads_ref[:, :hidden_width],
            gate_w[pl.ds(start, wide), :],
            CONTRACT_LAST,
            preferred_element_type=F32,
        )
        row_grad += lax.dot_general(
            grads_ref[:, hidden_width:],
            up_w[pl.ds(start, wide), :],
            CONTRACT_LAST,
            preferred_element_type=F32,
        )
        back_ref[:, :, ahead] = row_grad.astype(BF16).reshape(*lead, wide)
        return dots

    dots = lax.fori_loop(0, width // wide, outward, jnp.zeros((slots, 1), F32))
    table = split_parts(dots * mine, (slots, SIDE))
    back_ref[:, :, width : width + SIDE] = table.reshape(*lead, SIDE)


def run_expert(place, rows, weights):
    slots = rows.shape[0]
    width, hidden_width = weights[0].shape
    full = 2 * width + SIDE
    pieces = hidden_width // min(256, hidden_width)
    return pl.pallas_call(
        expert_kernel,
        out_shape=(
            jax.ShapeDtypeStruct((PLANE, MOST, full), BF16),
            jax.ShapeDtypeStruct((slots, hidden_width), BF16),
            jax.ShapeDtypeStruct((slots, width), BF16),
            jax.ShapeDtypeStruct((slots, 2 * hidden_width), BF16),
        ),
        grid=(1,),
        in_specs=[SCALAR, block_of(rows.shape)] + [ANYWHERE] * 3,
        out_specs=(
            block_of((PLANE, MOST, full)),
            block_of((slots, hidden_width)),
            block_of((slots, width)),
            block_of((slots, 2 * hidden_width)),
        ),
        scratch_shapes=[
            pltpu.VMEM((width, hidden_width), BF16),
            pltpu.VMEM((width, hidden_width), BF16),
            pltpu.VMEM((hidden_width, width), BF16),
            pltpu.SemaphoreType.DMA((pieces, 3)),
        ],
        compiler_params=limits(),
        cost_estimate=cost(12 * slots * width * hidden_width, 6 * width * hidden_width),
        name="expert",
    )(place, rows, *weights)


def shard_start(where_ref, core, r, shard):
    lo = (where_ref[1] + r) & (LO_SIZE - 1)
    return pl.multiple_of((lo * CORES + core) * shard, shard)


def wide_kernel(keep, shard, where_ref, near_x, far_x, near_grads, far_grads, *refs):
    turned, columns = refs[-2:]
    slots = near_x.shape[0]
    core = where_ref[0] if keep else 1 - where_ref[0]

    @pl.when(pl.program_id(0) == 0)
    def _():
        for r in range(LO_SIZE):
            span = pl.ds(shard_start(where_ref, core, r, shard), shard)
            here = slice(r * shard, (r + 1) * shard)
            turned[here, :slots] = jnp.transpose(near_x[:, span])
            turned[here, slots:] = jnp.transpose(far_x[:, span])

    columns[:slots] = near_grads[...]
    columns[slots:] = far_grads[...]
    total = jnp.dot(turned[...], columns[...], preferred_element_type=F32)
    for r in range(LO_SIZE):
        part = total[r * shard : (r + 1) * shard]
        if keep:
            part = (part + refs[0][r].astype(F32)).astype(BF16)
            refs[1 + r][...] = part
            if r & 1:
                @pl.when((where_ref[1] == 0) == (r != 1))
                def _():
                    refs[1 + LO_SIZE][...] = part
        else:
            refs[0][r] = part.astype(BF16)


def wide_grads(where, rows, grads, width, taken=None):
    shard = width // (LO_SIZE * CORES)
    slots, columns = grads[0].shape
    step = min(512, columns)
    block = pl.BlockSpec((LO_SIZE, shard, step), lambda n, s: (0, 0, n))
    tokens = pl.BlockSpec((slots, width), lambda n, s: (0, 0))
    part = pl.BlockSpec((slots, step), lambda n, s: (0, n))
    one = pl.BlockSpec((shard, step), lambda n, s: (0, n))
    keep = taken is not None
    if keep:
        out_shape = (jax.ShapeDtypeStruct((shard, columns), BF16),) * (LO_SIZE + 1)
    else:
        out_shape = jax.ShapeDtypeStruct((LO_SIZE, shard, columns), BF16)
    return pl.pallas_call(
        functools.partial(wide_kernel, keep, shard),
        grid_spec=pltpu.PrefetchScalarGridSpec(
            num_scalar_prefetch=1,
            grid=(columns // step,),
            in_specs=[tokens, tokens, part, part] + ([block] if keep else []),
            out_specs=(one,) * (LO_SIZE + 1) if keep else block,
            scratch_shapes=[
                pltpu.VMEM((LO_SIZE * shard, 2 * slots), BF16),
                pltpu.VMEM((2 * slots, step), BF16),
            ],
        ),
        out_shape=out_shape,
        compiler_params=limits(),
        cost_estimate=cost(2 * slots * width * columns, 2 * width * columns),
        name="wide",
    )(where, *rows, *grads, *([taken] if keep else []))


def down_kernel(
    where_ref, near_hidden, far_hidden, near_pick, far_pick, give_ref, keep_ref, turned, columns, acc
):
    core = where_ref[0]
    shard = give_ref.shape[1]
    slots = near_hidden.shape[0]

    @pl.when(pl.program_id(0) == 0)
    def _():
        turned[:, :slots] = jnp.transpose(near_hidden[...])
        turned[:, slots:] = jnp.transpose(far_hidden[...])

    columns[:slots] = near_pick[...]
    columns[slots:] = far_pick[...]
    acc[...] = jnp.dot(turned[...], columns[...], preferred_element_type=F32)
    for r in range(LO_SIZE):
        for which, ref in ((1 - core, give_ref), (core, keep_ref)):
            start = shard_start(where_ref, which, r, shard)
            ref[r] = acc[pl.ds(start, shard), :].astype(BF16)


def down_grads(where, hidden, pick):
    slots, hidden_width = hidden[0].shape
    width = pick[0].shape[1]
    shard = hidden_width // (LO_SIZE * CORES)
    step = min(512, width)
    same = pl.BlockSpec((slots, hidden_width), lambda n, s: (0, 0))
    part = pl.BlockSpec((slots, step), lambda n, s: (0, n))
    block = pl.BlockSpec((LO_SIZE, shard, step), lambda n, s: (0, 0, n))
    shape = jax.ShapeDtypeStruct((LO_SIZE, shard, width), BF16)
    return pl.pallas_call(
        down_kernel,
        grid_spec=pltpu.PrefetchScalarGridSpec(
            num_scalar_prefetch=1,
            grid=(width // step,),
            in_specs=[same, same, part, part],
            out_specs=(block, block),
            scratch_shapes=[
                pltpu.VMEM((hidden_width, 2 * slots), BF16),
                pltpu.VMEM((2 * slots, step), BF16),
                pltpu.VMEM((hidden_width, step), F32),
            ],
        ),
        out_shape=(shape, shape),
        compiler_params=limits(),
        cost_estimate=cost(4 * slots * width * hidden_width, 4 * width * hidden_width),
        name="down",
    )(where, *hidden, *pick)


def turned_picks(picked_ref):
    return jnp.transpose(picked_ref[...].astype(F32)).astype(BF16)


def gather_rows(turned, returned_ref, start, size):
    block = returned_ref[:, :, start : start + size].reshape(PLANE * MOST, size)
    return jnp.dot(turned, block, preferred_element_type=F32)


def spans(width):
    step = min(512, width)
    return [(n, step) for n in range(0, width, step)]


def collect_kernel(picked_ref, returned_ref, out_ref):
    turned = turned_picks(picked_ref)
    full = out_ref.shape[1]
    width = (full - SIDE) // 2
    for start, size in spans(width) + [(width, SIDE)] + [
        (width + SIDE + n, step) for n, step in spans(width)
    ]:
        out_ref[:, start : start + size] = gather_rows(turned, returned_ref, start, size).astype(
            BF16
        )


def collect(picked, returned):
    slots, rows = picked.shape
    full = returned.shape[2]
    return pl.pallas_call(
        collect_kernel,
        grid=(1,),
        in_specs=[block_of(picked.shape), block_of(returned.shape)],
        out_specs=block_of((rows, full)),
        out_shape=jax.ShapeDtypeStruct((rows, full), BF16),
        compiler_params=limits(),
        cost_estimate=cost(2 * slots * rows * full, 2 * slots * full),
        name="collect",
    )(picked, returned)


def finish_kernel(half_ref, ids_ref, picked_ref, returned_ref, far_ref, out_ref, token_ref, gate_ref):
    turned = turned_picks(picked_ref)
    rows, width = out_ref.shape
    for n, step in spans(width):
        near = gather_rows(turned, returned_ref, n, step)
        out_ref[:, n : n + step] = (near + far_ref[:, n : n + step].astype(F32)).astype(BF16)
        start = width + SIDE + n
        near = gather_rows(turned, returned_ref, start, step)
        far = far_ref[:, start : start + step].astype(F32)
        token_ref[:, n : n + step] = (near + far).astype(BF16)
    near_dots = gather_rows(turned, returned_ref, width, SIDE)
    far_dots = far_ref[:, width : width + SIDE].astype(F32)
    half = half_ref[0]
    near_names = lane_names((rows, SIDE), half)
    far_names = lane_names((rows, SIDE), 1 - half)
    for k in range(ids_ref.shape[1]):
        ids = ids_ref[:, k : k + 1]
        found = jnp.where(ids == near_names, near_dots, 0.0)
        found += jnp.where(ids == far_names, far_dots, 0.0)
        gate_ref[:, k : k + 1] = jnp.sum(found, axis=1, keepdims=True)


def finish(half, ids, picked, returned, far_total):
    slots, rows = picked.shape
    full = returned.shape[2]
    width = (full - SIDE) // 2
    wide = jax.ShapeDtypeStruct((rows, width), BF16)
    return pl.pallas_call(
        finish_kernel,
        grid=(1,),
        in_specs=[SCALAR]
        + [block_of(value.shape) for value in (ids, picked, returned, far_total)],
        out_specs=(block_of((rows, width)), block_of((rows, width)), block_of(ids.shape)),
        out_shape=(wide, wide, jax.ShapeDtypeStruct(ids.shape, F32)),
        compiler_params=limits(),
        cost_estimate=cost(2 * slots * rows * full, 2 * slots * full),
        name="finish",
    )(half, ids, picked, returned, far_total)


def core_swap(give):
    return lax.ppermute(give, "dp", [(i, i ^ 1) for i in range(LO_SIZE * CORES)])


def move(value, steps):
    pairs = [(a * CORES + c, b * CORES + c) for a, b in steps for c in range(CORES)]
    return lax.ppermute(value, "dp", pairs)


def to_next(value):
    return move(value, [(0, 1), (1, 2)]), move(value, [(3, 2), (2, 1)])


def to_owner(up, down):
    return move(up, [(0, 1), (1, 2), (2, 3)]), move(down, [(3, 2), (2, 1), (1, 0)])


def total(terms):
    result = terms[0].astype(F32)
    for term in terms[1:]:
        result = result + term.astype(F32)
    return result.astype(BF16)


def on_device(tokens, out_grad, expert_ids, route_gates, swap_flags, gate_proj, up_proj, down_proj):
    devices = lax.axis_size("expert")
    my_expert = lax.axis_index("expert")
    lo = lax.axis_index("dp") // CORES
    core = lax.axis_index("dp") % CORES
    half = ((my_expert // Y_SIZE) % HI_SIZE).astype(jnp.int32)[None]
    place = (my_expert % Y_SIZE) * X_SIZE + my_expert // (HI_SIZE * Y_SIZE)
    place = place.astype(jnp.int32)[None]
    where = jnp.stack([core, lo]).astype(jnp.int32)
    width = tokens.shape[1]
    hidden_width = gate_proj.shape[2]
    weights = (gate_proj[0], up_proj[0], down_proj[0])

    far_tokens = across(tokens)
    far_out_grad = across(out_grad)
    own_sides, far_sides = route(half, expert_ids, route_gates)
    far_sides = across(far_sides)
    near_blocks, near_picked = fill(own_sides, tokens, out_grad, 10**9)
    near_rows = to_plane(near_blocks.reshape(PLANE, MOST, -1)).reshape(PLANE * MOST, -1)
    far_blocks, far_picked = fill(far_sides, far_tokens, far_out_grad, 10**12)
    far_blocks, near_blocks = lax.optimization_barrier((far_blocks, near_blocks))
    far_rows = to_plane(far_blocks.reshape(PLANE, MOST, -1)).reshape(PLANE * MOST, -1)

    near_back, near_hidden, near_pick, near_grads = run_expert(place, near_rows, weights)
    far_back, far_hidden, far_pick, far_grads = run_expert(place, far_rows, weights)

    rows, grads = (near_rows, far_rows), (near_grads, far_grads)
    give = wide_grads(where, rows, grads, width)
    taken = core_swap(give)
    far_back, give = lax.optimization_barrier((far_back, give))
    far_returned = to_plane(far_back)
    give_down, keep_down = down_grads(where, (near_hidden, far_hidden), (near_pick, far_pick))
    taken, keep_down = lax.optimization_barrier((taken, keep_down))
    *wide, wide_first = wide_grads(where, rows, grads, width, taken)
    give_down, unused = lax.optimization_barrier((give_down, wide_first))

    arrived = move(wide_first, [(0, 1), (3, 2)])
    taken_down = core_swap(give_down)
    narrow = [total([keep_down[r], taken_down[r]]) for r in range(LO_SIZE)]
    narrow_arrived = move(jnp.where(lo == 0, narrow[3], narrow[1]), [(0, 1), (3, 2)])

    near_back, far_returned = lax.optimization_barrier((near_back, far_returned))
    near_returned = to_plane(near_back)
    collected = collect(far_picked, far_returned)
    far_total = across(collected)
    arrived, unused = lax.optimization_barrier((arrived, collected))

    up, down = to_next(total([wide[2], arrived]))
    up, down, far_total, narrow_arrived = lax.optimization_barrier(
        (up, down, far_total, narrow_arrived)
    )
    sent = lax.optimization_barrier((total([wide[1], up]), total([wide[3], down])))
    up, down = to_owner(*sent)
    narrow_arrived, unused = lax.optimization_barrier((narrow_arrived, sent))
    narrow_up, narrow_down = to_next(total([narrow[2], narrow_arrived]))
    narrow_up, narrow_down, up, down = lax.optimization_barrier((narrow_up, narrow_down, up, down))
    narrow_up, narrow_down = to_owner(
        total([narrow[1], narrow_up]), total([narrow[3], narrow_down])
    )
    gate_up_sum = total([wide[0], up, down])
    down_sum = total([narrow[0], narrow_up, narrow_down])

    layer_out, grad_tokens, gate_grads = finish(
        half, expert_ids, near_picked, near_returned, far_total
    )

    is_moved = swap_flags[my_expert] == 1
    swap = [(i, i ^ (devices // 2)) for i in range(devices)]
    other_gate_up = lax.ppermute(gate_up_sum, "expert", swap)
    other_down = lax.ppermute(down_sum, "expert", swap)
    gate_up_sum = jnp.where(is_moved, other_gate_up, gate_up_sum)
    down_sum = jnp.where(is_moved, other_down, down_sum)
    grad_gate = gate_up_sum[:, :hidden_width]
    grad_up = gate_up_sum[:, hidden_width:]
    return (layer_out, grad_tokens, gate_grads, grad_gate[None], grad_up[None], down_sum[None])


def solution(mesh):
    return jax.shard_map(
        on_device,
        mesh=mesh,
        in_specs=(
            P(("dp", "expert"), None),
            P(("dp", "expert"), None),
            P(("dp", "expert"), None),
            P(("dp", "expert"), None),
            P(),
            P("expert", None, None),
            P("expert", None, None),
            P("expert", None, None),
        ),
        out_specs=(
            P(("dp", "expert"), None),
            P(("dp", "expert"), None),
            P(("dp", "expert"), None),
            P("expert", "dp", None),
            P("expert", "dp", None),
            P("expert", "dp", None),
        ),
        check_vma=False,
    )
```

```python
import functools

import jax
import jax.numpy as jnp
from jax import lax
from jax.experimental import pallas as pl
from jax.experimental.pallas import tpu as pltpu
from jax.sharding import PartitionSpec as P

MOST = 16
X_SIZE, HI_SIZE, Y_SIZE = 4, 2, 4
LO_SIZE, CORES = 4, 2
PLANE = 16
SIDE = 128
PARTS = 3

BOTH = ("dp", "expert")
PLANE_GROUPS = [
    [x * HI_SIZE * Y_SIZE + hi * Y_SIZE + y for y in range(Y_SIZE) for x in range(X_SIZE)]
    for hi in range(HI_SIZE)
]
CONTRACT_LAST = (((1,), (1,)), ((), ()))
CONTRACT_FIRST = (((0,), (0,)), ((), ()))
BF16, F32 = jnp.bfloat16, jnp.float32
WHOLE = pl.BlockSpec(memory_space=pltpu.VMEM)
SCALAR = pl.BlockSpec(memory_space=pltpu.SMEM)
ANYWHERE = pl.BlockSpec(memory_space=pl.ANY)


def block_of(shape):
    return pl.BlockSpec(shape, lambda i: (0,) * len(shape))


def limits():
    return pltpu.CompilerParams(vmem_limit_bytes=62 << 20)


def cost(flops, moved):
    return pl.CostEstimate(flops=flops, bytes_accessed=moved, transcendentals=0)


def across(value):
    experts = lax.axis_size("expert")
    pairs = []
    for dp in range(lax.axis_size("dp")):
        lo, core = divmod(dp, CORES)
        other_dp = (LO_SIZE - 1 - lo) * CORES + core
        for expert in range(experts):
            pairs.append((dp * experts + expert, other_dp * experts + (expert ^ Y_SIZE)))
    return lax.ppermute(value, BOTH, pairs)


def to_plane(blocks):
    return lax.all_to_all(
        blocks, "expert", split_axis=0, concat_axis=0, axis_index_groups=PLANE_GROUPS, tiled=True
    )


def lane_names(shape, half):
    place = lax.broadcasted_iota(jnp.int32, shape, 1) & (PLANE - 1)
    return (place & (X_SIZE - 1)) * (HI_SIZE * Y_SIZE) + half * Y_SIZE + (place >> 2)


def split_parts(values, shape):
    part = lax.broadcasted_iota(jnp.int32, shape, 1) >> 4
    high = values.astype(BF16).astype(F32)
    middle = (values - high).astype(BF16).astype(F32)
    low = values - high - middle
    chosen = jnp.where(part == 0, high, jnp.where(part == 1, middle, low))
    return jnp.where(part < PARTS, chosen, 0.0).astype(BF16)


def route_kernel(half_ref, ids_ref, gates_ref, own_ref, far_ref):
    half = half_ref[0]
    shape = own_ref.shape
    for which, ref in ((half, own_ref), (1 - half, far_ref)):
        names = lane_names(shape, which)
        total = jnp.zeros(shape, F32)
        for k in range(ids_ref.shape[1]):
            total += jnp.where(ids_ref[:, k : k + 1] == names, gates_ref[:, k : k + 1], 0.0)
        ref[...] = split_parts(total, shape)


def route(half, ids, gates):
    table = jax.ShapeDtypeStruct((ids.shape[0], SIDE), BF16)
    return pl.pallas_call(
        route_kernel,
        out_shape=(table, table),
        in_specs=[SCALAR, WHOLE, WHOLE],
        out_specs=(WHOLE, WHOLE),
        cost_estimate=cost(1000000, 200000),
        name="route",
    )(half, ids, gates)


def fill_kernel(sides_ref, tokens_ref, grads_ref, blocks_ref, picked_ref):
    rows = sides_ref.shape[0]
    width = tokens_ref.shape[1]
    turned = jnp.transpose(sides_ref[...].astype(F32))
    chosen = jnp.where(turned[:PLANE] > 0, 1.0, 0.0)
    before = jnp.where(
        lax.broadcasted_iota(jnp.int32, (rows, rows), 0)
        < lax.broadcasted_iota(jnp.int32, (rows, rows), 1),
        1.0,
        0.0,
    ).astype(BF16)
    rank = jnp.dot(chosen.astype(BF16), before, preferred_element_type=F32)
    rank = jnp.where(chosen > 0, rank, -1.0)
    slot = lax.broadcasted_iota(jnp.int32, (MOST, rows), 0).astype(F32)
    for j in range(PLANE):
        hit = jnp.where(rank[j : j + 1] == slot, 1.0, 0.0)
        picked_ref[j * MOST : (j + 1) * MOST, :] = hit.astype(BF16)
    picked = picked_ref[...]
    blocks_ref[:, width : width + SIDE] = jnp.dot(
        picked, sides_ref[...], preferred_element_type=F32
    ).astype(BF16)
    step = min(512, width)
    for n in range(0, width, step):
        blocks_ref[:, n : n + step] = jnp.dot(
            picked, tokens_ref[:, n : n + step], preferred_element_type=F32
        ).astype(BF16)
        blocks_ref[:, width + SIDE + n : width + SIDE + n + step] = jnp.dot(
            picked, grads_ref[:, n : n + step], preferred_element_type=F32
        ).astype(BF16)


def fill(sides, tokens, grads, weight):
    rows, width = tokens.shape
    slots = PLANE * MOST
    return pl.pallas_call(
        fill_kernel,
        out_shape=(
            jax.ShapeDtypeStruct((slots, 2 * width + SIDE), BF16),
            jax.ShapeDtypeStruct((slots, rows), BF16),
        ),
        grid=(1,),
        in_specs=[block_of(sides.shape), block_of(tokens.shape), block_of(grads.shape)],
        out_specs=(block_of((slots, 2 * width + SIDE)), block_of((slots, rows))),
        compiler_params=limits(),
        cost_estimate=cost(weight, 8 * slots * width),
        name="fill",
    )(sides, tokens, grads)


def expert_kernel(
    place_ref,
    rows_ref,
    gate_hbm,
    up_hbm,
    down_hbm,
    back_ref,
    hidden_ref,
    pick_ref,
    grads_ref,
    gate_w,
    up_w,
    down_w,
    sems,
):
    width, hidden_width = gate_w.shape
    step = min(256, hidden_width)
    chunks = []
    for j in range(hidden_width // step):
        span = pl.ds(j * step, step)
        pairs = (
            (gate_hbm.at[:, span], gate_w.at[:, span]),
            (up_hbm.at[:, span], up_w.at[:, span]),
            (down_hbm.at[span, :], down_w.at[span, :]),
        )
        chunks.append(
            [pltpu.make_async_copy(*pair, sems.at[j, i]) for i, pair in enumerate(pairs)]
        )
    for chunk in chunks:
        for copy in chunk:
            copy.start()
    place = place_ref[0]
    slots = rows_ref.shape[0]
    lane = lax.broadcasted_iota(jnp.int32, (slots, SIDE), 1)
    mine = jnp.where((lane & (PLANE - 1)) == place, 1.0, 0.0)
    side = rows_ref[:, width : width + SIDE].astype(F32)
    slot_gate = jnp.sum(side * mine, axis=1, keepdims=True)
    pick_ref[...] = (slot_gate * rows_ref[:, width + SIDE :].astype(F32)).astype(BF16)

    for j, chunk in enumerate(chunks):
        for copy in chunk:
            copy.wait()
        span = slice(j * step, (j + 1) * step)
        gate_pre = jnp.dot(rows_ref[:, :width], gate_w[:, span], preferred_element_type=F32)
        up_pre = jnp.dot(rows_ref[:, :width], up_w[:, span], preferred_element_type=F32)
        hidden_grad = lax.dot_general(
            pick_ref[...], down_w[span, :], CONTRACT_LAST, preferred_element_type=F32
        )
        sigmoid = jax.nn.sigmoid(gate_pre)
        silu = gate_pre * sigmoid
        hidden_ref[:, span] = (silu * up_pre).astype(BF16)
        gate_grad = hidden_grad * up_pre * sigmoid * (1.0 + gate_pre * (1.0 - sigmoid))
        grads_ref[:, span] = gate_grad.astype(BF16)
        second = slice(hidden_width + j * step, hidden_width + (j + 1) * step)
        grads_ref[:, second] = (hidden_grad * silu).astype(BF16)

    wide = min(256, width)
    lead = back_ref.shape[:2]

    def outward(n, dots):
        start = pl.multiple_of(n * wide, wide)
        out = jnp.dot(hidden_ref[...], down_w[:, pl.ds(start, wide)], preferred_element_type=F32)
        ahead = pl.ds(pl.multiple_of(width + SIDE + n * wide, SIDE), wide)
        dots += jnp.sum(rows_ref[:, ahead].astype(F32) * out, axis=1, keepdims=True)
        back_ref[:, :, pl.ds(start, wide)] = (slot_gate * out).astype(BF16).reshape(*lead, wide)
        row_grad = lax.dot_general(
            grads_ref[:, :hidden_width],
            gate_w[pl.ds(start, wide), :],
            CONTRACT_LAST,
            preferred_element_type=F32,
        )
        row_grad += lax.dot_general(
            grads_ref[:, hidden_width:],
            up_w[pl.ds(start, wide), :],
            CONTRACT_LAST,
            preferred_element_type=F32,
        )
        back_ref[:, :, ahead] = row_grad.astype(BF16).reshape(*lead, wide)
        return dots

    dots = lax.fori_loop(0, width // wide, outward, jnp.zeros((slots, 1), F32))
    table = split_parts(dots * mine, (slots, SIDE))
    back_ref[:, :, width : width + SIDE] = table.reshape(*lead, SIDE)


def run_expert(place, rows, weights):
    slots = rows.shape[0]
    width, hidden_width = weights[0].shape
    full = 2 * width + SIDE
    pieces = hidden_width // min(256, hidden_width)
    return pl.pallas_call(
        expert_kernel,
        out_shape=(
            jax.ShapeDtypeStruct((PLANE, MOST, full), BF16),
            jax.ShapeDtypeStruct((slots, hidden_width), BF16),
            jax.ShapeDtypeStruct((slots, width), BF16),
            jax.ShapeDtypeStruct((slots, 2 * hidden_width), BF16),
        ),
        grid=(1,),
        in_specs=[SCALAR, block_of(rows.shape)] + [ANYWHERE] * 3,
        out_specs=(
            block_of((PLANE, MOST, full)),
            block_of((slots, hidden_width)),
            block_of((slots, width)),
            block_of((slots, 2 * hidden_width)),
        ),
        scratch_shapes=[
            pltpu.VMEM((width, hidden_width), BF16),
            pltpu.VMEM((width, hidden_width), BF16),
            pltpu.VMEM((hidden_width, width), BF16),
            pltpu.SemaphoreType.DMA((pieces, 3)),
        ],
        compiler_params=limits(),
        cost_estimate=cost(12 * slots * width * hidden_width, 6 * width * hidden_width),
        name="expert",
    )(place, rows, *weights)


def shard_start(where_ref, core, r, shard):
    lo = (where_ref[1] + r) & (LO_SIZE - 1)
    return pl.multiple_of((lo * CORES + core) * shard, shard)


def wide_kernel(keep, shard, where_ref, near_x, far_x, near_grads, far_grads, *refs):
    turned, columns = refs[-2:]
    slots = near_x.shape[0]
    core = where_ref[0] if keep else 1 - where_ref[0]

    @pl.when(pl.program_id(0) == 0)
    def _():
        for r in range(LO_SIZE):
            span = pl.ds(shard_start(where_ref, core, r, shard), shard)
            here = slice(r * shard, (r + 1) * shard)
            turned[here, :slots] = jnp.transpose(near_x[:, span])
            turned[here, slots:] = jnp.transpose(far_x[:, span])

    columns[:slots] = near_grads[...]
    columns[slots:] = far_grads[...]
    total = jnp.dot(turned[...], columns[...], preferred_element_type=F32)
    for r in range(LO_SIZE):
        part = total[r * shard : (r + 1) * shard]
        if keep:
            part = (part + refs[0][r].astype(F32)).astype(BF16)
            refs[1 + r][...] = part
            if r & 1:
                @pl.when((where_ref[1] == 0) == (r != 1))
                def _():
                    refs[1 + LO_SIZE][...] = part
        else:
            refs[0][r] = part.astype(BF16)


def wide_grads(where, rows, grads, width, taken=None):
    shard = width // (LO_SIZE * CORES)
    slots, columns = grads[0].shape
    step = min(512, columns)
    block = pl.BlockSpec((LO_SIZE, shard, step), lambda n, s: (0, 0, n))
    tokens = pl.BlockSpec((slots, width), lambda n, s: (0, 0))
    part = pl.BlockSpec((slots, step), lambda n, s: (0, n))
    one = pl.BlockSpec((shard, step), lambda n, s: (0, n))
    keep = taken is not None
    if keep:
        out_shape = (jax.ShapeDtypeStruct((shard, columns), BF16),) * (LO_SIZE + 1)
    else:
        out_shape = jax.ShapeDtypeStruct((LO_SIZE, shard, columns), BF16)
    return pl.pallas_call(
        functools.partial(wide_kernel, keep, shard),
        grid_spec=pltpu.PrefetchScalarGridSpec(
            num_scalar_prefetch=1,
            grid=(columns // step,),
            in_specs=[tokens, tokens, part, part] + ([block] if keep else []),
            out_specs=(one,) * (LO_SIZE + 1) if keep else block,
            scratch_shapes=[
                pltpu.VMEM((LO_SIZE * shard, 2 * slots), BF16),
                pltpu.VMEM((2 * slots, step), BF16),
            ],
        ),
        out_shape=out_shape,
        compiler_params=limits(),
        cost_estimate=cost(2 * slots * width * columns, 2 * width * columns),
        name="wide",
    )(where, *rows, *grads, *([taken] if keep else []))


def down_kernel(
    where_ref, near_hidden, far_hidden, near_pick, far_pick, give_ref, keep_ref, turned, columns, acc
):
    core = where_ref[0]
    shard = give_ref.shape[1]
    slots = near_hidden.shape[0]

    @pl.when(pl.program_id(0) == 0)
    def _():
        turned[:, :slots] = jnp.transpose(near_hidden[...])
        turned[:, slots:] = jnp.transpose(far_hidden[...])

    columns[:slots] = near_pick[...]
    columns[slots:] = far_pick[...]
    acc[...] = jnp.dot(turned[...], columns[...], preferred_element_type=F32)
    for r in range(LO_SIZE):
        for which, ref in ((1 - core, give_ref), (core, keep_ref)):
            start = shard_start(where_ref, which, r, shard)
            ref[r] = acc[pl.ds(start, shard), :].astype(BF16)


def down_grads(where, hidden, pick):
    slots, hidden_width = hidden[0].shape
    width = pick[0].shape[1]
    shard = hidden_width // (LO_SIZE * CORES)
    step = min(512, width)
    same = pl.BlockSpec((slots, hidden_width), lambda n, s: (0, 0))
    part = pl.BlockSpec((slots, step), lambda n, s: (0, n))
    block = pl.BlockSpec((LO_SIZE, shard, step), lambda n, s: (0, 0, n))
    shape = jax.ShapeDtypeStruct((LO_SIZE, shard, width), BF16)
    return pl.pallas_call(
        down_kernel,
        grid_spec=pltpu.PrefetchScalarGridSpec(
            num_scalar_prefetch=1,
            grid=(width // step,),
            in_specs=[same, same, part, part],
            out_specs=(block, block),
            scratch_shapes=[
                pltpu.VMEM((hidden_width, 2 * slots), BF16),
                pltpu.VMEM((2 * slots, step), BF16),
                pltpu.VMEM((hidden_width, step), F32),
            ],
        ),
        out_shape=(shape, shape),
        compiler_params=limits(),
        cost_estimate=cost(4 * slots * width * hidden_width, 4 * width * hidden_width),
        name="down",
    )(where, *hidden, *pick)


def turned_picks(picked_ref):
    return jnp.transpose(picked_ref[...].astype(F32)).astype(BF16)


def gather_rows(turned, returned_ref, start, size):
    block = returned_ref[:, :, start : start + size].reshape(PLANE * MOST, size)
    return jnp.dot(turned, block, preferred_element_type=F32)


def spans(width):
    step = min(512, width)
    return [(n, step) for n in range(0, width, step)]


def collect_kernel(picked_ref, returned_ref, out_ref):
    turned = turned_picks(picked_ref)
    full = out_ref.shape[1]
    width = (full - SIDE) // 2
    for start, size in spans(width) + [(width, SIDE)] + [
        (width + SIDE + n, step) for n, step in spans(width)
    ]:
        out_ref[:, start : start + size] = gather_rows(turned, returned_ref, start, size).astype(
            BF16
        )


def collect(picked, returned):
    slots, rows = picked.shape
    full = returned.shape[2]
    return pl.pallas_call(
        collect_kernel,
        grid=(1,),
        in_specs=[block_of(picked.shape), block_of(returned.shape)],
        out_specs=block_of((rows, full)),
        out_shape=jax.ShapeDtypeStruct((rows, full), BF16),
        compiler_params=limits(),
        cost_estimate=cost(2 * slots * rows * full, 2 * slots * full),
        name="collect",
    )(picked, returned)


def finish_kernel(half_ref, ids_ref, picked_ref, returned_ref, far_ref, out_ref, token_ref, gate_ref):
    turned = turned_picks(picked_ref)
    rows, width = out_ref.shape
    for n, step in spans(width):
        near = gather_rows(turned, returned_ref, n, step)
        out_ref[:, n : n + step] = (near + far_ref[:, n : n + step].astype(F32)).astype(BF16)
        start = width + SIDE + n
        near = gather_rows(turned, returned_ref, start, step)
        far = far_ref[:, start : start + step].astype(F32)
        token_ref[:, n : n + step] = (near + far).astype(BF16)
    near_dots = gather_rows(turned, returned_ref, width, SIDE)
    far_dots = far_ref[:, width : width + SIDE].astype(F32)
    half = half_ref[0]
    near_names = lane_names((rows, SIDE), half)
    far_names = lane_names((rows, SIDE), 1 - half)
    for k in range(ids_ref.shape[1]):
        ids = ids_ref[:, k : k + 1]
        found = jnp.where(ids == near_names, near_dots, 0.0)
        found += jnp.where(ids == far_names, far_dots, 0.0)
        gate_ref[:, k : k + 1] = jnp.sum(found, axis=1, keepdims=True)


def finish(half, ids, picked, returned, far_total):
    slots, rows = picked.shape
    full = returned.shape[2]
    width = (full - SIDE) // 2
    wide = jax.ShapeDtypeStruct((rows, width), BF16)
    return pl.pallas_call(
        finish_kernel,
        grid=(1,),
        in_specs=[SCALAR]
        + [block_of(value.shape) for value in (ids, picked, returned, far_total)],
        out_specs=(block_of((rows, width)), block_of((rows, width)), block_of(ids.shape)),
        out_shape=(wide, wide, jax.ShapeDtypeStruct(ids.shape, F32)),
        compiler_params=limits(),
        cost_estimate=cost(2 * slots * rows * full, 2 * slots * full),
        name="finish",
    )(half, ids, picked, returned, far_total)


def core_swap(give):
    return lax.ppermute(give, "dp", [(i, i ^ 1) for i in range(LO_SIZE * CORES)])


def move(value, steps):
    pairs = [(a * CORES + c, b * CORES + c) for a, b in steps for c in range(CORES)]
    return lax.ppermute(value, "dp", pairs)


def to_next(value):
    return move(value, [(0, 1), (1, 2)]), move(value, [(3, 2), (2, 1)])


def to_owner(up, down):
    return move(up, [(0, 1), (1, 2), (2, 3)]), move(down, [(3, 2), (2, 1), (1, 0)])


def total(terms):
    result = terms[0].astype(F32)
    for term in terms[1:]:
        result = result + term.astype(F32)
    return result.astype(BF16)


def on_device(tokens, out_grad, expert_ids, route_gates, swap_flags, gate_proj, up_proj, down_proj):
    devices = lax.axis_size("expert")
    my_expert = lax.axis_index("expert")
    lo = lax.axis_index("dp") // CORES
    core = lax.axis_index("dp") % CORES
    half = ((my_expert // Y_SIZE) % HI_SIZE).astype(jnp.int32)[None]
    place = (my_expert % Y_SIZE) * X_SIZE + my_expert // (HI_SIZE * Y_SIZE)
    place = place.astype(jnp.int32)[None]
    where = jnp.stack([core, lo]).astype(jnp.int32)
    width = tokens.shape[1]
    hidden_width = gate_proj.shape[2]
    weights = (gate_proj[0], up_proj[0], down_proj[0])

    far_tokens = across(tokens)
    far_out_grad = across(out_grad)
    own_sides, far_sides = route(half, expert_ids, route_gates)
    far_sides = across(far_sides)
    near_blocks, near_picked = fill(own_sides, tokens, out_grad, 10**9)
    near_rows = to_plane(near_blocks.reshape(PLANE, MOST, -1)).reshape(PLANE * MOST, -1)
    far_blocks, far_picked = fill(far_sides, far_tokens, far_out_grad, 10**12)
    far_blocks, near_blocks = lax.optimization_barrier((far_blocks, near_blocks))
    far_rows = to_plane(far_blocks.reshape(PLANE, MOST, -1)).reshape(PLANE * MOST, -1)

    near_back, near_hidden, near_pick, near_grads = run_expert(place, near_rows, weights)
    far_back, far_hidden, far_pick, far_grads = run_expert(place, far_rows, weights)

    rows, grads = (near_rows, far_rows), (near_grads, far_grads)
    give = wide_grads(where, rows, grads, width)
    taken = core_swap(give)
    far_back, give = lax.optimization_barrier((far_back, give))
    far_returned = to_plane(far_back)
    give_down, keep_down = down_grads(where, (near_hidden, far_hidden), (near_pick, far_pick))
    taken, keep_down = lax.optimization_barrier((taken, keep_down))
    *wide, wide_first = wide_grads(where, rows, grads, width, taken)
    give_down, unused = lax.optimization_barrier((give_down, wide_first))

    arrived = move(wide_first, [(0, 1), (3, 2)])
    taken_down = core_swap(give_down)
    narrow = [total([keep_down[r], taken_down[r]]) for r in range(LO_SIZE)]
    narrow_arrived = move(jnp.where(lo == 0, narrow[3], narrow[1]), [(0, 1), (3, 2)])

    near_back, far_returned = lax.optimization_barrier((near_back, far_returned))
    near_returned = to_plane(near_back)

    up, down = to_next(total([wide[2], arrived]))
    up, down, narrow_arrived = lax.optimization_barrier((up, down, narrow_arrived))
    sent = lax.optimization_barrier((total([wide[1], up]), total([wide[3], down])))
    up, down = to_owner(*sent)
    narrow_arrived, far_returned, unused = lax.optimization_barrier(
        (narrow_arrived, far_returned, sent)
    )
    narrow_up, narrow_down = to_next(total([narrow[2], narrow_arrived]))
    collected = collect(far_picked, far_returned)
    collected, near_returned, up, down = lax.optimization_barrier(
        (collected, near_returned, up, down)
    )
    far_total = across(collected)
    gate_up_sum = total([wide[0], up, down])
    narrow_up, narrow_down, unused = lax.optimization_barrier(
        (narrow_up, narrow_down, gate_up_sum)
    )
    narrow_up, narrow_down = to_owner(
        total([narrow[1], narrow_up]), total([narrow[3], narrow_down])
    )
    down_sum = total([narrow[0], narrow_up, narrow_down])

    layer_out, grad_tokens, gate_grads = finish(
        half, expert_ids, near_picked, near_returned, far_total
    )

    is_moved = swap_flags[my_expert] == 1
    swap = [(i, i ^ (devices // 2)) for i in range(devices)]
    other_gate_up = lax.ppermute(gate_up_sum, "expert", swap)
    other_down = lax.ppermute(down_sum, "expert", swap)
    other_down, unused = lax.optimization_barrier((other_down, far_total))
    gate_up_sum = jnp.where(is_moved, other_gate_up, gate_up_sum)
    down_sum = jnp.where(is_moved, other_down, down_sum)
    grad_gate = gate_up_sum[:, :hidden_width]
    grad_up = gate_up_sum[:, hidden_width:]
    return (layer_out, grad_tokens, gate_grads, grad_gate[None], grad_up[None], down_sum[None])


def solution(mesh):
    return jax.shard_map(
        on_device,
        mesh=mesh,
        in_specs=(
            P(("dp", "expert"), None),
            P(("dp", "expert"), None),
            P(("dp", "expert"), None),
            P(("dp", "expert"), None),
            P(),
            P("expert", None, None),
            P("expert", None, None),
            P("expert", None, None),
        ),
        out_specs=(
            P(("dp", "expert"), None),
            P(("dp", "expert"), None),
            P(("dp", "expert"), None),
            P("expert", "dp", None),
            P("expert", "dp", None),
            P("expert", "dp", None),
        ),
        check_vma=False,
    )
```

```python
import functools

import jax
import jax.numpy as jnp
from jax import lax
from jax.experimental import pallas as pl
from jax.experimental.pallas import tpu as pltpu
from jax.sharding import PartitionSpec as P

MOST = 16
X_SIZE, HI_SIZE, Y_SIZE = 4, 2, 4
LO_SIZE, CORES = 4, 2
PLANE = 16
SIDE = 128
PARTS = 3

BOTH = ("dp", "expert")
PLANE_GROUPS = [
    [x * HI_SIZE * Y_SIZE + hi * Y_SIZE + y for y in range(Y_SIZE) for x in range(X_SIZE)]
    for hi in range(HI_SIZE)
]
CONTRACT_LAST = (((1,), (1,)), ((), ()))
CONTRACT_FIRST = (((0,), (0,)), ((), ()))
BF16, F32 = jnp.bfloat16, jnp.float32
WHOLE = pl.BlockSpec(memory_space=pltpu.VMEM)
SCALAR = pl.BlockSpec(memory_space=pltpu.SMEM)
ANYWHERE = pl.BlockSpec(memory_space=pl.ANY)


def block_of(shape):
    return pl.BlockSpec(shape, lambda i: (0,) * len(shape))


def limits():
    return pltpu.CompilerParams(vmem_limit_bytes=62 << 20)


def cost(flops, moved):
    return pl.CostEstimate(flops=flops, bytes_accessed=moved, transcendentals=0)


def across(value):
    experts = lax.axis_size("expert")
    pairs = []
    for dp in range(lax.axis_size("dp")):
        lo, core = divmod(dp, CORES)
        other_dp = (LO_SIZE - 1 - lo) * CORES + core
        for expert in range(experts):
            pairs.append((dp * experts + expert, other_dp * experts + (expert ^ Y_SIZE)))
    return lax.ppermute(value, BOTH, pairs)


def to_plane(blocks):
    return lax.all_to_all(
        blocks, "expert", split_axis=0, concat_axis=0, axis_index_groups=PLANE_GROUPS, tiled=True
    )


def lane_names(shape, half):
    place = lax.broadcasted_iota(jnp.int32, shape, 1) & (PLANE - 1)
    return (place & (X_SIZE - 1)) * (HI_SIZE * Y_SIZE) + half * Y_SIZE + (place >> 2)


def split_parts(values, shape):
    part = lax.broadcasted_iota(jnp.int32, shape, 1) >> 4
    high = values.astype(BF16).astype(F32)
    middle = (values - high).astype(BF16).astype(F32)
    low = values - high - middle
    chosen = jnp.where(part == 0, high, jnp.where(part == 1, middle, low))
    return jnp.where(part < PARTS, chosen, 0.0).astype(BF16)


def route_kernel(half_ref, ids_ref, gates_ref, own_ref, far_ref):
    half = half_ref[0]
    shape = own_ref.shape
    for which, ref in ((half, own_ref), (1 - half, far_ref)):
        names = lane_names(shape, which)
        total = jnp.zeros(shape, F32)
        for k in range(ids_ref.shape[1]):
            total += jnp.where(ids_ref[:, k : k + 1] == names, gates_ref[:, k : k + 1], 0.0)
        ref[...] = split_parts(total, shape)


def route(half, ids, gates):
    table = jax.ShapeDtypeStruct((ids.shape[0], SIDE), BF16)
    return pl.pallas_call(
        route_kernel,
        out_shape=(table, table),
        in_specs=[SCALAR, WHOLE, WHOLE],
        out_specs=(WHOLE, WHOLE),
        cost_estimate=cost(1000000, 200000),
        name="route",
    )(half, ids, gates)


def fill_kernel(sides_ref, tokens_ref, grads_ref, blocks_ref, picked_ref):
    rows = sides_ref.shape[0]
    width = tokens_ref.shape[1]
    turned = jnp.transpose(sides_ref[...].astype(F32))
    chosen = jnp.where(turned[:PLANE] > 0, 1.0, 0.0)
    before = jnp.where(
        lax.broadcasted_iota(jnp.int32, (rows, rows), 0)
        < lax.broadcasted_iota(jnp.int32, (rows, rows), 1),
        1.0,
        0.0,
    ).astype(BF16)
    rank = jnp.dot(chosen.astype(BF16), before, preferred_element_type=F32)
    rank = jnp.where(chosen > 0, rank, -1.0)
    slot = lax.broadcasted_iota(jnp.int32, (MOST, rows), 0).astype(F32)
    for j in range(PLANE):
        hit = jnp.where(rank[j : j + 1] == slot, 1.0, 0.0)
        picked_ref[j * MOST : (j + 1) * MOST, :] = hit.astype(BF16)
    picked = picked_ref[...]
    blocks_ref[:, width : width + SIDE] = jnp.dot(
        picked, sides_ref[...], preferred_element_type=F32
    ).astype(BF16)
    step = min(512, width)
    for n in range(0, width, step):
        blocks_ref[:, n : n + step] = jnp.dot(
            picked, tokens_ref[:, n : n + step], preferred_element_type=F32
        ).astype(BF16)
        blocks_ref[:, width + SIDE + n : width + SIDE + n + step] = jnp.dot(
            picked, grads_ref[:, n : n + step], preferred_element_type=F32
        ).astype(BF16)


def fill(sides, tokens, grads, weight):
    rows, width = tokens.shape
    slots = PLANE * MOST
    return pl.pallas_call(
        fill_kernel,
        out_shape=(
            jax.ShapeDtypeStruct((slots, 2 * width + SIDE), BF16),
            jax.ShapeDtypeStruct((slots, rows), BF16),
        ),
        grid=(1,),
        in_specs=[block_of(sides.shape), block_of(tokens.shape), block_of(grads.shape)],
        out_specs=(block_of((slots, 2 * width + SIDE)), block_of((slots, rows))),
        compiler_params=limits(),
        cost_estimate=cost(weight, 8 * slots * width),
        name="fill",
    )(sides, tokens, grads)


def expert_kernel(
    place_ref,
    rows_ref,
    gate_hbm,
    up_hbm,
    down_hbm,
    back_ref,
    hidden_ref,
    pick_ref,
    grads_ref,
    gate_w,
    up_w,
    down_w,
    sems,
):
    width, hidden_width = gate_w.shape
    step = min(256, hidden_width)
    chunks = []
    for j in range(hidden_width // step):
        span = pl.ds(j * step, step)
        pairs = (
            (gate_hbm.at[:, span], gate_w.at[:, span]),
            (up_hbm.at[:, span], up_w.at[:, span]),
            (down_hbm.at[span, :], down_w.at[span, :]),
        )
        chunks.append(
            [pltpu.make_async_copy(*pair, sems.at[j, i]) for i, pair in enumerate(pairs)]
        )
    for chunk in chunks:
        for copy in chunk:
            copy.start()
    place = place_ref[0]
    slots = rows_ref.shape[0]
    lane = lax.broadcasted_iota(jnp.int32, (slots, SIDE), 1)
    mine = jnp.where((lane & (PLANE - 1)) == place, 1.0, 0.0)
    side = rows_ref[:, width : width + SIDE].astype(F32)
    slot_gate = jnp.sum(side * mine, axis=1, keepdims=True)
    pick_ref[...] = (slot_gate * rows_ref[:, width + SIDE :].astype(F32)).astype(BF16)

    for j, chunk in enumerate(chunks):
        for copy in chunk:
            copy.wait()
        span = slice(j * step, (j + 1) * step)
        gate_pre = jnp.dot(rows_ref[:, :width], gate_w[:, span], preferred_element_type=F32)
        up_pre = jnp.dot(rows_ref[:, :width], up_w[:, span], preferred_element_type=F32)
        hidden_grad = lax.dot_general(
            pick_ref[...], down_w[span, :], CONTRACT_LAST, preferred_element_type=F32
        )
        sigmoid = jax.nn.sigmoid(gate_pre)
        silu = gate_pre * sigmoid
        hidden_ref[:, span] = (silu * up_pre).astype(BF16)
        gate_grad = hidden_grad * up_pre * sigmoid * (1.0 + gate_pre * (1.0 - sigmoid))
        grads_ref[:, span] = gate_grad.astype(BF16)
        second = slice(hidden_width + j * step, hidden_width + (j + 1) * step)
        grads_ref[:, second] = (hidden_grad * silu).astype(BF16)

    wide = min(256, width)
    lead = back_ref.shape[:2]

    def outward(n, dots):
        start = pl.multiple_of(n * wide, wide)
        out = jnp.dot(hidden_ref[...], down_w[:, pl.ds(start, wide)], preferred_element_type=F32)
        ahead = pl.ds(pl.multiple_of(width + SIDE + n * wide, SIDE), wide)
        dots += jnp.sum(rows_ref[:, ahead].astype(F32) * out, axis=1, keepdims=True)
        back_ref[:, :, pl.ds(start, wide)] = (slot_gate * out).astype(BF16).reshape(*lead, wide)
        row_grad = lax.dot_general(
            grads_ref[:, :hidden_width],
            gate_w[pl.ds(start, wide), :],
            CONTRACT_LAST,
            preferred_element_type=F32,
        )
        row_grad += lax.dot_general(
            grads_ref[:, hidden_width:],
            up_w[pl.ds(start, wide), :],
            CONTRACT_LAST,
            preferred_element_type=F32,
        )
        back_ref[:, :, ahead] = row_grad.astype(BF16).reshape(*lead, wide)
        return dots

    dots = lax.fori_loop(0, width // wide, outward, jnp.zeros((slots, 1), F32))
    table = split_parts(dots * mine, (slots, SIDE))
    back_ref[:, :, width : width + SIDE] = table.reshape(*lead, SIDE)


def run_expert(place, rows, weights):
    slots = rows.shape[0]
    width, hidden_width = weights[0].shape
    full = 2 * width + SIDE
    pieces = hidden_width // min(256, hidden_width)
    return pl.pallas_call(
        expert_kernel,
        out_shape=(
            jax.ShapeDtypeStruct((PLANE, MOST, full), BF16),
            jax.ShapeDtypeStruct((slots, hidden_width), BF16),
            jax.ShapeDtypeStruct((slots, width), BF16),
            jax.ShapeDtypeStruct((slots, 2 * hidden_width), BF16),
        ),
        grid=(1,),
        in_specs=[SCALAR, block_of(rows.shape)] + [ANYWHERE] * 3,
        out_specs=(
            block_of((PLANE, MOST, full)),
            block_of((slots, hidden_width)),
            block_of((slots, width)),
            block_of((slots, 2 * hidden_width)),
        ),
        scratch_shapes=[
            pltpu.VMEM((width, hidden_width), BF16),
            pltpu.VMEM((width, hidden_width), BF16),
            pltpu.VMEM((hidden_width, width), BF16),
            pltpu.SemaphoreType.DMA((pieces, 3)),
        ],
        compiler_params=limits(),
        cost_estimate=cost(12 * slots * width * hidden_width, 6 * width * hidden_width),
        name="expert",
    )(place, rows, *weights)


def shard_start(where_ref, core, r, shard):
    lo = (where_ref[1] + r) & (LO_SIZE - 1)
    return pl.multiple_of((lo * CORES + core) * shard, shard)


def wide_kernel(keep, shard, where_ref, near_x, far_x, near_grads, far_grads, *refs):
    turned, columns = refs[-2:]
    slots = near_x.shape[0]
    core = where_ref[0] if keep else 1 - where_ref[0]

    @pl.when(pl.program_id(0) == 0)
    def _():
        for r in range(LO_SIZE):
            span = pl.ds(shard_start(where_ref, core, r, shard), shard)
            here = slice(r * shard, (r + 1) * shard)
            turned[here, :slots] = jnp.transpose(near_x[:, span])
            turned[here, slots:] = jnp.transpose(far_x[:, span])

    columns[:slots] = near_grads[...]
    columns[slots:] = far_grads[...]
    total = jnp.dot(turned[...], columns[...], preferred_element_type=F32)
    for r in range(LO_SIZE):
        part = total[r * shard : (r + 1) * shard]
        if keep:
            part = (part + refs[0][r].astype(F32)).astype(BF16)
            refs[1 + r][...] = part
            if r & 1:
                @pl.when((where_ref[1] == 0) == (r != 1))
                def _():
                    refs[1 + LO_SIZE][...] = part
        else:
            refs[0][r] = part.astype(BF16)


def wide_grads(where, rows, grads, width, taken=None):
    shard = width // (LO_SIZE * CORES)
    slots, columns = grads[0].shape
    step = min(512, columns)
    block = pl.BlockSpec((LO_SIZE, shard, step), lambda n, s: (0, 0, n))
    tokens = pl.BlockSpec((slots, width), lambda n, s: (0, 0))
    part = pl.BlockSpec((slots, step), lambda n, s: (0, n))
    one = pl.BlockSpec((shard, step), lambda n, s: (0, n))
    keep = taken is not None
    if keep:
        out_shape = (jax.ShapeDtypeStruct((shard, columns), BF16),) * (LO_SIZE + 1)
    else:
        out_shape = jax.ShapeDtypeStruct((LO_SIZE, shard, columns), BF16)
    return pl.pallas_call(
        functools.partial(wide_kernel, keep, shard),
        grid_spec=pltpu.PrefetchScalarGridSpec(
            num_scalar_prefetch=1,
            grid=(columns // step,),
            in_specs=[tokens, tokens, part, part] + ([block] if keep else []),
            out_specs=(one,) * (LO_SIZE + 1) if keep else block,
            scratch_shapes=[
                pltpu.VMEM((LO_SIZE * shard, 2 * slots), BF16),
                pltpu.VMEM((2 * slots, step), BF16),
            ],
        ),
        out_shape=out_shape,
        compiler_params=limits(),
        cost_estimate=cost(2 * slots * width * columns, 2 * width * columns),
        name="wide",
    )(where, *rows, *grads, *([taken] if keep else []))


def down_kernel(
    where_ref, near_hidden, far_hidden, near_pick, far_pick, give_ref, keep_ref, turned, columns, acc
):
    core = where_ref[0]
    shard = give_ref.shape[1]
    slots = near_hidden.shape[0]

    @pl.when(pl.program_id(0) == 0)
    def _():
        turned[:, :slots] = jnp.transpose(near_hidden[...])
        turned[:, slots:] = jnp.transpose(far_hidden[...])

    columns[:slots] = near_pick[...]
    columns[slots:] = far_pick[...]
    acc[...] = jnp.dot(turned[...], columns[...], preferred_element_type=F32)
    for r in range(LO_SIZE):
        for which, ref in ((1 - core, give_ref), (core, keep_ref)):
            start = shard_start(where_ref, which, r, shard)
            ref[r] = acc[pl.ds(start, shard), :].astype(BF16)


def down_grads(where, hidden, pick):
    slots, hidden_width = hidden[0].shape
    width = pick[0].shape[1]
    shard = hidden_width // (LO_SIZE * CORES)
    step = min(512, width)
    same = pl.BlockSpec((slots, hidden_width), lambda n, s: (0, 0))
    part = pl.BlockSpec((slots, step), lambda n, s: (0, n))
    block = pl.BlockSpec((LO_SIZE, shard, step), lambda n, s: (0, 0, n))
    shape = jax.ShapeDtypeStruct((LO_SIZE, shard, width), BF16)
    return pl.pallas_call(
        down_kernel,
        grid_spec=pltpu.PrefetchScalarGridSpec(
            num_scalar_prefetch=1,
            grid=(width // step,),
            in_specs=[same, same, part, part],
            out_specs=(block, block),
            scratch_shapes=[
                pltpu.VMEM((hidden_width, 2 * slots), BF16),
                pltpu.VMEM((2 * slots, step), BF16),
                pltpu.VMEM((hidden_width, step), F32),
            ],
        ),
        out_shape=(shape, shape),
        compiler_params=limits(),
        cost_estimate=cost(4 * slots * width * hidden_width, 4 * width * hidden_width),
        name="down",
    )(where, *hidden, *pick)


def turned_picks(picked_ref):
    return jnp.transpose(picked_ref[...].astype(F32)).astype(BF16)


def gather_rows(turned, returned_ref, start, size):
    block = returned_ref[:, :, start : start + size].reshape(PLANE * MOST, size)
    return jnp.dot(turned, block, preferred_element_type=F32)


def spans(width):
    step = min(512, width)
    return [(n, step) for n in range(0, width, step)]


def collect_kernel(picked_ref, returned_ref, out_ref):
    turned = turned_picks(picked_ref)
    full = out_ref.shape[1]
    width = (full - SIDE) // 2
    for start, size in spans(width) + [(width, SIDE)] + [
        (width + SIDE + n, step) for n, step in spans(width)
    ]:
        out_ref[:, start : start + size] = gather_rows(turned, returned_ref, start, size).astype(
            BF16
        )


def collect(picked, returned):
    slots, rows = picked.shape
    full = returned.shape[2]
    return pl.pallas_call(
        collect_kernel,
        grid=(1,),
        in_specs=[block_of(picked.shape), block_of(returned.shape)],
        out_specs=block_of((rows, full)),
        out_shape=jax.ShapeDtypeStruct((rows, full), BF16),
        compiler_params=limits(),
        cost_estimate=cost(2 * slots * rows * full, 2 * slots * full),
        name="collect",
    )(picked, returned)


def finish_kernel(half_ref, ids_ref, picked_ref, returned_ref, far_ref, out_ref, token_ref, gate_ref):
    turned = turned_picks(picked_ref)
    rows, width = out_ref.shape
    for n, step in spans(width):
        near = gather_rows(turned, returned_ref, n, step)
        out_ref[:, n : n + step] = (near + far_ref[:, n : n + step].astype(F32)).astype(BF16)
        start = width + SIDE + n
        near = gather_rows(turned, returned_ref, start, step)
        far = far_ref[:, start : start + step].astype(F32)
        token_ref[:, n : n + step] = (near + far).astype(BF16)
    near_dots = gather_rows(turned, returned_ref, width, SIDE)
    far_dots = far_ref[:, width : width + SIDE].astype(F32)
    half = half_ref[0]
    near_names = lane_names((rows, SIDE), half)
    far_names = lane_names((rows, SIDE), 1 - half)
    for k in range(ids_ref.shape[1]):
        ids = ids_ref[:, k : k + 1]
        found = jnp.where(ids == near_names, near_dots, 0.0)
        found += jnp.where(ids == far_names, far_dots, 0.0)
        gate_ref[:, k : k + 1] = jnp.sum(found, axis=1, keepdims=True)


def finish(half, ids, picked, returned, far_total):
    slots, rows = picked.shape
    full = returned.shape[2]
    width = (full - SIDE) // 2
    wide = jax.ShapeDtypeStruct((rows, width), BF16)
    return pl.pallas_call(
        finish_kernel,
        grid=(1,),
        in_specs=[SCALAR]
        + [block_of(value.shape) for value in (ids, picked, returned, far_total)],
        out_specs=(block_of((rows, width)), block_of((rows, width)), block_of(ids.shape)),
        out_shape=(wide, wide, jax.ShapeDtypeStruct(ids.shape, F32)),
        compiler_params=limits(),
        cost_estimate=cost(2 * slots * rows * full, 2 * slots * full),
        name="finish",
    )(half, ids, picked, returned, far_total)


def core_swap(give):
    return lax.ppermute(give, "dp", [(i, i ^ 1) for i in range(LO_SIZE * CORES)])


def move(value, steps):
    pairs = [(a * CORES + c, b * CORES + c) for a, b in steps for c in range(CORES)]
    return lax.ppermute(value, "dp", pairs)


def to_next(value):
    return move(value, [(0, 1), (1, 2)]), move(value, [(3, 2), (2, 1)])


def to_owner(up, down):
    return move(up, [(0, 1), (1, 2), (2, 3)]), move(down, [(3, 2), (2, 1), (1, 0)])


def total(terms):
    result = terms[0].astype(F32)
    for term in terms[1:]:
        result = result + term.astype(F32)
    return result.astype(BF16)


def on_device(tokens, out_grad, expert_ids, route_gates, swap_flags, gate_proj, up_proj, down_proj):
    devices = lax.axis_size("expert")
    my_expert = lax.axis_index("expert")
    lo = lax.axis_index("dp") // CORES
    core = lax.axis_index("dp") % CORES
    half = ((my_expert // Y_SIZE) % HI_SIZE).astype(jnp.int32)[None]
    place = (my_expert % Y_SIZE) * X_SIZE + my_expert // (HI_SIZE * Y_SIZE)
    place = place.astype(jnp.int32)[None]
    where = jnp.stack([core, lo]).astype(jnp.int32)
    width = tokens.shape[1]
    hidden_width = gate_proj.shape[2]
    weights = (gate_proj[0], up_proj[0], down_proj[0])

    far_tokens = across(tokens)
    far_out_grad = across(out_grad)
    own_sides, far_sides = route(half, expert_ids, route_gates)
    far_sides = across(far_sides)
    near_blocks, near_picked = fill(own_sides, tokens, out_grad, 10**9)
    near_rows = to_plane(near_blocks.reshape(PLANE, MOST, -1)).reshape(PLANE * MOST, -1)
    far_blocks, far_picked = fill(far_sides, far_tokens, far_out_grad, 10**12)
    far_blocks, near_blocks = lax.optimization_barrier((far_blocks, near_blocks))
    far_rows = to_plane(far_blocks.reshape(PLANE, MOST, -1)).reshape(PLANE * MOST, -1)

    near_back, near_hidden, near_pick, near_grads = run_expert(place, near_rows, weights)
    far_back, far_hidden, far_pick, far_grads = run_expert(place, far_rows, weights)

    rows, grads = (near_rows, far_rows), (near_grads, far_grads)
    give = wide_grads(where, rows, grads, width)
    taken = core_swap(give)
    far_back, give = lax.optimization_barrier((far_back, give))
    far_returned = to_plane(far_back)
    give_down, keep_down = down_grads(where, (near_hidden, far_hidden), (near_pick, far_pick))
    taken, keep_down = lax.optimization_barrier((taken, keep_down))
    *wide, wide_first = wide_grads(where, rows, grads, width, taken)
    give_down, unused = lax.optimization_barrier((give_down, wide_first))

    arrived = move(wide_first, [(0, 1), (3, 2)])
    taken_down = core_swap(give_down)
    narrow = [total([keep_down[r], taken_down[r]]) for r in range(LO_SIZE)]
    narrow_arrived = move(jnp.where(lo == 0, narrow[3], narrow[1]), [(0, 1), (3, 2)])

    near_back, far_returned = lax.optimization_barrier((near_back, far_returned))
    near_returned = to_plane(near_back)
    collected = collect(far_picked, far_returned)
    far_total = across(collected)
    arrived, unused = lax.optimization_barrier((arrived, collected))

    up, down = to_next(total([wide[2], arrived]))
    up, down, far_total, narrow_arrived = lax.optimization_barrier(
        (up, down, far_total, narrow_arrived)
    )
    sent = lax.optimization_barrier((total([wide[1], up]), total([wide[3], down])))
    up, down = to_owner(*sent)
    narrow_arrived, unused = lax.optimization_barrier((narrow_arrived, sent))
    narrow_up, narrow_down = to_next(total([narrow[2], narrow_arrived]))
    narrow_up, narrow_down, up, down = lax.optimization_barrier((narrow_up, narrow_down, up, down))
    narrow_up, narrow_down = to_owner(
        total([narrow[1], narrow_up]), total([narrow[3], narrow_down])
    )
    gate_up_sum = total([wide[0], up, down])
    down_sum = total([narrow[0], narrow_up, narrow_down])

    layer_out, grad_tokens, gate_grads = finish(
        half, expert_ids, near_picked, near_returned, far_total
    )

    is_moved = swap_flags[my_expert] == 1
    swap = [(i, i ^ (devices // 2)) for i in range(devices)]
    other_gate_up = lax.ppermute(gate_up_sum, "expert", swap)
    other_down = lax.ppermute(down_sum, "expert", swap)
    gate_up_sum = jnp.where(is_moved, other_gate_up, gate_up_sum)
    down_sum = jnp.where(is_moved, other_down, down_sum)
    grad_gate = gate_up_sum[:, :hidden_width]
    grad_up = gate_up_sum[:, hidden_width:]
    return (layer_out, grad_tokens, gate_grads, grad_gate[None], grad_up[None], down_sum[None])


def solution(mesh):
    return jax.shard_map(
        on_device,
        mesh=mesh,
        in_specs=(
            P(("dp", "expert"), None),
            P(("dp", "expert"), None),
            P(("dp", "expert"), None),
            P(("dp", "expert"), None),
            P(),
            P("expert", None, None),
            P("expert", None, None),
            P("expert", None, None),
        ),
        out_specs=(
            P(("dp", "expert"), None),
            P(("dp", "expert"), None),
            P(("dp", "expert"), None),
            P("expert", "dp", None),
            P("expert", "dp", None),
            P("expert", "dp", None),
        ),
        check_vma=False,
    )
```

```python
import functools

import jax
import jax.numpy as jnp
from jax import lax
from jax.experimental import pallas as pl
from jax.experimental.pallas import tpu as pltpu
from jax.sharding import PartitionSpec as P

MOST = 16
X_SIZE, HI_SIZE, Y_SIZE = 4, 2, 4
LO_SIZE, CORES = 4, 2
PLANE = 16
SIDE = 128
PARTS = 3

BOTH = ("dp", "expert")
PLANE_GROUPS = [
    [x * HI_SIZE * Y_SIZE + hi * Y_SIZE + y for y in range(Y_SIZE) for x in range(X_SIZE)]
    for hi in range(HI_SIZE)
]
CONTRACT_LAST = (((1,), (1,)), ((), ()))
CONTRACT_FIRST = (((0,), (0,)), ((), ()))
BF16, F32 = jnp.bfloat16, jnp.float32
WHOLE = pl.BlockSpec(memory_space=pltpu.VMEM)
SCALAR = pl.BlockSpec(memory_space=pltpu.SMEM)
ANYWHERE = pl.BlockSpec(memory_space=pl.ANY)


def limits():
    return pltpu.CompilerParams(vmem_limit_bytes=48 << 20)


def cost(flops, moved):
    return pl.CostEstimate(flops=flops, bytes_accessed=moved, transcendentals=0)


def across(value):
    experts = lax.axis_size("expert")
    pairs = []
    for dp in range(lax.axis_size("dp")):
        lo, core = divmod(dp, CORES)
        other_dp = (LO_SIZE - 1 - lo) * CORES + core
        for expert in range(experts):
            pairs.append((dp * experts + expert, other_dp * experts + (expert ^ Y_SIZE)))
    return lax.ppermute(value, BOTH, pairs)


def to_plane(blocks):
    return lax.all_to_all(
        blocks, "expert", split_axis=0, concat_axis=0, axis_index_groups=PLANE_GROUPS, tiled=True
    )


def lane_names(shape, half):
    place = lax.broadcasted_iota(jnp.int32, shape, 1) & (PLANE - 1)
    return (place & (X_SIZE - 1)) * (HI_SIZE * Y_SIZE) + half * Y_SIZE + (place >> 2)


def split_parts(values, shape):
    part = lax.broadcasted_iota(jnp.int32, shape, 1) >> 4
    high = values.astype(BF16).astype(F32)
    middle = (values - high).astype(BF16).astype(F32)
    low = values - high - middle
    chosen = jnp.where(part == 0, high, jnp.where(part == 1, middle, low))
    return jnp.where(part < PARTS, chosen, 0.0).astype(BF16)


def route_kernel(half_ref, ids_ref, gates_ref, own_ref, far_ref):
    half = half_ref[0]
    shape = own_ref.shape
    for which, ref in ((half, own_ref), (1 - half, far_ref)):
        names = lane_names(shape, which)
        total = jnp.zeros(shape, F32)
        for k in range(ids_ref.shape[1]):
            total += jnp.where(ids_ref[:, k : k + 1] == names, gates_ref[:, k : k + 1], 0.0)
        ref[...] = split_parts(total, shape)


def route(half, ids, gates):
    table = jax.ShapeDtypeStruct((ids.shape[0], SIDE), BF16)
    return pl.pallas_call(
        route_kernel,
        out_shape=(table, table),
        in_specs=[SCALAR, WHOLE, WHOLE],
        out_specs=(WHOLE, WHOLE),
        cost_estimate=cost(1000000, 200000),
        name="route",
    )(half, ids, gates)


def fill_kernel(sides_ref, tokens_ref, grads_ref, blocks_ref, picked_ref):
    rows = sides_ref.shape[0]
    width = tokens_ref.shape[1]
    turned = jnp.transpose(sides_ref[...].astype(F32))
    chosen = jnp.where(turned[:PLANE] > 0, 1.0, 0.0)
    before = jnp.where(
        lax.broadcasted_iota(jnp.int32, (rows, rows), 0)
        < lax.broadcasted_iota(jnp.int32, (rows, rows), 1),
        1.0,
        0.0,
    ).astype(BF16)
    rank = jnp.dot(chosen.astype(BF16), before, preferred_element_type=F32)
    rank = jnp.where(chosen > 0, rank, -1.0)
    slot = lax.broadcasted_iota(jnp.int32, (MOST, rows), 0).astype(F32)
    for j in range(PLANE):
        hit = jnp.where(rank[j : j + 1] == slot, 1.0, 0.0)
        picked_ref[j * MOST : (j + 1) * MOST, :] = hit.astype(BF16)
    picked = picked_ref[...]
    blocks_ref[:, width : width + SIDE] = jnp.dot(
        picked, sides_ref[...], preferred_element_type=F32
    ).astype(BF16)
    step = min(512, width)
    for n in range(0, width, step):
        blocks_ref[:, n : n + step] = jnp.dot(
            picked, tokens_ref[:, n : n + step], preferred_element_type=F32
        ).astype(BF16)
        blocks_ref[:, width + SIDE + n : width + SIDE + n + step] = jnp.dot(
            picked, grads_ref[:, n : n + step], preferred_element_type=F32
        ).astype(BF16)


def fill(sides, tokens, grads, weight):
    rows, width = tokens.shape
    slots = PLANE * MOST
    return pl.pallas_call(
        fill_kernel,
        out_shape=(
            jax.ShapeDtypeStruct((slots, 2 * width + SIDE), BF16),
            jax.ShapeDtypeStruct((slots, rows), BF16),
        ),
        in_specs=[WHOLE] * 3,
        out_specs=(WHOLE, WHOLE),
        compiler_params=limits(),
        cost_estimate=cost(weight, 8 * slots * width),
        name="fill",
    )(sides, tokens, grads)


def expert_kernel(
    place_ref,
    rows_ref,
    gate_hbm,
    up_hbm,
    down_hbm,
    back_ref,
    hidden_ref,
    pick_ref,
    grads_ref,
    gate_w,
    up_w,
    down_w,
    sems,
):
    width, hidden_width = gate_w.shape
    step = min(256, hidden_width)
    chunks = []
    for j in range(hidden_width // step):
        span = pl.ds(j * step, step)
        pairs = (
            (gate_hbm.at[:, span], gate_w.at[:, span]),
            (up_hbm.at[:, span], up_w.at[:, span]),
            (down_hbm.at[span, :], down_w.at[span, :]),
        )
        chunks.append(
            [pltpu.make_async_copy(*pair, sems.at[j, i]) for i, pair in enumerate(pairs)]
        )
    for chunk in chunks:
        for copy in chunk:
            copy.start()
    place = place_ref[0]
    slots = rows_ref.shape[0]
    lane = lax.broadcasted_iota(jnp.int32, (slots, SIDE), 1)
    mine = jnp.where((lane & (PLANE - 1)) == place, 1.0, 0.0)
    side = rows_ref[:, width : width + SIDE].astype(F32)
    slot_gate = jnp.sum(side * mine, axis=1, keepdims=True)
    pick_ref[...] = (slot_gate * rows_ref[:, width + SIDE :].astype(F32)).astype(BF16)

    for j, chunk in enumerate(chunks):
        for copy in chunk:
            copy.wait()
        span = slice(j * step, (j + 1) * step)
        gate_pre = jnp.dot(rows_ref[:, :width], gate_w[:, span], preferred_element_type=F32)
        up_pre = jnp.dot(rows_ref[:, :width], up_w[:, span], preferred_element_type=F32)
        hidden_grad = lax.dot_general(
            pick_ref[...], down_w[span, :], CONTRACT_LAST, preferred_element_type=F32
        )
        sigmoid = jax.nn.sigmoid(gate_pre)
        silu = gate_pre * sigmoid
        hidden_ref[:, span] = (silu * up_pre).astype(BF16)
        gate_grad = hidden_grad * up_pre * sigmoid * (1.0 + gate_pre * (1.0 - sigmoid))
        grads_ref[:, span] = gate_grad.astype(BF16)
        second = slice(hidden_width + j * step, hidden_width + (j + 1) * step)
        grads_ref[:, second] = (hidden_grad * silu).astype(BF16)

    wide = min(256, width)
    lead = back_ref.shape[:2]

    def outward(n, dots):
        start = pl.multiple_of(n * wide, wide)
        out = jnp.dot(hidden_ref[...], down_w[:, pl.ds(start, wide)], preferred_element_type=F32)
        ahead = pl.ds(pl.multiple_of(width + SIDE + n * wide, SIDE), wide)
        dots += jnp.sum(rows_ref[:, ahead].astype(F32) * out, axis=1, keepdims=True)
        back_ref[:, :, pl.ds(start, wide)] = (slot_gate * out).astype(BF16).reshape(*lead, wide)
        row_grad = lax.dot_general(
            grads_ref[:, :hidden_width],
            gate_w[pl.ds(start, wide), :],
            CONTRACT_LAST,
            preferred_element_type=F32,
        )
        row_grad += lax.dot_general(
            grads_ref[:, hidden_width:],
            up_w[pl.ds(start, wide), :],
            CONTRACT_LAST,
            preferred_element_type=F32,
        )
        back_ref[:, :, ahead] = row_grad.astype(BF16).reshape(*lead, wide)
        return dots

    dots = lax.fori_loop(0, width // wide, outward, jnp.zeros((slots, 1), F32))
    table = split_parts(dots * mine, (slots, SIDE))
    back_ref[:, :, width : width + SIDE] = table.reshape(*lead, SIDE)


def run_expert(place, rows, weights):
    slots = rows.shape[0]
    width, hidden_width = weights[0].shape
    full = 2 * width + SIDE
    pieces = hidden_width // min(256, hidden_width)
    return pl.pallas_call(
        expert_kernel,
        out_shape=(
            jax.ShapeDtypeStruct((PLANE, MOST, full), BF16),
            jax.ShapeDtypeStruct((slots, hidden_width), BF16),
            jax.ShapeDtypeStruct((slots, width), BF16),
            jax.ShapeDtypeStruct((slots, 2 * hidden_width), BF16),
        ),
        in_specs=[SCALAR, WHOLE] + [ANYWHERE] * 3,
        out_specs=(WHOLE,) * 4,
        scratch_shapes=[
            pltpu.VMEM((width, hidden_width), BF16),
            pltpu.VMEM((width, hidden_width), BF16),
            pltpu.VMEM((hidden_width, width), BF16),
            pltpu.SemaphoreType.DMA((pieces, 3)),
        ],
        compiler_params=limits(),
        cost_estimate=cost(12 * slots * width * hidden_width, 6 * width * hidden_width),
        name="expert",
    )(place, rows, *weights)


def wide_kernel(keep, shard, where_ref, near_x, far_x, near_grads, far_grads, *refs):
    turned, columns = refs[-2:]
    slots = near_x.shape[0]

    @pl.when(pl.program_id(0) == 0)
    def _():
        for z in range(LO_SIZE):
            span = pl.ds(pl.multiple_of((z * CORES + where_ref[0]) * shard, shard), shard)
            here = slice(z * shard, (z + 1) * shard)
            turned[here, :slots] = jnp.transpose(near_x[:, span])
            turned[here, slots:] = jnp.transpose(far_x[:, span])

    columns[:slots] = near_grads[...]
    columns[slots:] = far_grads[...]
    total = jnp.dot(turned[...], columns[...], preferred_element_type=F32)
    if keep:
        taken_ref, out_ref, first_ref = refs[:3]
        for z in range(LO_SIZE):
            part = total[z * shard : (z + 1) * shard] + taken_ref[z].astype(F32)
            part = part.astype(BF16)
            out_ref[z] = part
            if z in (0, LO_SIZE - 1):

                @pl.when((where_ref[1] == 0) == (z != 0))
                def _():
                    first_ref[...] = part
    else:
        for z in range(LO_SIZE):
            refs[0][z] = total[z * shard : (z + 1) * shard].astype(BF16)


def wide_grads(where, rows, grads, width, taken=None):
    shard = width // (LO_SIZE * CORES)
    slots, columns = grads[0].shape
    step = min(512, columns)
    block = pl.BlockSpec((LO_SIZE, shard, step), lambda n, s: (0, 0, n))
    tokens = pl.BlockSpec((slots, width), lambda n, s: (0, 0))
    part = pl.BlockSpec((slots, step), lambda n, s: (0, n))
    shape = jax.ShapeDtypeStruct((LO_SIZE, shard, columns), BF16)
    extra = [] if taken is None else [taken]
    first = jax.ShapeDtypeStruct((shard, columns), BF16)
    first_block = pl.BlockSpec((shard, step), lambda n, s: (0, n))
    return pl.pallas_call(
        functools.partial(wide_kernel, taken is not None, shard),
        grid_spec=pltpu.PrefetchScalarGridSpec(
            num_scalar_prefetch=1,
            grid=(columns // step,),
            in_specs=[tokens, tokens, part, part] + [block] * len(extra),
            out_specs=(block, first_block) if extra else block,
            scratch_shapes=[
                pltpu.VMEM((LO_SIZE * shard, 2 * slots), BF16),
                pltpu.VMEM((2 * slots, step), BF16),
            ],
        ),
        out_shape=(shape, first) if extra else shape,
        compiler_params=limits(),
        cost_estimate=cost(2 * slots * width * columns, 2 * width * columns),
        name="wide",
    )(where, *rows, *grads, *extra)


def down_kernel(
    core_ref, near_hidden, far_hidden, near_pick, far_pick, give_ref, keep_ref, turned, columns, acc
):
    core = core_ref[0]
    shard = give_ref.shape[1]
    slots = near_hidden.shape[0]

    @pl.when(pl.program_id(0) == 0)
    def _():
        turned[:, :slots] = jnp.transpose(near_hidden[...])
        turned[:, slots:] = jnp.transpose(far_hidden[...])

    columns[:slots] = near_pick[...]
    columns[slots:] = far_pick[...]
    acc[...] = jnp.dot(turned[...], columns[...], preferred_element_type=F32)
    for z in range(LO_SIZE):
        for which, ref in ((1 - core, give_ref), (core, keep_ref)):
            start = pl.multiple_of((z * CORES + which) * shard, shard)
            ref[z] = acc[pl.ds(start, shard), :].astype(BF16)


def down_grads(core, hidden, pick):
    slots, hidden_width = hidden[0].shape
    width = pick[0].shape[1]
    shard = hidden_width // (LO_SIZE * CORES)
    step = min(512, width)
    same = pl.BlockSpec((slots, hidden_width), lambda n, s: (0, 0))
    part = pl.BlockSpec((slots, step), lambda n, s: (0, n))
    block = pl.BlockSpec((LO_SIZE, shard, step), lambda n, s: (0, 0, n))
    shape = jax.ShapeDtypeStruct((LO_SIZE, shard, width), BF16)
    return pl.pallas_call(
        down_kernel,
        grid_spec=pltpu.PrefetchScalarGridSpec(
            num_scalar_prefetch=1,
            grid=(width // step,),
            in_specs=[same, same, part, part],
            out_specs=(block, block),
            scratch_shapes=[
                pltpu.VMEM((hidden_width, 2 * slots), BF16),
                pltpu.VMEM((2 * slots, step), BF16),
                pltpu.VMEM((hidden_width, step), F32),
            ],
        ),
        out_shape=(shape, shape),
        compiler_params=limits(),
        cost_estimate=cost(4 * slots * width * hidden_width, 4 * width * hidden_width),
        name="down",
    )(core, *hidden, *pick)


def turned_picks(picked_ref):
    return jnp.transpose(picked_ref[...].astype(F32)).astype(BF16)


def gather_rows(turned, returned_ref, start, size):
    block = returned_ref[:, :, start : start + size].reshape(PLANE * MOST, size)
    return jnp.dot(turned, block, preferred_element_type=F32)


def spans(width):
    step = min(512, width)
    return [(n, step) for n in range(0, width, step)]


def collect_kernel(picked_ref, returned_ref, out_ref):
    turned = turned_picks(picked_ref)
    full = out_ref.shape[1]
    width = (full - SIDE) // 2
    for start, size in spans(width) + [(width, SIDE)] + [
        (width + SIDE + n, step) for n, step in spans(width)
    ]:
        out_ref[:, start : start + size] = gather_rows(turned, returned_ref, start, size).astype(
            BF16
        )


def collect(picked, returned):
    slots, rows = picked.shape
    full = returned.shape[2]
    return pl.pallas_call(
        collect_kernel,
        in_specs=[WHOLE, WHOLE],
        out_specs=WHOLE,
        out_shape=jax.ShapeDtypeStruct((rows, full), BF16),
        compiler_params=limits(),
        cost_estimate=cost(2 * slots * rows * full, 2 * slots * full),
        name="collect",
    )(picked, returned)


def finish_kernel(half_ref, ids_ref, picked_ref, returned_ref, far_ref, out_ref, token_ref, gate_ref):
    turned = turned_picks(picked_ref)
    rows, width = out_ref.shape
    for n, step in spans(width):
        near = gather_rows(turned, returned_ref, n, step)
        out_ref[:, n : n + step] = (near + far_ref[:, n : n + step].astype(F32)).astype(BF16)
        start = width + SIDE + n
        near = gather_rows(turned, returned_ref, start, step)
        far = far_ref[:, start : start + step].astype(F32)
        token_ref[:, n : n + step] = (near + far).astype(BF16)
    near_dots = gather_rows(turned, returned_ref, width, SIDE)
    far_dots = far_ref[:, width : width + SIDE].astype(F32)
    half = half_ref[0]
    near_names = lane_names((rows, SIDE), half)
    far_names = lane_names((rows, SIDE), 1 - half)
    for k in range(ids_ref.shape[1]):
        ids = ids_ref[:, k : k + 1]
        found = jnp.where(ids == near_names, near_dots, 0.0)
        found += jnp.where(ids == far_names, far_dots, 0.0)
        gate_ref[:, k : k + 1] = jnp.sum(found, axis=1, keepdims=True)


def finish(half, ids, picked, returned, far_total):
    slots, rows = picked.shape
    full = returned.shape[2]
    width = (full - SIDE) // 2
    wide = jax.ShapeDtypeStruct((rows, width), BF16)
    return pl.pallas_call(
        finish_kernel,
        in_specs=[SCALAR] + [WHOLE] * 4,
        out_specs=(WHOLE,) * 3,
        out_shape=(wide, wide, jax.ShapeDtypeStruct(ids.shape, F32)),
        compiler_params=limits(),
        cost_estimate=cost(2 * slots * rows * full, 2 * slots * full),
        name="finish",
    )(half, ids, picked, returned, far_total)


def neighbours(steps):
    return [(a * CORES + core, b * CORES + core) for a, b in steps for core in range(CORES)]


def core_swap(give):
    return lax.ppermute(give, "dp", [(i, i ^ 1) for i in range(LO_SIZE * CORES)])


def shard_of(parts, index):
    index = jnp.clip(index, 0, LO_SIZE - 1)
    return lax.dynamic_index_in_dim(parts, index, axis=0, keepdims=False).astype(F32)


def line_sum(parts, first, lo):
    arrived = lax.ppermute(first, "dp", neighbours([(0, 1), (3, 2)])).astype(F32)
    up = (shard_of(parts, lo + 2) + arrived).astype(BF16)
    down = (shard_of(parts, lo - 2) + arrived).astype(BF16)
    middle = up
    up = lax.ppermute(up, "dp", neighbours([(0, 1), (1, 2)]))
    down = lax.ppermute(down, "dp", neighbours([(3, 2), (2, 1)]))
    up = (shard_of(parts, lo + 1) + up.astype(F32)).astype(BF16)
    down = (shard_of(parts, lo - 1) + down.astype(F32)).astype(BF16)
    up = lax.ppermute(up, "dp", neighbours([(0, 1), (1, 2), (2, 3)])).astype(F32)
    down = lax.ppermute(down, "dp", neighbours([(3, 2), (2, 1), (1, 0)])).astype(F32)
    return (shard_of(parts, lo) + up + down).astype(BF16), middle


def on_device(tokens, out_grad, expert_ids, route_gates, swap_flags, gate_proj, up_proj, down_proj):
    devices = lax.axis_size("expert")
    my_expert = lax.axis_index("expert")
    lo = lax.axis_index("dp") // CORES
    core = lax.axis_index("dp") % CORES
    half = ((my_expert // Y_SIZE) % HI_SIZE).astype(jnp.int32)[None]
    place = (my_expert % Y_SIZE) * X_SIZE + my_expert // (HI_SIZE * Y_SIZE)
    place = place.astype(jnp.int32)[None]
    here = core.astype(jnp.int32)[None]
    line = lo.astype(jnp.int32)[None]
    width = tokens.shape[1]
    hidden_width = gate_proj.shape[2]
    weights = (gate_proj[0], up_proj[0], down_proj[0])

    far_tokens = across(tokens)
    far_out_grad = across(out_grad)
    own_sides, far_sides = route(half, expert_ids, route_gates)
    far_sides = across(far_sides)
    near_blocks, near_picked = fill(own_sides, tokens, out_grad, 10**9)
    near_rows = to_plane(near_blocks.reshape(PLANE, MOST, -1)).reshape(PLANE * MOST, -1)
    far_blocks, far_picked = fill(far_sides, far_tokens, far_out_grad, 10**12)
    far_blocks, near_blocks = lax.optimization_barrier((far_blocks, near_blocks))
    far_rows = to_plane(far_blocks.reshape(PLANE, MOST, -1)).reshape(PLANE * MOST, -1)

    near_back, near_hidden, near_pick, near_grads = run_expert(place, near_rows, weights)
    far_back, far_hidden, far_pick, far_grads = run_expert(place, far_rows, weights)

    rows, grads = (near_rows, far_rows), (near_grads, far_grads)
    give = wide_grads(jnp.concatenate([1 - here, line]), rows, grads, width)
    taken = core_swap(give)
    far_back, give = lax.optimization_barrier((far_back, give))
    far_returned = to_plane(far_back)
    give_down, keep_down = down_grads(here, (near_hidden, far_hidden), (near_pick, far_pick))
    taken, keep_down = lax.optimization_barrier((taken, keep_down))
    gate_up_parts, first = wide_grads(jnp.concatenate([here, line]), rows, grads, width, taken)
    give_down, first = lax.optimization_barrier((give_down, first))
    taken_down = core_swap(give_down)
    gate_up_sum, middle = line_sum(gate_up_parts, first, lo)
    down_parts = (keep_down.astype(F32) + taken_down.astype(F32)).astype(BF16)
    first_down = jnp.where(lo == 0, down_parts[LO_SIZE - 1], down_parts[0])
    down_sum, unused = line_sum(down_parts, first_down, lo)

    near_back, far_returned = lax.optimization_barrier((near_back, far_returned))
    near_returned = to_plane(near_back)
    far_returned, middle = lax.optimization_barrier((far_returned, middle))
    far_total = across(collect(far_picked, far_returned))
    layer_out, grad_tokens, gate_grads = finish(
        half, expert_ids, near_picked, near_returned, far_total
    )

    is_moved = swap_flags[my_expert] == 1
    swap = [(i, i ^ (devices // 2)) for i in range(devices)]
    other_gate_up = lax.ppermute(gate_up_sum, "expert", swap)
    other_down = lax.ppermute(down_sum, "expert", swap)
    gate_up_sum = jnp.where(is_moved, other_gate_up, gate_up_sum)
    down_sum = jnp.where(is_moved, other_down, down_sum)
    grad_gate = gate_up_sum[:, :hidden_width]
    grad_up = gate_up_sum[:, hidden_width:]
    return (layer_out, grad_tokens, gate_grads, grad_gate[None], grad_up[None], down_sum[None])


def solution(mesh):
    return jax.shard_map(
        on_device,
        mesh=mesh,
        in_specs=(
            P(("dp", "expert"), None),
            P(("dp", "expert"), None),
            P(("dp", "expert"), None),
            P(("dp", "expert"), None),
            P(),
            P("expert", None, None),
            P("expert", None, None),
            P("expert", None, None),
        ),
        out_specs=(
            P(("dp", "expert"), None),
            P(("dp", "expert"), None),
            P(("dp", "expert"), None),
            P("expert", "dp", None),
            P("expert", "dp", None),
            P("expert", "dp", None),
        ),
        check_vma=False,
    )
```
